32 devices in a mesh: strip: 2 (over x), az: 4 (over z), tile: 4 (over y, core).
Axes of the slice: x: 2, y: 2, z: 4, core: 2. Of those that a mesh axis runs over, the one named last changes fastest.
Arguments:
- raw_echo: float32 [2, 4096, 4096], P(None, ('strip', 'az', 'tile')), parts along dimension 1, may hold values from -6 to 6
- phase_scaling: float32 [1024, 4096], P(None, 'tile'), may hold values from -3.140625 to 3.140625
- phase_range: float32 [1024, 4096], P('tile'), may hold values from -3.140625 to 3.140625
- phase_azimuth: float32 [1024, 4096], P(None, 'tile'), may hold values from -3.140625 to 3.140625
Outputs:
- image: float32 [2, 4096, 4096], P(None, ('strip', 'az'), 'tile'), parts along dimension 1
The draws below stay inside these ranges and needn't reach their ends.
There are 2 independent parts, one for each index of `strip`. The reference program is written for one: setup_inputs(seed, part) draws one part's arguments, and reference() takes and returns one part's arrays. A program takes and returns all parts, laid end to end along the dimension named above; an argument that names none is the same for every part. Nothing has to cross between parts.
All inputs are finite; a program needn't handle non-finite values.
Results may differ from the reference program's by a relative error of at most 0.00007.
Values sent between devices are 32-bit elements; how exact they have to be, the bound alone decides.
A program may use at most 128 MiB of HBM per device.

```python
import jax
import jax.numpy as jnp
from jax import lax

RANGES = 4096
PULSES = 512
TAIL = 512
LENGTH = 1024
STRIP_PULSES = 2048
N_AZ = 4


def block_levels(stream_key, extent, cuts, low, top_value):
    def one(dim, blocks):
        steps = jax.random.uniform(jax.random.fold_in(jax.random.fold_in(stream_key, 6), dim), (blocks,), jnp.float32, low / len(cuts), top_value / len(cuts))
        return jnp.repeat(jnp.exp(steps), extent[dim] // blocks).reshape((-1,) + (1,) * (len(extent) - dim - 1))

    loudness = one(*cuts[0])
    for cut in cuts[1:]:
        loudness = loudness * one(*cut)
    return loudness


def gaussian(own_key, shape, scale, bound, shards=(), dtype=jnp.bfloat16):
    result = jax.random.normal(own_key, shape, jnp.float32) * scale
    if len(shards) > 0:
        result = block_levels(own_key, shape, shards, -0.22, 0.18) * result
    return jnp.clip(result, min=-bound, max=bound).astype(dtype)


def setup_inputs(seed: int = 0, part: int = 0) -> dict:
    key_list = jax.random.split(jax.random.key(seed), 5)
    own_keys = jax.random.split(jax.random.fold_in(key_list[4], part), 5)
    return {
        "raw_echo": gaussian(own_keys[0], (2, STRIP_PULSES, RANGES), 1.0, 6.0, ((1, 16),), jnp.float32),
        "phase_scaling": jnp.clip(jax.random.uniform(key_list[1], (LENGTH, RANGES), jnp.float32, -3.140625, 3.140625), -3.140625, 3.140625),
        "phase_range": jnp.clip(jax.random.uniform(key_list[2], (LENGTH, RANGES), jnp.float32, -3.140625, 3.140625), -3.140625, 3.140625),
        "phase_azimuth": jnp.clip(jax.random.uniform(key_list[3], (LENGTH, RANGES), jnp.float32, -3.140625, 3.140625), -3.140625, 3.140625),
    }


def reference(raw_echo, phase_scaling, phase_range, phase_azimuth):
    blocks = raw_echo.reshape(2, N_AZ, PULSES, RANGES).transpose(1, 0, 2, 3)
    turn_one = lax.complex(jnp.cos(phase_scaling), jnp.sin(phase_scaling))
    turn_two = lax.complex(jnp.cos(phase_range), jnp.sin(phase_range))
    turn_three = lax.complex(jnp.cos(phase_azimuth), jnp.sin(phase_azimuth))

    def focus_block(block):
        signal = lax.complex(block[0], block[1])
        signal = jnp.pad(signal, ((0, TAIL), (0, 0)))
        signal = jnp.fft.fft(signal, axis=0) * turn_one
        signal = jnp.fft.fft(signal, axis=1) * turn_two
        signal = jnp.fft.ifft(signal, axis=1) * turn_three
        signal = jnp.fft.ifft(signal, axis=0)
        return jnp.stack([jnp.real(signal), jnp.imag(signal)])

    focused = lax.map(focus_block, blocks)
    head_rows = focused[:, :, :PULSES]
    tail_rows = focused[:, :, PULSES:]
    previous = jnp.concatenate([jnp.zeros_like(tail_rows[:1]), tail_rows[:-1]], axis=0)
    head_rows = head_rows.at[:, :, :TAIL].add(previous)
    return head_rows.transpose(1, 0, 2, 3).reshape(2, N_AZ * PULSES, RANGES)
```

```python
import functools
import math

import jax
import jax.numpy as jnp
import numpy as np
from jax import lax
from jax.experimental import pallas as pl
from jax.experimental.pallas import tpu as pltpu
from jax.sharding import PartitionSpec as P

F32 = jnp.float32
BF16 = jnp.bfloat16
LANES = 128


def halves(table):
    hi = np.asarray(table, np.float32).astype(jnp.bfloat16)
    lo = (np.asarray(table, np.float64) - hi.astype(np.float64)).astype(jnp.bfloat16)
    return np.stack([hi, lo])


def roots(rows, cols, modulus, direction):
    residue = np.outer(rows, cols) % modulus
    angle = residue * (direction * 2.0 * math.pi / modulus)
    return np.cos(angle), np.sin(angle)


def left_table(rows, cols, modulus, direction, scale=1.0):
    c, s = roots(rows, cols, modulus, direction)
    return halves(np.block([[c, -s], [s, c]]) * scale)


def right_table(rows, cols, modulus, direction, scale=1.0):
    c, s = roots(rows, cols, modulus, direction)
    return halves(np.block([[c, s], [-s, c]]) * scale)


def twist_table(count, length, modulus, direction):
    c, s = roots(np.arange(count), np.arange(length), modulus, direction)
    full = np.stack([c, s]).astype(np.float32)
    return np.ascontiguousarray(np.broadcast_to(full[..., None], full.shape + (LANES,)))


def split(x):
    hi = x.astype(BF16)
    return hi, (x - hi.astype(F32)).astype(BF16)


def mm(a, b):
    return jnp.dot(a, b, preferred_element_type=F32)


def times(a, t):
    return a[0] * t[0] - a[1] * t[1], a[0] * t[1] + a[1] * t[0]


def plus(a, b):
    return a[0] + b[0], a[1] + b[1]


def minus(a, b):
    return a[0] - b[0], a[1] - b[1]


def quarter(a, direction):
    return (-a[1], a[0]) if direction > 0 else (a[1], -a[0])


def four(v, direction):
    a, b = plus(v[0], v[2]), minus(v[0], v[2])
    c, d = plus(v[1], v[3]), quarter(minus(v[1], v[3]), direction)
    return [plus(a, c), plus(b, d), minus(a, c), minus(b, d)]


def fft(v, direction):
    n = len(v)
    if n == 1:
        return v
    if n == 2:
        return [plus(v[0], v[1]), minus(v[0], v[1])]
    if n == 4:
        return four(v, direction)
    parts = [fft(v[e::4], direction) for e in range(4)] if n % 4 == 0 else None
    out = [None] * n
    m = n // 4
    for f in range(m):
        items = []
        for e in range(4):
            x = parts[e][f]
            k = e * f % n
            if k == 0:
                pass
            elif 8 * k == n:
                h = np.float32(math.sqrt(0.5))
                q = quarter(x, direction)
                x = ((x[0] + q[0]) * h, (x[1] + q[1]) * h)
            elif 4 * k == n:
                x = quarter(x, direction)
            elif 8 * k == 3 * n:
                h = np.float32(math.sqrt(0.5))
                q = quarter(x, direction)
                x = ((q[0] - x[0]) * h, (q[1] - x[1]) * h)
            else:
                ang = direction * 2.0 * math.pi * k / n
                x = times(x, (np.float32(math.cos(ang)), np.float32(math.sin(ang))))
            items.append(x)
        got = four(items, direction)
        for j in range(4):
            out[f + j * m] = got[j]
    return out


def sincos(x):
    y = x * 0.5
    z = y * y
    s, c = -1.0 / 39916800, 1.0 / 479001600
    for a, b in ((362880, -3628800), (-5040, 40320), (120, -720), (-6, 24), (1, -2)):
        s = s * z + np.float32(1.0 / a)
        c = c * z + np.float32(1.0 / b)
    s = s * y
    c = c * z + 1.0
    return 1.0 - 2.0 * s * s, 2.0 * s * c


def greet(partners):
    barrier = pltpu.get_barrier_semaphore()
    for device in partners:
        pl.semaphore_signal(barrier, inc=1, device_id=device, device_id_type=pl.DeviceIdType.MESH)
    return barrier


def lanes(j):
    return pl.ds(pl.multiple_of(j * LANES, LANES), LANES)


def filter_rows(x_ref, base, block, fwd_ref, inv_ref, twist_ref, phase_ref, hi_ref, lo_ref, mid_ref):
    n_one = phase_ref.shape[0]
    step = 16
    f_hi, f_lo = fwd_ref[0], fwd_ref[1]
    b_hi, b_lo = inv_ref[0], inv_ref[1]

    @pl.loop(0, block // step)
    def _(i):
        rows = pl.ds(pl.multiple_of(i * step, step), step)
        at = pl.ds(pl.multiple_of(base + i * step, step), step)
        v = [
            tuple(x_ref[c, at, pl.ds(a * LANES, LANES)] for c in (0, 1))
            for a in range(n_one)
        ]
        for k, x in enumerate(fft(v, -1)):
            if k:
                x = times(x, (twist_ref[0, k : k + 1, :], twist_ref[1, k : k + 1, :]))
            for c in (0, 1):
                h, l = split(x[c])
                hi_ref[k, rows, pl.ds(c * LANES, LANES)] = h
                lo_ref[k, rows, pl.ds(c * LANES, LANES)] = l

    group = 4

    @pl.loop(0, n_one // group)
    def _(i):
        ks = pl.ds(i * group, group)
        flat = (group * block, 2 * LANES)
        h, l = hi_ref[ks].reshape(flat), lo_ref[ks].reshape(flat)
        r = mm(h, f_hi) + mm(l, f_hi) + mm(h, f_lo)
        turn = phase_ref[ks, pl.ds(pl.multiple_of(base, block), block), :]
        r = times((r[:, :LANES], r[:, LANES:]), sincos(turn.reshape(group * block, LANES)))
        h, l = split(jnp.concatenate(r, axis=1))
        r = mm(h, b_hi) + mm(l, b_hi) + mm(h, b_lo)
        at = pl.ds(pl.multiple_of(i * group * block, block), group * block)
        mid_ref[0, at, :] = r[:, :LANES]
        mid_ref[1, at, :] = r[:, LANES:]

    @pl.loop(0, block // 8)
    def _(i):
        at = pl.ds(pl.multiple_of(base + i * 8, 8), 8)
        v = []
        for k in range(n_one):
            x = tuple(mid_ref[c, pl.ds(pl.multiple_of(k * block + i * 8, 8), 8), :] for c in (0, 1))
            if k:
                x = times(x, (twist_ref[0, k : k + 1, :], -twist_ref[1, k : k + 1, :]))
            v.append(x)
        for a, x in enumerate(fft(v, 1)):
            for c in (0, 1):
                x_ref[c, at, pl.ds(a * LANES, LANES)] = x[c]


def permute_turn(o_ref, mid, turn):
    n_one, count, _ = turn.shape
    half = mid.shape[1]
    some = min(count, LANES)
    part = half // n_one

    @pl.loop(0, count // some)
    def _(i):
        @pl.loop(0, n_one)
        def _(g):
            c, row, j = piece(g, count, o_ref)
            at = pl.ds(pl.multiple_of(row + i * some, some), some)
            x = o_ref[c, at, lanes(j)]
            if some < LANES:
                x = jnp.concatenate([x] * (LANES // some), axis=0)
            per = half // LANES
            mid[g // per, pl.ds(pl.multiple_of(g % per * LANES, LANES), LANES), :] = x.T

        @pl.loop(0, n_one)
        def _(k):
            rows = pl.ds(k, part, stride=n_one)
            x = jnp.concatenate([mid[h, rows, :] for h in range(LANES // part)], axis=0)
            at = pl.ds(pl.multiple_of(i * some, some), some)
            turn[k, at, :] = x.T[:some]


def piece(g, count, o_ref):
    across = o_ref.shape[2] // LANES
    down = o_ref.shape[1] // count
    return g // (across * down), g // across % down * count, g % across


def focus_kernel(
    tiles, length, block,
    raw_ref, scaling_ref, range_ref, azimuth_ref,
    front_ref, twist_ref, fwd_ref, inv_ref, range_twist_ref, table_ref,
    o_ref,
    spec, scaling, turn, phase, dop, ret, tail_out, tail_in, head, hi_ref, lo_ref, mid,
    send_e, recv_e, local_e, send_a, recv_a, local_a, send_b, recv_b, local_b,
    send_c, recv_c, load, load_range,
):
    me = lax.axis_index("tile")
    az = lax.axis_index("az")
    count = dop.shape[1]
    width = o_ref.shape[2]
    pulses = o_ref.shape[1]
    tail = tail_in.shape[2]
    rows_own = raw_ref.shape[1]
    n_one = turn.shape[0]
    blocks = count // block
    early = (blocks - 1) * block
    spans = width // LANES
    cols = tail_out
    m = spec.shape[1] // 4
    q = pulses // 4
    mine = pl.ds(pl.multiple_of(me * width, LANES), width)
    own = pl.ds(pl.multiple_of(me * count, count), count)
    own_pulses = pl.ds(pl.multiple_of(me * rows_own, rows_own), rows_own)

    def remote(src, dst, send, recv, device):
        return pltpu.make_async_remote_copy(
            src_ref=src, dst_ref=dst, send_sem=send, recv_sem=recv,
            device_id=device, device_id_type=pl.DeviceIdType.MESH,
        )

    def echo(j, k):
        to = lax.rem(me + k, tiles)
        return remote(
            raw_ref.at[:, :, lanes(to * spans + j)], cols.at[j, :, own_pulses, :],
            send_e.at[j, k - 1], recv_e.at[j, k - 1], {"tile": to},
        )

    def keep_echo(j):
        return pltpu.make_async_copy(
            raw_ref.at[:, :, lanes(me * spans + j)], cols.at[j, :, own_pulses, :], local_e.at[j]
        )

    def load_piece(g):
        c, row, j = piece(g, count, o_ref)
        return pltpu.make_async_copy(
            range_ref.at[:, lanes(g)],
            o_ref.at[c, pl.ds(pl.multiple_of(row, count), count), lanes(j)],
            load_range.at[g],
        )

    def out_part(i, k, lo, n, slot):
        to = lax.rem(me + k, tiles)
        at = pl.ds(pl.multiple_of(me * width + lo, LANES), n)
        return remote(
            spec.at[:, pl.ds(pl.multiple_of(to * count + i * block, block), block), pl.ds(lo, n)],
            dop.at[:, pl.ds(pl.multiple_of(i * block, block), block), at],
            send_a.at[slot, k - 1], recv_a.at[slot, k - 1], {"tile": to},
        )

    def out(i, k):
        return out_part(i, k, 0, width, i)

    def first_out(k):
        return out_part(0, k, 0, width - LANES, blocks)

    def last_out(k):
        return out_part(0, k, width - LANES, LANES, 0)

    def back_rows(j, k, lo, n, slot):
        to = lax.rem(me + k, tiles)
        return remote(
            dop.at[:, pl.ds(lo, n), lanes(to * spans + j)],
            ret.at[j, :, pl.ds(pl.multiple_of(me * count + lo, 8), n), :],
            send_b.at[slot, k - 1], recv_b.at[slot, k - 1], {"tile": to},
        )

    def first_rows(k):
        return back_rows(0, k, 0, early, spans)

    def last_rows(k):
        return back_rows(0, k, early, count - early, 0)

    def back(j, k):
        return back_rows(j, k, 0, count, j)

    def keep(j):
        return pltpu.make_async_copy(
            dop.at[:, :, lanes(me * spans + j)], ret.at[j, :, own, :], local_b.at[j]
        )

    def onward(j):
        return remote(
            tail_out.at[j, :, pl.ds(0, tail), :], tail_in.at[j], send_c.at[j], recv_c.at[j],
            {"az": lax.rem(az + 1, length)},
        )

    barrier = greet(
        [{"tile": lax.rem(me + k, tiles)} for k in range(1, tiles)]
        + [{"az": lax.rem(az + 1, length)}, {"az": lax.rem(az + length - 1, length)}]
    )
    get_scaling = pltpu.make_async_copy(scaling_ref, scaling, load.at[0])
    get_phase = pltpu.make_async_copy(azimuth_ref, phase, load.at[1])
    pl.semaphore_wait(barrier, tiles + 1)

    @pl.loop(0, spans)
    def _(j):
        for k in range(1, tiles):
            echo(j, k).start()
        keep_echo(j).start()

    @pl.loop(0, n_one)
    def _(g):
        load_piece(g).start()

    get_scaling.start()
    get_phase.start()

    get_scaling.wait()

    @pl.loop(0, spans)
    def _(j):
        @pl.when(j == spans - 1)
        def _():
            for k in range(1, tiles):
                first_out(k).start()

        for k in range(1, tiles):
            echo(j, k).wait_recv()
        keep_echo(j).wait()
        hi, lo = front_ref[0], front_ref[1]
        z = []
        for e in range(4):
            rows = pl.ds(e, q, stride=4)
            s = jnp.concatenate([cols[j, 0, rows, :], cols[j, 1, rows, :]], axis=0)
            s_hi, s_lo = split(s)
            r = mm(hi, s_hi) + mm(hi, s_lo) + mm(lo, s_hi)
            r = (r[:m], r[m:])
            if e:
                r = times(r, (twist_ref[0, e], -twist_ref[1, e]))
            z.append(r)
        for f, x in enumerate(four(z, -1)):
            rows = pl.ds(f * m, m)
            x = times(x, sincos(scaling[rows, lanes(j)]))
            spec[0, rows, lanes(j)] = x[0]
            spec[1, rows, lanes(j)] = x[1]

    for k in range(1, tiles):
        last_out(k).start()

    @pl.loop(1, blocks)
    def _(i):
        for k in range(1, tiles):
            out(i, k).start()

    first = pltpu.make_async_copy(spec.at[:, own, :], dop.at[:, :, mine], local_a)
    first.start()

    @pl.loop(0, n_one)
    def _(g):
        load_piece(g).wait()

    permute_turn(o_ref, mid, turn)
    first.wait()

    @pl.loop(0, blocks)
    def _(i):
        if early:
            @pl.when(i == blocks - 1)
            def _():
                for k in range(1, tiles):
                    first_rows(k).start()

        @pl.when(i == 0)
        def _():
            for k in range(1, tiles):
                first_out(k).wait_recv()
                last_out(k).wait_recv()

        @pl.when(i > 0)
        def _():
            for k in range(1, tiles):
                out(i, k).wait_recv()

        filter_rows(
            dop, i * block, block, fwd_ref, inv_ref, range_twist_ref, turn,
            hi_ref, lo_ref, mid,
        )

    for k in range(1, tiles):
        last_rows(k).start()
    keep(0).start()

    @pl.loop(1, spans)
    def _(j):
        for k in range(1, tiles):
            back(j, k).start()
        keep(j).start()

    get_phase.wait()

    @pl.loop(0, spans)
    def _(j):
        @pl.when(j == 0)
        def _():
            for k in range(1, tiles):
                if early:
                    first_rows(k).wait_recv()
                last_rows(k).wait_recv()

        @pl.when(j > 0)
        def _():
            for k in range(1, tiles):
                back(j, k).wait_recv()

        keep(j).wait()
        hi, lo = table_ref[0], table_ref[1]
        v = []
        for f in range(4):
            rows = pl.ds(f * m, m)
            v.append(times((ret[j, 0, rows, :], ret[j, 1, rows, :]), sincos(phase[rows, lanes(j)])))
        for e, x in enumerate(four(v, 1)):
            if e:
                x = times(x, (twist_ref[0, e], twist_ref[1, e]))
            s_hi, s_lo = split(jnp.concatenate(x, axis=0))
            r = mm(hi, s_hi) + mm(hi, s_lo) + mm(lo, s_hi)
            for c in (0, 1):
                head[c, pl.ds(e, q, stride=4), :] = r[c * m : c * m + q]
                tail_out[j, c, pl.ds(e, m - q, stride=4), :] = r[c * m + q : (c + 1) * m]

        @pl.when(az < length - 1)
        def _():
            onward(j).start()

        o_ref[:, :, lanes(j)] = head[...]

    @pl.when(az > 0)
    def _():
        @pl.loop(0, spans)
        def _(j):
            onward(j).wait_recv()
            o_ref[:, pl.ds(0, tail), lanes(j)] += tail_in[j]

    for k in range(1, tiles):
        first_out(k).wait_send()
        last_out(k).wait_send()

    @pl.loop(1, blocks)
    def _(i):
        for k in range(1, tiles):
            out(i, k).wait_send()

    for k in range(1, tiles):
        if early:
            first_rows(k).wait_send()
        last_rows(k).wait_send()

    @pl.loop(1, spans)
    def _(j):
        for k in range(1, tiles):
            back(j, k).wait_send()

    @pl.loop(0, spans)
    def _(j):
        for k in range(1, tiles):
            echo(j, k).wait_send()

    @pl.when(az < length - 1)
    def _():
        @pl.loop(0, spans)
        def _(j):
            onward(j).wait_send()


def tail_body(raw_echo, phase_scaling, phase_range, phase_azimuth):
    tiles = lax.axis_size("tile")
    length = lax.axis_size("az")
    pulses = raw_echo.shape[1] * tiles
    extent, width = phase_scaling.shape
    count, ranges = phase_range.shape
    m, q, tail = extent // 4, pulses // 4, extent - pulses
    n_one, spans = ranges // LANES, width // LANES
    block = min(64, count)
    rows, lane = np.arange(m), np.arange(LANES)
    vmem = pl.BlockSpec(memory_space=pltpu.VMEM)
    anyspace = pl.BlockSpec(memory_space=pl.ANY)
    dma = pltpu.SemaphoreType.DMA
    c, s = roots(np.arange(n_one), lane, ranges, -1)
    return pl.pallas_call(
        functools.partial(focus_kernel, tiles, length, block),
        out_shape=jax.ShapeDtypeStruct((2, pulses, width), F32),
        in_specs=[anyspace] * 4 + [vmem] * 6,
        out_specs=vmem,
        scratch_shapes=[
            pltpu.VMEM((2, extent, width), F32),
            pltpu.VMEM((extent, width), F32),
            pltpu.VMEM((n_one, count, LANES), F32),
            pltpu.VMEM((extent, width), F32),
            pltpu.VMEM((2, count, ranges), F32),
            pltpu.VMEM((spans, 2, extent, LANES), F32),
            pltpu.VMEM((spans, 2, max(tail, pulses), LANES), F32),
            pltpu.VMEM((spans, 2, tail, LANES), F32),
            pltpu.VMEM((2, pulses, LANES), F32),
            pltpu.VMEM((n_one, block, 2 * LANES), BF16),
            pltpu.VMEM((n_one, block, 2 * LANES), BF16),
            pltpu.VMEM((2, n_one * block, LANES), F32),
            dma((spans, tiles - 1)),
            dma((spans, tiles - 1)),
            dma((spans,)),
            dma((count // block + 1, tiles - 1)),
            dma((count // block + 1, tiles - 1)),
            dma,
            dma((spans + 1, tiles - 1)),
            dma((spans + 1, tiles - 1)),
            dma((spans,)),
            dma((spans,)),
            dma((spans,)),
            dma((2,)),
            dma((n_one,)),
        ],
        compiler_params=pltpu.CompilerParams(
            collective_id=0, has_side_effects=True, vmem_limit_bytes=63 << 20
        ),
    )(
        raw_echo,
        phase_scaling,
        phase_range,
        phase_azimuth,
        left_table(rows, np.arange(q), m, -1),
        twist_table(4, m, extent, 1),
        right_table(lane, lane, LANES, -1),
        right_table(lane, lane, LANES, 1, 1.0 / ranges),
        np.stack([c, s]).astype(np.float32),
        left_table(rows, rows, m, 1, 1.0 / extent),
    )


def pair_rows(extent, chip, core):
    m = extent // 4
    return 2 * np.arange(m // 2) + chip + m * core


def pair_front(extent, pulses, tiles):
    out = []
    for t in range(tiles):
        rows = pair_rows(extent, t // 2, t % 2)
        out.append(np.stack([left_table(rows, 2 * np.arange(pulses // 2) + e, extent, -1) for e in (0, 1)], axis=1))
    return np.stack(out)


def filter_block(
    x_ref, base, block, scal_ref, fwd_ref, inv_ref, twist_ref, phase_ref, hi_ref, lo_ref, mid_ref
):
    n_one = phase_ref.shape[0]
    step = 16
    group = max(1, 256 // block)
    f_hi, f_lo = fwd_ref[0], fwd_ref[1]
    b_hi, b_lo = inv_ref[0], inv_ref[1]
    whole = pl.ds(pl.multiple_of(base, block), block)

    @pl.loop(0, n_one)
    def _(a):
        x = times((x_ref[0, whole, lanes(a)], x_ref[1, whole, lanes(a)]), sincos(scal_ref[whole, lanes(a)]))
        x_ref[0, whole, lanes(a)] = x[0]
        x_ref[1, whole, lanes(a)] = x[1]

    @pl.loop(0, block // step)
    def _(i):
        rows = pl.ds(pl.multiple_of(i * step, step), step)
        at = pl.ds(pl.multiple_of(base + i * step, step), step)
        v = [
            tuple(x_ref[c, at, pl.ds(a * LANES, LANES)] for c in (0, 1))
            for a in range(n_one)
        ]
        for k, x in enumerate(fft(v, -1)):
            if k:
                x = times(x, (twist_ref[0, k : k + 1, :], twist_ref[1, k : k + 1, :]))
            for c in (0, 1):
                h, l = split(x[c])
                hi_ref[k, rows, pl.ds(c * LANES, LANES)] = h
                lo_ref[k, rows, pl.ds(c * LANES, LANES)] = l

    @pl.loop(0, n_one // group)
    def _(i):
        ks = pl.ds(i * group, group)
        flat = (group * block, 2 * LANES)
        h, l = hi_ref[ks].reshape(flat), lo_ref[ks].reshape(flat)
        r = mm(h, f_hi) + mm(l, f_hi) + mm(h, f_lo)
        turn = phase_ref[ks, whole, :]
        r = times((r[:, :LANES], r[:, LANES:]), sincos(turn.reshape(group * block, LANES)))
        h, l = split(jnp.concatenate(r, axis=1))
        r = mm(h, b_hi) + mm(l, b_hi) + mm(h, b_lo)
        at = pl.ds(pl.multiple_of(i * group * block, block), group * block)
        mid_ref[0, at, :] = r[:, :LANES]
        mid_ref[1, at, :] = r[:, LANES:]

    @pl.loop(0, block // 8)
    def _(i):
        at = pl.ds(pl.multiple_of(base + i * 8, 8), 8)
        v = []
        for k in range(n_one):
            x = tuple(mid_ref[c, pl.ds(pl.multiple_of(k * block + i * 8, 8), 8), :] for c in (0, 1))
            if k:
                x = times(x, (twist_ref[0, k : k + 1, :], -twist_ref[1, k : k + 1, :]))
            v.append(x)
        for a, x in enumerate(fft(v, 1)):
            for c in (0, 1):
                x_ref[c, at, pl.ds(a * LANES, LANES)] = x[c]


def turn_rows(load, mid, turn, base):
    n_one = turn.shape[0]
    half = n_one * LANES // 2
    part = half // n_one
    per = half // LANES
    at = pl.ds(pl.multiple_of(base, LANES), LANES)

    @pl.loop(0, n_one)
    def _(g):
        mid[g // per, pl.ds(pl.multiple_of(g % per * LANES, LANES), LANES), :] = load(g).T

    @pl.loop(0, n_one)
    def _(k):
        rows = pl.ds(k, part, stride=n_one)
        x = jnp.concatenate([mid[h, rows, :] for h in range(LANES // part)], axis=0)
        turn[k, at, :] = x.T


def pair_kernel(
    n_strip, n_az, block, chunk,
    raw_ref, scaling_ref, range_ref, azimuth_ref, front_ref,
    twist_ref, fwd_ref, inv_ref, range_twist_ref, table_ref,
    o_ref,
    cols, prev, dop, scal, far, turn, phase, ret, for_core, for_chip, for_range,
    front, head, hi_ref, lo_ref, mid,
    load, load_range, load_echo, load_front, z_send, z_recv, y_send, y_recv, c_send, c_recv, f_send, f_recv,
    s_send, s_recv, p_send, p_recv, az_send, az_recv, x_send, x_recv,
    w_send, w_recv, w_local, v_send, v_recv, v_local, out_sem,
):
    t = lax.axis_index("tile")
    az = lax.axis_index("az")
    strip = lax.axis_index("strip")
    y, c = t // 2, t % 2
    tiles = 4
    count, ranges = range_ref.shape
    half = count // 2
    extent, width = scaling_ref.shape
    m = extent // 4
    pulses = o_ref.shape[1]
    q = pulses // 4
    rows_own = raw_ref.shape[1]
    spans = width // LANES
    n_one = ranges // LANES
    chunks = n_one // chunk
    blocks = count // block
    part = half // blocks
    whole = blocks // 2 + 1
    partner, across = {"tile": 2 * y + 1 - c}, {"tile": 2 * (1 - y) + c}
    other = pl.ds(pl.multiple_of(2 * (1 - y) * width, LANES), 2 * width)
    mine = pl.ds(pl.multiple_of(t * width, LANES), width)
    slab = strip * n_az + az

    def remote(src, dst, send, recv, device):
        return pltpu.make_async_remote_copy(
            src_ref=src, dst_ref=dst, send_sem=send, recv_sem=recv,
            device_id=device, device_id_type=pl.DeviceIdType.MESH,
        )

    def pulse_rows(tile):
        return pl.ds(pl.multiple_of(tile * rows_own, rows_own), rows_own)

    def groups(j):
        return pl.ds(j * chunk, chunk)

    def onward(a):
        return remote(
            raw_ref.at[:, :, lanes(a)], prev.at[a], z_send.at[a], z_recv.at[a],
            {"az": lax.rem(az + 1, n_az)},
        )

    def own_echo(a):
        return pltpu.make_async_copy(
            raw_ref.at[:, :, lanes(a)], cols.at[a, :, pulse_rows(t), :], load_echo.at[a]
        )

    def own_range(a):
        return pltpu.make_async_copy(range_ref.at[:, lanes(a)], turn.at[a], load_range.at[a])

    def own_phase(source, j, k):
        return pltpu.make_async_copy(source.at[:, lanes(j)], phase.at[j], load.at[k, j])

    def echo_across(j):
        return remote(
            prev.at[groups(j)], cols.at[groups(j), :, pulse_rows(t), :],
            y_send.at[j], y_recv.at[j], across,
        )

    def echo_core(j):
        at = cols.at[groups(j), :, pulse_rows(t), :]
        return remote(at, at, c_send.at[j], c_recv.at[j], partner)

    def echo_forward(j):
        at = cols.at[groups(j), :, pulse_rows(2 * (1 - y) + c), :]
        return remote(at, at, f_send.at[j], f_recv.at[j], partner)

    def scaling_core():
        return remote(for_core, scal.at[:, mine], s_send, s_recv, partner)

    def scaling_chip(k):
        to = {"tile": 2 * (1 - y) + lax.rem(c + k, 2)}
        return remote(
            for_chip.at[lax.rem(c + k, 2)],
            scal.at[pl.ds(pl.multiple_of(slab * block, block), block), mine],
            p_send.at[k], p_recv.at[k], to,
        )

    def far_rows(g):
        return far.at[pl.ds(pl.multiple_of(g * part, part), part), :]

    def scal_rows(g):
        return scal.at[pl.ds(pl.multiple_of(g * block, block), block), other]

    def range_chip():
        return remote(for_range, far_rows(slab), p_send.at[2], p_recv.at[2], across)

    def along(d, z, k):
        to = {"az": lax.rem(az + d, n_az)}
        at = (scal_rows, far_rows)[k](strip * n_az + z)
        return remote(at, at, az_send.at[d, k], az_recv.at[z, k], to)

    def sideways(z, k):
        at = (scal_rows, far_rows)[k](strip * n_az + z)
        return remote(at, at, x_send.at[z, k], x_recv.at[z, k], {"strip": 1 - strip})

    def order(n):
        return jnp.where(az + n < n_az, az + n, n_az - 1 - n)

    def place(n):
        s = y if n < n_az else 1 - y
        z = order(n % n_az)
        base = (s * n_az + z) * block
        row = (2 * s + c) * m + y * half + z * block
        return pl.ds(pl.multiple_of(base, block), block), pl.ds(pl.multiple_of(row, block), block), base

    def back(n, k):
        to = lax.rem(t + k, tiles)
        src, dst, _ = place(n)
        at = pl.ds(pl.multiple_of(to * width, LANES), width)
        return remote(
            dop.at[:, src, at], ret.at[:, dst, :], w_send.at[n, k - 1], w_recv.at[n, k - 1], {"tile": to}
        )

    def keep(n):
        src, dst, _ = place(n)
        return pltpu.make_async_copy(dop.at[:, src, mine], ret.at[:, dst, :], w_local.at[n])

    def back_span(j, n, k):
        to = lax.rem(t + k, tiles)
        src, dst, _ = place(n)
        return remote(
            dop.at[:, src, lanes(to * spans + j)], ret.at[:, dst, lanes(j)],
            v_send.at[j, n - whole, k - 1], v_recv.at[j, n - whole, k - 1], {"tile": to},
        )

    def keep_span(j, n):
        src, dst, _ = place(n)
        return pltpu.make_async_copy(
            dop.at[:, src, lanes(t * spans + j)], ret.at[:, dst, lanes(j)], v_local.at[j, n - whole]
        )

    def put(j):
        slot = lax.rem(j, 2)
        return pltpu.make_async_copy(head.at[slot], o_ref.at[:, :, lanes(j)], out_sem.at[slot])

    get_front = pltpu.make_async_copy(front_ref.at[t], front, load_front)

    @pl.loop(0, spans)
    def _(j):
        own_phase(scaling_ref, j, 0).start()

    @pl.loop(0, n_one)
    def _(a):
        own_range(a).start()

    @pl.loop(0, n_one)
    def _(a):
        own_echo(a).start()

    get_front.start()
    barrier = greet(
        [{"tile": lax.rem(t + k, tiles)} for k in range(1, tiles)]
        + [{"az": lax.rem(az + k, n_az)} for k in range(1, n_az)]
        + [{"strip": 1 - strip}]
    )
    pl.semaphore_wait(barrier, tiles + n_az - 1)

    @pl.when(az < n_az - 1)
    def _():
        @pl.loop(0, n_one)
        def _(a):
            onward(a).start()

    @pl.when(az == 0)
    def _():
        @pl.loop(0, n_one)
        def _(a):
            prev[a] = jnp.zeros((2, rows_own, LANES), F32)

    @pl.loop(0, spans)
    def _(j):
        own_phase(scaling_ref, j, 0).wait()
        for k in (0, 1):
            first = (2 * strip + k) * m + 2 * az * block + 1 - y
            for_chip[k, :, lanes(j)] = phase[j, pl.ds(first, block, stride=2), :]

    for k in (0, 1):
        scaling_chip(k).start()

    @pl.loop(0, n_one)
    def _(g):
        own_range(g).wait()
        for_range[:, lanes(g)] = turn[g, pl.ds(2 * part * slab + 1 - y, part, stride=2), :]

    range_chip().start()

    @pl.loop(0, spans)
    def _(j):
        for h in (0, 1):
            rows = pl.ds(h * half, half)
            for_core[rows, lanes(j)] = phase[j, pl.ds((2 * h + 1 - c) * m + y, half, stride=2), :]
            scal[rows, lanes(t * spans + j)] = phase[j, pl.ds((2 * h + c) * m + y, half, stride=2), :]

    scaling_core().start()
    turn_rows(lambda g: turn[g, pl.ds(y, half, stride=2), :], mid, turn, y * half)

    @pl.loop(0, spans)
    def _(j):
        own_phase(azimuth_ref, j, 1).start()

    get_front.wait()
    sign = (1 - 2 * y).astype(F32)

    @pl.loop(0, chunks + 3)
    def _(j):
        @pl.when(j < chunks)
        def _():
            for i in range(chunk):
                at = j * chunk + i
                own_echo(at).wait()

                @pl.when(az > 0)
                def _():
                    onward(at).wait_recv()

                for k in (0, 1):
                    a = cols[at, k, pulse_rows(t), :]
                    b = prev[at, k] * sign
                    cols[at, k, pulse_rows(t), :] = a + b
                    prev[at, k] = a - b
            echo_across(j).start()
            echo_core(j).start()

        @pl.when(j == 4)
        def _():
            for k in (0, 1):
                scaling_chip(k).wait_recv()
            range_chip().wait_recv()
            for k in (0, 1):
                sideways(az, k).start()
                for d in range(n_az - 1, 0, -1):
                    along(d, az, k).start()

        for d in range(1, n_az):
            @pl.when((j == chunks - n_az + d - 1) & (az + d < n_az))
            def _():
                for k in (0, 1):
                    along(n_az - d, az + d, k).wait_recv()
                    sideways(az + d, k).start()

        @pl.when((j >= 2) & (j < chunks + 2))
        def _():
            echo_across(j - 2).wait_recv()
            echo_forward(j - 2).start()

        @pl.when(j >= 3)
        def _():
            now = j - 3
            echo_core(now).wait_recv()
            echo_forward(now).wait_recv()
            r = []
            for e in (0, 1):
                rows = pl.ds(e, pulses // 2, stride=2)
                s = jnp.concatenate(
                    [
                        jnp.concatenate([cols[now * chunk + i, k, rows, :] for k in (0, 1)], axis=0)
                        for i in range(chunk)
                    ],
                    axis=1,
                )
                s_hi, s_lo = split(s)
                hi, lo = front[0, e], front[1, e]
                r.append(mm(hi, s_hi) + mm(hi, s_lo) + mm(lo, s_hi))
            for k in (0, 1):
                a, b = (x[k * half : (k + 1) * half] for x in r)
                at = pl.ds(pl.multiple_of(now * chunk * LANES, LANES), chunk * LANES)
                dop[k, pl.ds(0, half), at] = a + b
                dop[k, pl.ds(half, half), at] = a - b

    scaling_core().wait_recv()

    for n in range(blocks):
        if n < n_az:
            z = order(n)

            @pl.when(az + n >= n_az)
            def _():
                for k in (0, 1):
                    along(n_az - 1, z, k).wait_recv()
                    sideways(z, k).start()

            for k in (0, 1):
                sideways(z, k).wait_recv()
        if n == n_az:
            turn_rows(lambda g: far[:, lanes(g)], mid, turn, (1 - y) * half)
        filter_block(
            dop, place(n)[2], block, scal, fwd_ref, inv_ref, range_twist_ref, turn, hi_ref, lo_ref, mid
        )
        if n < whole:
            for k in range(tiles - 1, 0, -1):
                back(n, k).start()
            keep(n).start()

    @pl.loop(0, spans)
    def _(j):
        for n in range(whole, blocks):
            for k in range(tiles - 1, 0, -1):
                back_span(j, n, k).start()
            keep_span(j, n).start()

    @pl.loop(0, spans)
    def _(j):
        own_phase(azimuth_ref, j, 1).wait()

    for n in range(whole):
        for k in range(1, tiles):
            back(n, k).wait_recv()
        keep(n).wait()

    @pl.loop(0, spans)
    def _(j):
        for n in range(whole, blocks):
            for k in range(1, tiles):
                back_span(j, n, k).wait_recv()
            keep_span(j, n).wait()
        hi, lo = table_ref[0], table_ref[1]
        slot = lax.rem(j, 2)

        @pl.when(j > 1)
        def _():
            put(j - 2).wait()

        v = []
        for f in range(4):
            rows = pl.ds(f * m, m)
            angle = jnp.concatenate(
                [phase[j, pl.ds(f * m + p, half, stride=2), :] for p in (0, 1)], axis=0
            )
            v.append(times((ret[0, rows, lanes(j)], ret[1, rows, lanes(j)]), sincos(angle)))
        for e, x in enumerate(four(v, 1)):
            if e:
                x = times(x, (twist_ref[0, e], twist_ref[1, e]))
            s_hi, s_lo = split(jnp.concatenate(x, axis=0))
            r = mm(hi, s_hi) + mm(hi, s_lo) + mm(lo, s_hi)
            for k in (0, 1):
                head[slot, k, pl.ds(e, q, stride=4), :] = r[k * q : (k + 1) * q]
        put(j).start()

    for j in range(max(0, spans - 2), spans):
        put(j).wait()

    @pl.when(az < n_az - 1)
    def _():
        @pl.loop(0, n_one)
        def _(a):
            onward(a).wait_send()

    @pl.loop(0, chunks)
    def _(j):
        echo_across(j).wait_send()
        echo_core(j).wait_send()
        echo_forward(j).wait_send()

    scaling_core().wait_send()
    range_chip().wait_send()
    for k in (0, 1):
        scaling_chip(k).wait_send()
        for d in range(1, n_az):
            along(d, az, k).wait_send()
        for z in range(n_az):
            sideways(z, k).wait_send()
    for n in range(whole):
        for k in range(1, tiles):
            back(n, k).wait_send()

    @pl.loop(0, spans)
    def _(j):
        for n in range(whole, blocks):
            for k in range(1, tiles):
                back_span(j, n, k).wait_send()


def pair_body(raw_echo, phase_scaling, phase_range, phase_azimuth):
    tiles = lax.axis_size("tile")
    n_az, n_strip = lax.axis_size("az"), lax.axis_size("strip")
    pulses = raw_echo.shape[1] * tiles
    extent, width = phase_scaling.shape
    count, ranges = phase_range.shape
    m, q, half = extent // 4, pulses // 4, count // 2
    n_one, spans = ranges // LANES, width // LANES
    blocks = n_strip * n_az
    block = count // blocks
    chunk = 2
    chunks = n_one // chunk
    whole = blocks // 2 + 1
    rest = blocks - whole
    fine = np.concatenate([np.arange(0, m, 2), np.arange(1, m, 2)])
    lane = np.arange(LANES)
    vmem = pl.BlockSpec(memory_space=pltpu.VMEM)
    anyspace = pl.BlockSpec(memory_space=pl.ANY)
    dma = pltpu.SemaphoreType.DMA
    c, s = roots(np.arange(n_one), lane, ranges, -1)
    return pl.pallas_call(
        functools.partial(pair_kernel, n_strip, n_az, block, chunk),
        out_shape=jax.ShapeDtypeStruct((2, pulses, width), F32),
        in_specs=[anyspace] * 5 + [vmem] * 5,
        out_specs=anyspace,
        scratch_shapes=[
            pltpu.VMEM((n_one, 2, pulses, LANES), F32),
            pltpu.VMEM((n_one, 2, pulses // tiles, LANES), F32),
            pltpu.VMEM((2, count, ranges), F32),
            pltpu.VMEM((count, ranges), F32),
            pltpu.VMEM((half, ranges), F32),
            pltpu.VMEM((n_one, count, LANES), F32),
            pltpu.VMEM((spans, extent, LANES), F32),
            pltpu.VMEM((2, extent, width), F32),
            pltpu.VMEM((count, width), F32),
            pltpu.VMEM((2, block, width), F32),
            pltpu.VMEM((half // blocks, ranges), F32),
            pltpu.VMEM((2, 2, count, pulses), BF16),
            pltpu.VMEM((2, 2, pulses, LANES), F32),
            pltpu.VMEM((n_one, block, 2 * LANES), BF16),
            pltpu.VMEM((n_one, block, 2 * LANES), BF16),
            pltpu.VMEM((2, n_one * LANES // 2, LANES), F32),
            dma((2, spans)), dma((n_one,)), dma((n_one,)), dma,
            dma((n_one,)), dma((n_one,)),
            dma((chunks,)), dma((chunks,)),
            dma((chunks,)), dma((chunks,)),
            dma((chunks,)), dma((chunks,)),
            dma, dma,
            dma((3,)), dma((3,)),
            dma((n_az, 2)), dma((n_az, 2)),
            dma((n_az, 2)), dma((n_az, 2)),
            dma((whole, tiles - 1)), dma((whole, tiles - 1)), dma((whole,)),
            dma((spans, rest, tiles - 1)), dma((spans, rest, tiles - 1)), dma((spans, rest)),
            dma((2,)),
        ],
        compiler_params=pltpu.CompilerParams(
            collective_id=0, has_side_effects=True, vmem_limit_bytes=63 << 20
        ),
    )(
        raw_echo,
        phase_scaling,
        phase_range,
        phase_azimuth,
        pair_front(extent, pulses, tiles),
        np.ascontiguousarray(twist_table(4, m, extent, 1)[:, :, fine]),
        right_table(lane, lane, LANES, -1),
        right_table(lane, lane, LANES, 1, 1.0 / ranges),
        np.stack([c, s]).astype(np.float32),
        left_table(np.arange(q), fine, m, 1, 1.0 / extent),
    )


def paired(raw_echo, phase_scaling, phase_range):
    tiles, n_az, n_strip = (lax.axis_size(a) for a in ("tile", "az", "strip"))
    count = phase_range.shape[0]
    blocks = n_az * n_strip
    return (
        tiles == 4
        and n_strip == 2
        and n_az > 1
        and count == 2 * LANES
        and phase_scaling.shape[0] == 2 * raw_echo.shape[1] * tiles
        and count % (16 * blocks) == 0
        and phase_range.shape[1] % (2 * LANES) == 0
    )


def body(raw_echo, phase_scaling, phase_range, phase_azimuth):
    plan = pair_body if paired(raw_echo, phase_scaling, phase_range) else tail_body
    return plan(raw_echo, phase_scaling, phase_range, phase_azimuth)


def solution(mesh):
    return jax.shard_map(
        body,
        mesh=mesh,
        in_specs=(
            P(None, ("strip", "az", "tile"), None),
            P(None, "tile"),
            P("tile", None),
            P(None, "tile"),
        ),
        out_specs=P(None, ("strip", "az"), "tile"),
        check_vma=False,
    )
```

```python
import functools
import math

import jax
import jax.numpy as jnp
import numpy as np
from jax import lax
from jax.experimental import pallas as pl
from jax.experimental.pallas import tpu as pltpu
from jax.sharding import PartitionSpec as P

F32 = jnp.float32
BF16 = jnp.bfloat16
LANES = 128


def halves(table):
    hi = np.asarray(table, np.float32).astype(jnp.bfloat16)
    lo = (np.asarray(table, np.float64) - hi.astype(np.float64)).astype(jnp.bfloat16)
    return np.stack([hi, lo])


def roots(rows, cols, modulus, direction):
    residue = np.outer(rows, cols) % modulus
    angle = residue * (direction * 2.0 * math.pi / modulus)
    return np.cos(angle), np.sin(angle)


def left_table(rows, cols, modulus, direction, scale=1.0):
    c, s = roots(rows, cols, modulus, direction)
    return halves(np.block([[c, -s], [s, c]]) * scale)


def right_table(rows, cols, modulus, direction, scale=1.0):
    c, s = roots(rows, cols, modulus, direction)
    return halves(np.block([[c, s], [-s, c]]) * scale)


def twist_table(count, length, modulus, direction):
    c, s = roots(np.arange(count), np.arange(length), modulus, direction)
    full = np.stack([c, s]).astype(np.float32)
    return np.ascontiguousarray(np.broadcast_to(full[..., None], full.shape + (LANES,)))


def split(x):
    hi = x.astype(BF16)
    return hi, (x - hi.astype(F32)).astype(BF16)


def mm(a, b):
    return jnp.dot(a, b, preferred_element_type=F32)


def times(a, t):
    return a[0] * t[0] - a[1] * t[1], a[0] * t[1] + a[1] * t[0]


def plus(a, b):
    return a[0] + b[0], a[1] + b[1]


def minus(a, b):
    return a[0] - b[0], a[1] - b[1]


def quarter(a, direction):
    return (-a[1], a[0]) if direction > 0 else (a[1], -a[0])


def four(v, direction):
    a, b = plus(v[0], v[2]), minus(v[0], v[2])
    c, d = plus(v[1], v[3]), quarter(minus(v[1], v[3]), direction)
    return [plus(a, c), plus(b, d), minus(a, c), minus(b, d)]


def fft(v, direction):
    n = len(v)
    if n == 1:
        return v
    if n == 2:
        return [plus(v[0], v[1]), minus(v[0], v[1])]
    if n == 4:
        return four(v, direction)
    parts = [fft(v[e::4], direction) for e in range(4)] if n % 4 == 0 else None
    out = [None] * n
    m = n // 4
    for f in range(m):
        items = []
        for e in range(4):
            x = parts[e][f]
            k = e * f % n
            if k == 0:
                pass
            elif 8 * k == n:
                h = np.float32(math.sqrt(0.5))
                q = quarter(x, direction)
                x = ((x[0] + q[0]) * h, (x[1] + q[1]) * h)
            elif 4 * k == n:
                x = quarter(x, direction)
            elif 8 * k == 3 * n:
                h = np.float32(math.sqrt(0.5))
                q = quarter(x, direction)
                x = ((q[0] - x[0]) * h, (q[1] - x[1]) * h)
            else:
                ang = direction * 2.0 * math.pi * k / n
                x = times(x, (np.float32(math.cos(ang)), np.float32(math.sin(ang))))
            items.append(x)
        got = four(items, direction)
        for j in range(4):
            out[f + j * m] = got[j]
    return out


def sincos(x):
    y = x * 0.5
    z = y * y
    s, c = -1.0 / 39916800, 1.0 / 479001600
    for a, b in ((362880, -3628800), (-5040, 40320), (120, -720), (-6, 24), (1, -2)):
        s = s * z + np.float32(1.0 / a)
        c = c * z + np.float32(1.0 / b)
    s = s * y
    c = c * z + 1.0
    return 1.0 - 2.0 * s * s, 2.0 * s * c


def greet(partners):
    barrier = pltpu.get_barrier_semaphore()
    for device in partners:
        pl.semaphore_signal(barrier, inc=1, device_id=device, device_id_type=pl.DeviceIdType.MESH)
    return barrier


def lanes(j):
    return pl.ds(pl.multiple_of(j * LANES, LANES), LANES)


def filter_rows(x_ref, base, block, fwd_ref, inv_ref, twist_ref, phase_ref, hi_ref, lo_ref, mid_ref):
    n_one = phase_ref.shape[0]
    step = 16
    f_hi, f_lo = fwd_ref[0], fwd_ref[1]
    b_hi, b_lo = inv_ref[0], inv_ref[1]

    @pl.loop(0, block // step)
    def _(i):
        rows = pl.ds(pl.multiple_of(i * step, step), step)
        at = pl.ds(pl.multiple_of(base + i * step, step), step)
        v = [
            tuple(x_ref[c, at, pl.ds(a * LANES, LANES)] for c in (0, 1))
            for a in range(n_one)
        ]
        for k, x in enumerate(fft(v, -1)):
            if k:
                x = times(x, (twist_ref[0, k : k + 1, :], twist_ref[1, k : k + 1, :]))
            for c in (0, 1):
                h, l = split(x[c])
                hi_ref[k, rows, pl.ds(c * LANES, LANES)] = h
                lo_ref[k, rows, pl.ds(c * LANES, LANES)] = l

    group = 4

    @pl.loop(0, n_one // group)
    def _(i):
        ks = pl.ds(i * group, group)
        flat = (group * block, 2 * LANES)
        h, l = hi_ref[ks].reshape(flat), lo_ref[ks].reshape(flat)
        r = mm(h, f_hi) + mm(l, f_hi) + mm(h, f_lo)
        turn = phase_ref[ks, pl.ds(pl.multiple_of(base, block), block), :]
        r = times((r[:, :LANES], r[:, LANES:]), sincos(turn.reshape(group * block, LANES)))
        h, l = split(jnp.concatenate(r, axis=1))
        r = mm(h, b_hi) + mm(l, b_hi) + mm(h, b_lo)
        at = pl.ds(pl.multiple_of(i * group * block, block), group * block)
        mid_ref[0, at, :] = r[:, :LANES]
        mid_ref[1, at, :] = r[:, LANES:]

    @pl.loop(0, block // 8)
    def _(i):
        at = pl.ds(pl.multiple_of(base + i * 8, 8), 8)
        v = []
        for k in range(n_one):
            x = tuple(mid_ref[c, pl.ds(pl.multiple_of(k * block + i * 8, 8), 8), :] for c in (0, 1))
            if k:
                x = times(x, (twist_ref[0, k : k + 1, :], -twist_ref[1, k : k + 1, :]))
            v.append(x)
        for a, x in enumerate(fft(v, 1)):
            for c in (0, 1):
                x_ref[c, at, pl.ds(a * LANES, LANES)] = x[c]


def permute_turn(o_ref, mid, turn):
    n_one, count, _ = turn.shape
    half = mid.shape[1]
    some = min(count, LANES)
    part = half // n_one

    @pl.loop(0, count // some)
    def _(i):
        @pl.loop(0, n_one)
        def _(g):
            c, row, j = piece(g, count, o_ref)
            at = pl.ds(pl.multiple_of(row + i * some, some), some)
            x = o_ref[c, at, lanes(j)]
            if some < LANES:
                x = jnp.concatenate([x] * (LANES // some), axis=0)
            per = half // LANES
            mid[g // per, pl.ds(pl.multiple_of(g % per * LANES, LANES), LANES), :] = x.T

        @pl.loop(0, n_one)
        def _(k):
            rows = pl.ds(k, part, stride=n_one)
            x = jnp.concatenate([mid[h, rows, :] for h in range(LANES // part)], axis=0)
            at = pl.ds(pl.multiple_of(i * some, some), some)
            turn[k, at, :] = x.T[:some]


def piece(g, count, o_ref):
    across = o_ref.shape[2] // LANES
    down = o_ref.shape[1] // count
    return g // (across * down), g // across % down * count, g % across


def focus_kernel(
    tiles, length, block,
    raw_ref, scaling_ref, range_ref, azimuth_ref,
    front_ref, twist_ref, fwd_ref, inv_ref, range_twist_ref, table_ref,
    o_ref,
    spec, scaling, turn, phase, dop, ret, tail_out, tail_in, head, hi_ref, lo_ref, mid,
    send_e, recv_e, local_e, send_a, recv_a, local_a, send_b, recv_b, local_b,
    send_c, recv_c, load, load_range,
):
    me = lax.axis_index("tile")
    az = lax.axis_index("az")
    count = dop.shape[1]
    width = o_ref.shape[2]
    pulses = o_ref.shape[1]
    tail = tail_in.shape[2]
    rows_own = raw_ref.shape[1]
    n_one = turn.shape[0]
    blocks = count // block
    early = (blocks - 1) * block
    spans = width // LANES
    cols = tail_out
    m = spec.shape[1] // 4
    q = pulses // 4
    mine = pl.ds(pl.multiple_of(me * width, LANES), width)
    own = pl.ds(pl.multiple_of(me * count, count), count)
    own_pulses = pl.ds(pl.multiple_of(me * rows_own, rows_own), rows_own)

    def remote(src, dst, send, recv, device):
        return pltpu.make_async_remote_copy(
            src_ref=src, dst_ref=dst, send_sem=send, recv_sem=recv,
            device_id=device, device_id_type=pl.DeviceIdType.MESH,
        )

    def echo(j, k):
        to = lax.rem(me + k, tiles)
        return remote(
            raw_ref.at[:, :, lanes(to * spans + j)], cols.at[j, :, own_pulses, :],
            send_e.at[j, k - 1], recv_e.at[j, k - 1], {"tile": to},
        )

    def keep_echo(j):
        return pltpu.make_async_copy(
            raw_ref.at[:, :, lanes(me * spans + j)], cols.at[j, :, own_pulses, :], local_e.at[j]
        )

    def load_piece(g):
        c, row, j = piece(g, count, o_ref)
        return pltpu.make_async_copy(
            range_ref.at[:, lanes(g)],
            o_ref.at[c, pl.ds(pl.multiple_of(row, count), count), lanes(j)],
            load_range.at[g],
        )

    def out_part(i, k, lo, n, slot):
        to = lax.rem(me + k, tiles)
        at = pl.ds(pl.multiple_of(me * width + lo, LANES), n)
        return remote(
            spec.at[:, pl.ds(pl.multiple_of(to * count + i * block, block), block), pl.ds(lo, n)],
            dop.at[:, pl.ds(pl.multiple_of(i * block, block), block), at],
            send_a.at[slot, k - 1], recv_a.at[slot, k - 1], {"tile": to},
        )

    def out(i, k):
        return out_part(i, k, 0, width, i)

    def first_out(k):
        return out_part(0, k, 0, width - LANES, blocks)

    def last_out(k):
        return out_part(0, k, width - LANES, LANES, 0)

    def back_rows(j, k, lo, n, slot):
        to = lax.rem(me + k, tiles)
        return remote(
            dop.at[:, pl.ds(lo, n), lanes(to * spans + j)],
            ret.at[j, :, pl.ds(pl.multiple_of(me * count + lo, 8), n), :],
            send_b.at[slot, k - 1], recv_b.at[slot, k - 1], {"tile": to},
        )

    def first_rows(k):
        return back_rows(0, k, 0, early, spans)

    def last_rows(k):
        return back_rows(0, k, early, count - early, 0)

    def back(j, k):
        return back_rows(j, k, 0, count, j)

    def keep(j):
        return pltpu.make_async_copy(
            dop.at[:, :, lanes(me * spans + j)], ret.at[j, :, own, :], local_b.at[j]
        )

    def onward(j):
        return remote(
            tail_out.at[j, :, pl.ds(0, tail), :], tail_in.at[j], send_c.at[j], recv_c.at[j],
            {"az": lax.rem(az + 1, length)},
        )

    barrier = greet(
        [{"tile": lax.rem(me + k, tiles)} for k in range(1, tiles)]
        + [{"az": lax.rem(az + 1, length)}, {"az": lax.rem(az + length - 1, length)}]
    )
    get_scaling = pltpu.make_async_copy(scaling_ref, scaling, load.at[0])
    get_phase = pltpu.make_async_copy(azimuth_ref, phase, load.at[1])
    pl.semaphore_wait(barrier, tiles + 1)

    @pl.loop(0, spans)
    def _(j):
        for k in range(1, tiles):
            echo(j, k).start()
        keep_echo(j).start()

    @pl.loop(0, n_one)
    def _(g):
        load_piece(g).start()

    get_scaling.start()
    get_phase.start()

    get_scaling.wait()

    @pl.loop(0, spans)
    def _(j):
        @pl.when(j == spans - 1)
        def _():
            for k in range(1, tiles):
                first_out(k).start()

        for k in range(1, tiles):
            echo(j, k).wait_recv()
        keep_echo(j).wait()
        hi, lo = front_ref[0], front_ref[1]
        z = []
        for e in range(4):
            rows = pl.ds(e, q, stride=4)
            s = jnp.concatenate([cols[j, 0, rows, :], cols[j, 1, rows, :]], axis=0)
            s_hi, s_lo = split(s)
            r = mm(hi, s_hi) + mm(hi, s_lo) + mm(lo, s_hi)
            r = (r[:m], r[m:])
            if e:
                r = times(r, (twist_ref[0, e], -twist_ref[1, e]))
            z.append(r)
        for f, x in enumerate(four(z, -1)):
            rows = pl.ds(f * m, m)
            x = times(x, sincos(scaling[rows, lanes(j)]))
            spec[0, rows, lanes(j)] = x[0]
            spec[1, rows, lanes(j)] = x[1]

    for k in range(1, tiles):
        last_out(k).start()

    @pl.loop(1, blocks)
    def _(i):
        for k in range(1, tiles):
            out(i, k).start()

    first = pltpu.make_async_copy(spec.at[:, own, :], dop.at[:, :, mine], local_a)
    first.start()

    @pl.loop(0, n_one)
    def _(g):
        load_piece(g).wait()

    permute_turn(o_ref, mid, turn)
    first.wait()

    @pl.loop(0, blocks)
    def _(i):
        if early:
            @pl.when(i == blocks - 1)
            def _():
                for k in range(1, tiles):
                    first_rows(k).start()

        @pl.when(i == 0)
        def _():
            for k in range(1, tiles):
                first_out(k).wait_recv()
                last_out(k).wait_recv()

        @pl.when(i > 0)
        def _():
            for k in range(1, tiles):
                out(i, k).wait_recv()

        filter_rows(
            dop, i * block, block, fwd_ref, inv_ref, range_twist_ref, turn,
            hi_ref, lo_ref, mid,
        )

    for k in range(1, tiles):
        last_rows(k).start()
    keep(0).start()

    @pl.loop(1, spans)
    def _(j):
        for k in range(1, tiles):
            back(j, k).start()
        keep(j).start()

    get_phase.wait()

    @pl.loop(0, spans)
    def _(j):
        @pl.when(j == 0)
        def _():
            for k in range(1, tiles):
                if early:
                    first_rows(k).wait_recv()
                last_rows(k).wait_recv()

        @pl.when(j > 0)
        def _():
            for k in range(1, tiles):
                back(j, k).wait_recv()

        keep(j).wait()
        hi, lo = table_ref[0], table_ref[1]
        v = []
        for f in range(4):
            rows = pl.ds(f * m, m)
            v.append(times((ret[j, 0, rows, :], ret[j, 1, rows, :]), sincos(phase[rows, lanes(j)])))
        for e, x in enumerate(four(v, 1)):
            if e:
                x = times(x, (twist_ref[0, e], twist_ref[1, e]))
            s_hi, s_lo = split(jnp.concatenate(x, axis=0))
            r = mm(hi, s_hi) + mm(hi, s_lo) + mm(lo, s_hi)
            for c in (0, 1):
                head[c, pl.ds(e, q, stride=4), :] = r[c * m : c * m + q]
                tail_out[j, c, pl.ds(e, m - q, stride=4), :] = r[c * m + q : (c + 1) * m]

        @pl.when(az < length - 1)
        def _():
            onward(j).start()

        o_ref[:, :, lanes(j)] = head[...]

    @pl.when(az > 0)
    def _():
        @pl.loop(0, spans)
        def _(j):
            onward(j).wait_recv()
            o_ref[:, pl.ds(0, tail), lanes(j)] += tail_in[j]

    for k in range(1, tiles):
        first_out(k).wait_send()
        last_out(k).wait_send()

    @pl.loop(1, blocks)
    def _(i):
        for k in range(1, tiles):
            out(i, k).wait_send()

    for k in range(1, tiles):
        if early:
            first_rows(k).wait_send()
        last_rows(k).wait_send()

    @pl.loop(1, spans)
    def _(j):
        for k in range(1, tiles):
            back(j, k).wait_send()

    @pl.loop(0, spans)
    def _(j):
        for k in range(1, tiles):
            echo(j, k).wait_send()

    @pl.when(az < length - 1)
    def _():
        @pl.loop(0, spans)
        def _(j):
            onward(j).wait_send()


def tail_body(raw_echo, phase_scaling, phase_range, phase_azimuth):
    tiles = lax.axis_size("tile")
    length = lax.axis_size("az")
    pulses = raw_echo.shape[1] * tiles
    extent, width = phase_scaling.shape
    count, ranges = phase_range.shape
    m, q, tail = extent // 4, pulses // 4, extent - pulses
    n_one, spans = ranges // LANES, width // LANES
    block = min(64, count)
    rows, lane = np.arange(m), np.arange(LANES)
    vmem = pl.BlockSpec(memory_space=pltpu.VMEM)
    anyspace = pl.BlockSpec(memory_space=pl.ANY)
    dma = pltpu.SemaphoreType.DMA
    c, s = roots(np.arange(n_one), lane, ranges, -1)
    return pl.pallas_call(
        functools.partial(focus_kernel, tiles, length, block),
        out_shape=jax.ShapeDtypeStruct((2, pulses, width), F32),
        in_specs=[anyspace] * 4 + [vmem] * 6,
        out_specs=vmem,
        scratch_shapes=[
            pltpu.VMEM((2, extent, width), F32),
            pltpu.VMEM((extent, width), F32),
            pltpu.VMEM((n_one, count, LANES), F32),
            pltpu.VMEM((extent, width), F32),
            pltpu.VMEM((2, count, ranges), F32),
            pltpu.VMEM((spans, 2, extent, LANES), F32),
            pltpu.VMEM((spans, 2, max(tail, pulses), LANES), F32),
            pltpu.VMEM((spans, 2, tail, LANES), F32),
            pltpu.VMEM((2, pulses, LANES), F32),
            pltpu.VMEM((n_one, block, 2 * LANES), BF16),
            pltpu.VMEM((n_one, block, 2 * LANES), BF16),
            pltpu.VMEM((2, n_one * block, LANES), F32),
            dma((spans, tiles - 1)),
            dma((spans, tiles - 1)),
            dma((spans,)),
            dma((count // block + 1, tiles - 1)),
            dma((count // block + 1, tiles - 1)),
            dma,
            dma((spans + 1, tiles - 1)),
            dma((spans + 1, tiles - 1)),
            dma((spans,)),
            dma((spans,)),
            dma((spans,)),
            dma((2,)),
            dma((n_one,)),
        ],
        compiler_params=pltpu.CompilerParams(
            collective_id=0, has_side_effects=True, vmem_limit_bytes=63 << 20
        ),
    )(
        raw_echo,
        phase_scaling,
        phase_range,
        phase_azimuth,
        left_table(rows, np.arange(q), m, -1),
        twist_table(4, m, extent, 1),
        right_table(lane, lane, LANES, -1),
        right_table(lane, lane, LANES, 1, 1.0 / ranges),
        np.stack([c, s]).astype(np.float32),
        left_table(rows, rows, m, 1, 1.0 / extent),
    )


def pair_front(extent, pulses):
    m = extent // 4
    return np.stack(
        [left_table(2 * np.arange(m // 2) + y, 2 * np.arange(pulses // 2), extent, -1) for y in (0, 1)]
    )


def pair_twists(extent, fine):
    m = extent // 4
    out = np.zeros((m, LANES), np.float32)
    for e in range(1, 4):
        c, s = roots(fine, [e], extent, 1)
        out[:, 2 * e - 2 : 2 * e - 1], out[:, 2 * e - 1 : 2 * e] = c, s
    for t in range(4):
        c, s = roots(2 * np.arange(m // 2) + t // 2 + m * (t % 2), [1], extent, -1)
        out[: m // 2, 6 + 2 * t : 7 + 2 * t], out[: m // 2, 7 + 2 * t : 8 + 2 * t] = c, s
    return out


def filter_block(
    x_ref, base, block, scal_ref, fwd_ref, inv_ref, twist_ref, phase_ref, hi_ref, lo_ref, mid_ref
):
    n_one = phase_ref.shape[0]
    step = 16
    group = max(1, 256 // block)
    f_hi, f_lo = fwd_ref[0], fwd_ref[1]
    b_hi, b_lo = inv_ref[0], inv_ref[1]
    whole = pl.ds(pl.multiple_of(base, block), block)

    @pl.loop(0, n_one)
    def _(a):
        x = times((x_ref[0, whole, lanes(a)], x_ref[1, whole, lanes(a)]), sincos(scal_ref[whole, lanes(a)]))
        x_ref[0, whole, lanes(a)] = x[0]
        x_ref[1, whole, lanes(a)] = x[1]

    @pl.loop(0, block // step)
    def _(i):
        rows = pl.ds(pl.multiple_of(i * step, step), step)
        at = pl.ds(pl.multiple_of(base + i * step, step), step)
        v = [
            tuple(x_ref[c, at, pl.ds(a * LANES, LANES)] for c in (0, 1))
            for a in range(n_one)
        ]
        for k, x in enumerate(fft(v, -1)):
            if k:
                x = times(x, (twist_ref[0, k : k + 1, :], twist_ref[1, k : k + 1, :]))
            for c in (0, 1):
                h, l = split(x[c])
                hi_ref[k, rows, pl.ds(c * LANES, LANES)] = h
                lo_ref[k, rows, pl.ds(c * LANES, LANES)] = l

    @pl.loop(0, n_one // group)
    def _(i):
        ks = pl.ds(i * group, group)
        flat = (group * block, 2 * LANES)
        h, l = hi_ref[ks].reshape(flat), lo_ref[ks].reshape(flat)
        r = mm(h, f_hi) + mm(l, f_hi) + mm(h, f_lo)
        turn = phase_ref[ks, whole, :]
        r = times((r[:, :LANES], r[:, LANES:]), sincos(turn.reshape(group * block, LANES)))
        h, l = split(jnp.concatenate(r, axis=1))
        r = mm(h, b_hi) + mm(l, b_hi) + mm(h, b_lo)
        at = pl.ds(pl.multiple_of(i * group * block, block), group * block)
        mid_ref[0, at, :] = r[:, :LANES]
        mid_ref[1, at, :] = r[:, LANES:]

    @pl.loop(0, block // 8)
    def _(i):
        at = pl.ds(pl.multiple_of(base + i * 8, 8), 8)
        v = []
        for k in range(n_one):
            x = tuple(mid_ref[c, pl.ds(pl.multiple_of(k * block + i * 8, 8), 8), :] for c in (0, 1))
            if k:
                x = times(x, (twist_ref[0, k : k + 1, :], -twist_ref[1, k : k + 1, :]))
            v.append(x)
        for a, x in enumerate(fft(v, 1)):
            for c in (0, 1):
                x_ref[c, at, pl.ds(a * LANES, LANES)] = x[c]


def turn_rows(load, mid, turn, base):
    n_one = turn.shape[0]
    half = n_one * LANES // 2
    part = half // n_one
    per = half // LANES
    at = pl.ds(pl.multiple_of(base, LANES), LANES)

    @pl.loop(0, n_one)
    def _(g):
        mid[g // per, pl.ds(pl.multiple_of(g % per * LANES, LANES), LANES), :] = load(g).T

    @pl.loop(0, n_one)
    def _(k):
        rows = pl.ds(k, part, stride=n_one)
        x = jnp.concatenate([mid[h, rows, :] for h in range(LANES // part)], axis=0)
        turn[k, at, :] = x.T


def pair_kernel(
    n_strip, n_az, block, chunk,
    raw_ref, scaling_ref, range_ref, azimuth_ref, front_ref,
    twists_ref, fwd_ref, inv_ref, range_twist_ref, table_ref,
    o_ref,
    cols, prev, dop, scal, far, turn, phase, ret, for_core, for_chip, for_range,
    front, turn_front, twist_ref, head, hi_ref, lo_ref, mid,
    load, load_range, load_echo, load_front, z_send, z_recv, y_send, y_recv, c_send, c_recv, f_send, f_recv,
    s_send, s_recv, p_send, p_recv, az_send, az_recv, x_send, x_recv,
    w_send, w_recv, w_local, v_send, v_recv, v_local, out_sem,
):
    t = lax.axis_index("tile")
    az = lax.axis_index("az")
    strip = lax.axis_index("strip")
    y, c = t // 2, t % 2
    tiles = 4
    count, ranges = range_ref.shape
    half = count // 2
    extent, width = scaling_ref.shape
    m = extent // 4
    pulses = o_ref.shape[1]
    q = pulses // 4
    rows_own = raw_ref.shape[1]
    spans = width // LANES
    n_one = ranges // LANES
    chunks = n_one // chunk
    blocks = count // block
    part = half // blocks
    whole = blocks // 2 + 1
    partner, across = {"tile": 2 * y + 1 - c}, {"tile": 2 * (1 - y) + c}
    other = pl.ds(pl.multiple_of(2 * (1 - y) * width, LANES), 2 * width)
    mine = pl.ds(pl.multiple_of(t * width, LANES), width)
    slab = strip * n_az + az

    def remote(src, dst, send, recv, device):
        return pltpu.make_async_remote_copy(
            src_ref=src, dst_ref=dst, send_sem=send, recv_sem=recv,
            device_id=device, device_id_type=pl.DeviceIdType.MESH,
        )

    def pulse_rows(tile):
        return pl.ds(pl.multiple_of(tile * rows_own, rows_own), rows_own)

    def groups(j):
        return pl.ds(j * chunk, chunk)

    def onward(a):
        return remote(
            raw_ref.at[:, :, lanes(a)], prev.at[a], z_send.at[a], z_recv.at[a],
            {"az": lax.rem(az + 1, n_az)},
        )

    def own_echo(a):
        return pltpu.make_async_copy(
            raw_ref.at[:, :, lanes(a)], cols.at[a, :, pulse_rows(t), :], load_echo.at[a]
        )

    def own_range(a):
        return pltpu.make_async_copy(range_ref.at[:, lanes(a)], turn.at[a], load_range.at[a])

    def own_phase(source, j, k):
        return pltpu.make_async_copy(source.at[:, lanes(j)], phase.at[j], load.at[k, j])

    def echo_across(j):
        return remote(
            prev.at[groups(j)], cols.at[groups(j), :, pulse_rows(t), :],
            y_send.at[j], y_recv.at[j], across,
        )

    def echo_core(j):
        at = cols.at[groups(j), :, pulse_rows(t), :]
        return remote(at, at, c_send.at[j], c_recv.at[j], partner)

    def echo_forward(j):
        at = cols.at[groups(j), :, pulse_rows(2 * (1 - y) + c), :]
        return remote(at, at, f_send.at[j], f_recv.at[j], partner)

    def scaling_core():
        return remote(for_core, scal.at[:, mine], s_send, s_recv, partner)

    def scaling_chip(k):
        to = {"tile": 2 * (1 - y) + lax.rem(c + k, 2)}
        return remote(
            for_chip.at[lax.rem(c + k, 2)],
            scal.at[pl.ds(pl.multiple_of(slab * block, block), block), mine],
            p_send.at[k], p_recv.at[k], to,
        )

    def far_rows(g):
        return far.at[pl.ds(pl.multiple_of(g * part, part), part), :]

    def scal_rows(g):
        return scal.at[pl.ds(pl.multiple_of(g * block, block), block), other]

    def range_chip():
        return remote(for_range, far_rows(slab), p_send.at[2], p_recv.at[2], across)

    def along(d, z, k):
        to = {"az": lax.rem(az + d, n_az)}
        at = (scal_rows, far_rows)[k](strip * n_az + z)
        return remote(at, at, az_send.at[d, k], az_recv.at[z, k], to)

    def sideways(z, k):
        at = (scal_rows, far_rows)[k](strip * n_az + z)
        return remote(at, at, x_send.at[z, k], x_recv.at[z, k], {"strip": 1 - strip})

    def order(n):
        return jnp.where(az + n < n_az, az + n, n_az - 1 - n)

    def place(n):
        s = jnp.where(n < n_az, y, 1 - y)
        z = order(lax.rem(n, n_az))
        base = (s * n_az + z) * block
        row = (2 * s + c) * m + y * half + z * block
        return pl.ds(pl.multiple_of(base, block), block), pl.ds(pl.multiple_of(row, block), block), base

    def back(n, k):
        to = lax.rem(t + k, tiles)
        src, dst, _ = place(n)
        at = pl.ds(pl.multiple_of(to * width, LANES), width)
        return remote(
            dop.at[:, src, at], ret.at[:, dst, :], w_send.at[n, k - 1], w_recv.at[n, k - 1], {"tile": to}
        )

    def keep(n):
        src, dst, _ = place(n)
        return pltpu.make_async_copy(dop.at[:, src, mine], ret.at[:, dst, :], w_local.at[n])

    def back_span(j, n, k):
        to = lax.rem(t + k, tiles)
        src, dst, _ = place(n)
        return remote(
            dop.at[:, src, lanes(to * spans + j)], ret.at[:, dst, lanes(j)],
            v_send.at[j, n - whole, k - 1], v_recv.at[j, n - whole, k - 1], {"tile": to},
        )

    def keep_span(j, n):
        src, dst, _ = place(n)
        return pltpu.make_async_copy(
            dop.at[:, src, lanes(t * spans + j)], ret.at[:, dst, lanes(j)], v_local.at[j, n - whole]
        )

    def put(j):
        slot = lax.rem(j, 2)
        return pltpu.make_async_copy(head.at[slot], o_ref.at[:, :, lanes(j)], out_sem.at[slot])

    get_front = pltpu.make_async_copy(front_ref.at[y], front, load_front)

    @pl.loop(0, spans)
    def _(j):
        own_phase(scaling_ref, j, 0).start()

    @pl.loop(0, n_one)
    def _(a):
        own_range(a).start()

    @pl.loop(0, n_one)
    def _(a):
        own_echo(a).start()

    get_front.start()
    barrier = greet(
        [{"tile": lax.rem(t + k, tiles)} for k in range(1, tiles)]
        + [{"az": lax.rem(az + k, n_az)} for k in range(1, n_az)]
        + [{"strip": 1 - strip}]
    )
    pl.semaphore_wait(barrier, tiles + n_az - 1)

    @pl.when(az < n_az - 1)
    def _():
        @pl.loop(0, n_one)
        def _(a):
            onward(a).start()

    @pl.when(az == 0)
    def _():
        @pl.loop(0, n_one)
        def _(a):
            prev[a] = jnp.zeros((2, rows_own, LANES), F32)

    @pl.loop(0, spans)
    def _(j):
        own_phase(scaling_ref, j, 0).wait()
        for k in (0, 1):
            first = (2 * strip + k) * m + 2 * az * block + 1 - y
            for_chip[k, :, lanes(j)] = phase[j, pl.ds(first, block, stride=2), :]

    for k in (0, 1):
        scaling_chip(k).start()

    @pl.loop(0, n_one)
    def _(g):
        own_range(g).wait()
        for_range[:, lanes(g)] = turn[g, pl.ds(2 * part * slab + 1 - y, part, stride=2), :]

    range_chip().start()

    @pl.loop(0, spans)
    def _(j):
        for h in (0, 1):
            rows = pl.ds(h * half, half)
            for_core[rows, lanes(j)] = phase[j, pl.ds((2 * h + 1 - c) * m + y, half, stride=2), :]
            scal[rows, lanes(t * spans + j)] = phase[j, pl.ds((2 * h + c) * m + y, half, stride=2), :]

    scaling_core().start()
    turn_rows(lambda g: turn[g, pl.ds(y, half, stride=2), :], mid, turn, y * half)

    @pl.loop(0, spans)
    def _(j):
        own_phase(azimuth_ref, j, 1).start()

    for k in range(6):
        twist_ref[k] = jnp.broadcast_to(twists_ref[:, k : k + 1], (m, LANES))
    for k in (0, 1):
        x = twists_ref[pl.ds(0, half), 6 + k : 7 + k]
        for i in range(1, tiles):
            x = jnp.where(t == i, twists_ref[pl.ds(0, half), 6 + 2 * i + k : 7 + 2 * i + k], x)
        turn_front[k] = jnp.broadcast_to(x, (half, LANES))
    get_front.wait()
    odd = lax.rem(lax.broadcasted_iota(jnp.int32, (1, pulses), 1), 2) * c
    for k in (0, 1):
        front[k] = (front[k].astype(F32) * (1 - 2 * odd).astype(F32)).astype(BF16)
    sign = (1 - 2 * y).astype(F32)

    @pl.loop(0, chunks + 3)
    def _(j):
        @pl.when(j < chunks)
        def _():
            for i in range(chunk):
                at = j * chunk + i
                own_echo(at).wait()

                @pl.when(az > 0)
                def _():
                    onward(at).wait_recv()

                for k in (0, 1):
                    a = cols[at, k, pulse_rows(t), :]
                    b = prev[at, k] * sign
                    cols[at, k, pulse_rows(t), :] = a + b
                    prev[at, k] = a - b
            echo_across(j).start()
            echo_core(j).start()

        @pl.when(j == 4)
        def _():
            for k in (0, 1):
                scaling_chip(k).wait_recv()
            range_chip().wait_recv()
            for k in (0, 1):
                sideways(az, k).start()
                for d in range(n_az - 1, 0, -1):
                    along(d, az, k).start()

        for d in range(1, n_az):
            @pl.when((j == chunks - n_az + d - 1) & (az + d < n_az))
            def _():
                for k in (0, 1):
                    along(n_az - d, az + d, k).wait_recv()
                    sideways(az + d, k).start()

        @pl.when((j >= 2) & (j < chunks + 2))
        def _():
            echo_across(j - 2).wait_recv()
            echo_forward(j - 2).start()

        @pl.when(j >= 3)
        def _():
            now = j - 3
            echo_core(now).wait_recv()
            echo_forward(now).wait_recv()
            r = []
            for e in (0, 1):
                rows = pl.ds(e, pulses // 2, stride=2)
                s = jnp.concatenate(
                    [
                        jnp.concatenate([cols[now * chunk + i, k, rows, :] for k in (0, 1)], axis=0)
                        for i in range(chunk)
                    ],
                    axis=1,
                )
                s_hi, s_lo = split(s)
                hi, lo = front[0], front[1]
                x = mm(hi, s_hi) + mm(hi, s_lo) + mm(lo, s_hi)
                r.append((x[:half], x[half:]))
            w = tuple(jnp.concatenate([turn_front[k]] * chunk, axis=1) for k in (0, 1))
            r[1] = times(r[1], w)
            for k in (0, 1):
                a, b = r[0][k], r[1][k]
                at = pl.ds(pl.multiple_of(now * chunk * LANES, LANES), chunk * LANES)
                dop[k, pl.ds(0, half), at] = a + b
                dop[k, pl.ds(half, half), at] = a - b

    scaling_core().wait_recv()

    @pl.loop(0, blocks)
    def _(n):
        @pl.when(n < n_az)
        def _():
            z = order(n)

            @pl.when(az + n >= n_az)
            def _():
                for k in (0, 1):
                    along(n_az - 1, z, k).wait_recv()
                    sideways(z, k).start()

            for k in (0, 1):
                sideways(z, k).wait_recv()

        @pl.when(n == n_az)
        def _():
            turn_rows(lambda g: far[:, lanes(g)], mid, turn, (1 - y) * half)

        filter_block(
            dop, place(n)[2], block, scal, fwd_ref, inv_ref, range_twist_ref, turn, hi_ref, lo_ref, mid
        )

        @pl.when(n < whole)
        def _():
            for k in range(tiles - 1, 0, -1):
                back(n, k).start()
            keep(n).start()

    @pl.loop(0, spans)
    def _(j):
        for n in range(whole, blocks):
            for k in range(tiles - 1, 0, -1):
                back_span(j, n, k).start()
            keep_span(j, n).start()

    @pl.loop(0, spans)
    def _(j):
        own_phase(azimuth_ref, j, 1).wait()

    for n in range(whole):
        for k in range(1, tiles):
            back(n, k).wait_recv()
        keep(n).wait()

    @pl.loop(0, spans)
    def _(j):
        for n in range(whole, blocks):
            for k in range(1, tiles):
                back_span(j, n, k).wait_recv()
            keep_span(j, n).wait()
        hi, lo = table_ref[0], table_ref[1]
        slot = lax.rem(j, 2)

        @pl.when(j > 1)
        def _():
            put(j - 2).wait()

        v = []
        for f in range(4):
            rows = pl.ds(f * m, m)
            angle = jnp.concatenate(
                [phase[j, pl.ds(f * m + p, half, stride=2), :] for p in (0, 1)], axis=0
            )
            v.append(times((ret[0, rows, lanes(j)], ret[1, rows, lanes(j)]), sincos(angle)))
        for e, x in enumerate(four(v, 1)):
            if e:
                x = times(x, (twist_ref[2 * e - 2], twist_ref[2 * e - 1]))
            s_hi, s_lo = split(jnp.concatenate(x, axis=0))
            r = mm(hi, s_hi) + mm(hi, s_lo) + mm(lo, s_hi)
            for k in (0, 1):
                head[slot, k, pl.ds(e, q, stride=4), :] = r[k * q : (k + 1) * q]
        put(j).start()

    for j in range(max(0, spans - 2), spans):
        put(j).wait()

    @pl.when(az < n_az - 1)
    def _():
        @pl.loop(0, n_one)
        def _(a):
            onward(a).wait_send()

    @pl.loop(0, chunks)
    def _(j):
        echo_across(j).wait_send()
        echo_core(j).wait_send()
        echo_forward(j).wait_send()

    scaling_core().wait_send()
    range_chip().wait_send()
    for k in (0, 1):
        scaling_chip(k).wait_send()
        for d in range(1, n_az):
            along(d, az, k).wait_send()
        for z in range(n_az):
            sideways(z, k).wait_send()
    for n in range(whole):
        for k in range(1, tiles):
            back(n, k).wait_send()

    @pl.loop(0, spans)
    def _(j):
        for n in range(whole, blocks):
            for k in range(1, tiles):
                back_span(j, n, k).wait_send()


def pair_body(raw_echo, phase_scaling, phase_range, phase_azimuth):
    tiles = lax.axis_size("tile")
    n_az, n_strip = lax.axis_size("az"), lax.axis_size("strip")
    pulses = raw_echo.shape[1] * tiles
    extent, width = phase_scaling.shape
    count, ranges = phase_range.shape
    m, q, half = extent // 4, pulses // 4, count // 2
    n_one, spans = ranges // LANES, width // LANES
    blocks = n_strip * n_az
    block = count // blocks
    chunk = 2
    chunks = n_one // chunk
    whole = blocks // 2 + 1
    rest = blocks - whole
    fine = np.concatenate([np.arange(0, m, 2), np.arange(1, m, 2)])
    lane = np.arange(LANES)
    vmem = pl.BlockSpec(memory_space=pltpu.VMEM)
    anyspace = pl.BlockSpec(memory_space=pl.ANY)
    dma = pltpu.SemaphoreType.DMA
    c, s = roots(np.arange(n_one), lane, ranges, -1)
    return pl.pallas_call(
        functools.partial(pair_kernel, n_strip, n_az, block, chunk),
        out_shape=jax.ShapeDtypeStruct((2, pulses, width), F32),
        in_specs=[anyspace] * 5 + [vmem] * 5,
        out_specs=anyspace,
        scratch_shapes=[
            pltpu.VMEM((n_one, 2, pulses, LANES), F32),
            pltpu.VMEM((n_one, 2, pulses // tiles, LANES), F32),
            pltpu.VMEM((2, count, ranges), F32),
            pltpu.VMEM((count, ranges), F32),
            pltpu.VMEM((half, ranges), F32),
            pltpu.VMEM((n_one, count, LANES), F32),
            pltpu.VMEM((spans, extent, LANES), F32),
            pltpu.VMEM((2, extent, width), F32),
            pltpu.VMEM((count, width), F32),
            pltpu.VMEM((2, block, width), F32),
            pltpu.VMEM((half // blocks, ranges), F32),
            pltpu.VMEM((2, count, pulses), BF16),
            pltpu.VMEM((2, half, LANES), F32),
            pltpu.VMEM((6, m, LANES), F32),
            pltpu.VMEM((2, 2, pulses, LANES), F32),
            pltpu.VMEM((n_one, block, 2 * LANES), BF16),
            pltpu.VMEM((n_one, block, 2 * LANES), BF16),
            pltpu.VMEM((2, n_one * LANES // 2, LANES), F32),
            dma((2, spans)), dma((n_one,)), dma((n_one,)), dma,
            dma((n_one,)), dma((n_one,)),
            dma((chunks,)), dma((chunks,)),
            dma((chunks,)), dma((chunks,)),
            dma((chunks,)), dma((chunks,)),
            dma, dma,
            dma((3,)), dma((3,)),
            dma((n_az, 2)), dma((n_az, 2)),
            dma((n_az, 2)), dma((n_az, 2)),
            dma((whole, tiles - 1)), dma((whole, tiles - 1)), dma((whole,)),
            dma((spans, rest, tiles - 1)), dma((spans, rest, tiles - 1)), dma((spans, rest)),
            dma((2,)),
        ],
        compiler_params=pltpu.CompilerParams(
            collective_id=0, has_side_effects=True, vmem_limit_bytes=63 << 20
        ),
    )(
        raw_echo,
        phase_scaling,
        phase_range,
        phase_azimuth,
        pair_front(extent, pulses),
        pair_twists(extent, fine),
        right_table(lane, lane, LANES, -1),
        right_table(lane, lane, LANES, 1, 1.0 / ranges),
        np.stack([c, s]).astype(np.float32),
        left_table(np.arange(q), fine, m, 1, 1.0 / extent),
    )


def paired(raw_echo, phase_scaling, phase_range):
    tiles, n_az, n_strip = (lax.axis_size(a) for a in ("tile", "az", "strip"))
    count = phase_range.shape[0]
    blocks = n_az * n_strip
    return (
        tiles == 4
        and n_strip == 2
        and n_az > 1
        and count == 2 * LANES
        and phase_scaling.shape[0] == 2 * raw_echo.shape[1] * tiles
        and count % (16 * blocks) == 0
        and phase_range.shape[1] % (2 * LANES) == 0
    )


def body(raw_echo, phase_scaling, phase_range, phase_azimuth):
    plan = pair_body if paired(raw_echo, phase_scaling, phase_range) else tail_body
    return plan(raw_echo, phase_scaling, phase_range, phase_azimuth)


def solution(mesh):
    return jax.shard_map(
        body,
        mesh=mesh,
        in_specs=(
            P(None, ("strip", "az", "tile"), None),
            P(None, "tile"),
            P("tile", None),
            P(None, "tile"),
        ),
        out_specs=P(None, ("strip", "az"), "tile"),
        check_vma=False,
    )
```

```python
import functools
import math

import jax
import jax.numpy as jnp
import numpy as np
from jax import lax
from jax.experimental import pallas as pl
from jax.experimental.pallas import tpu as pltpu
from jax.sharding import PartitionSpec as P

F32 = jnp.float32
BF16 = jnp.bfloat16
LANES = 128


def halves(table):
    hi = np.asarray(table, np.float32).astype(jnp.bfloat16)
    lo = (np.asarray(table, np.float64) - hi.astype(np.float64)).astype(jnp.bfloat16)
    return np.stack([hi, lo])


def roots(rows, cols, modulus, direction):
    residue = np.outer(rows, cols) % modulus
    angle = residue * (direction * 2.0 * math.pi / modulus)
    return np.cos(angle), np.sin(angle)


def left_table(rows, cols, modulus, direction, scale=1.0):
    c, s = roots(rows, cols, modulus, direction)
    return halves(np.block([[c, -s], [s, c]]) * scale)


def right_table(rows, cols, modulus, direction, scale=1.0):
    c, s = roots(rows, cols, modulus, direction)
    return halves(np.block([[c, s], [-s, c]]) * scale)


def twist_table(count, length, modulus, direction):
    c, s = roots(np.arange(count), np.arange(length), modulus, direction)
    full = np.stack([c, s]).astype(np.float32)
    return np.ascontiguousarray(np.broadcast_to(full[..., None], full.shape + (LANES,)))


def split(x):
    hi = x.astype(BF16)
    return hi, (x - hi.astype(F32)).astype(BF16)


def mm(a, b):
    return jnp.dot(a, b, preferred_element_type=F32)


def times(a, t):
    return a[0] * t[0] - a[1] * t[1], a[0] * t[1] + a[1] * t[0]


def plus(a, b):
    return a[0] + b[0], a[1] + b[1]


def minus(a, b):
    return a[0] - b[0], a[1] - b[1]


def quarter(a, direction):
    return (-a[1], a[0]) if direction > 0 else (a[1], -a[0])


def four(v, direction):
    a, b = plus(v[0], v[2]), minus(v[0], v[2])
    c, d = plus(v[1], v[3]), quarter(minus(v[1], v[3]), direction)
    return [plus(a, c), plus(b, d), minus(a, c), minus(b, d)]


def fft(v, direction):
    n = len(v)
    if n == 1:
        return v
    if n == 2:
        return [plus(v[0], v[1]), minus(v[0], v[1])]
    if n == 4:
        return four(v, direction)
    parts = [fft(v[e::4], direction) for e in range(4)] if n % 4 == 0 else None
    out = [None] * n
    m = n // 4
    for f in range(m):
        items = []
        for e in range(4):
            x = parts[e][f]
            k = e * f % n
            if k == 0:
                pass
            elif 8 * k == n:
                h = np.float32(math.sqrt(0.5))
                q = quarter(x, direction)
                x = ((x[0] + q[0]) * h, (x[1] + q[1]) * h)
            elif 4 * k == n:
                x = quarter(x, direction)
            elif 8 * k == 3 * n:
                h = np.float32(math.sqrt(0.5))
                q = quarter(x, direction)
                x = ((q[0] - x[0]) * h, (q[1] - x[1]) * h)
            else:
                ang = direction * 2.0 * math.pi * k / n
                x = times(x, (np.float32(math.cos(ang)), np.float32(math.sin(ang))))
            items.append(x)
        got = four(items, direction)
        for j in range(4):
            out[f + j * m] = got[j]
    return out


def sincos(x):
    y = x * 0.5
    z = y * y
    s, c = -1.0 / 39916800, 1.0 / 479001600
    for a, b in ((362880, -3628800), (-5040, 40320), (120, -720), (-6, 24), (1, -2)):
        s = s * z + np.float32(1.0 / a)
        c = c * z + np.float32(1.0 / b)
    s = s * y
    c = c * z + 1.0
    return 1.0 - 2.0 * s * s, 2.0 * s * c


def greet(partners):
    barrier = pltpu.get_barrier_semaphore()
    for device in partners:
        pl.semaphore_signal(barrier, inc=1, device_id=device, device_id_type=pl.DeviceIdType.MESH)
    return barrier


def lanes(j):
    return pl.ds(pl.multiple_of(j * LANES, LANES), LANES)


def filter_rows(x_ref, base, block, fwd_ref, inv_ref, twist_ref, phase_ref, hi_ref, lo_ref, mid_ref):
    n_one = phase_ref.shape[0]
    step = 16
    f_hi, f_lo = fwd_ref[0], fwd_ref[1]
    b_hi, b_lo = inv_ref[0], inv_ref[1]

    @pl.loop(0, block // step)
    def _(i):
        rows = pl.ds(pl.multiple_of(i * step, step), step)
        at = pl.ds(pl.multiple_of(base + i * step, step), step)
        v = [
            tuple(x_ref[c, at, pl.ds(a * LANES, LANES)] for c in (0, 1))
            for a in range(n_one)
        ]
        for k, x in enumerate(fft(v, -1)):
            if k:
                x = times(x, (twist_ref[0, k : k + 1, :], twist_ref[1, k : k + 1, :]))
            for c in (0, 1):
                h, l = split(x[c])
                hi_ref[k, rows, pl.ds(c * LANES, LANES)] = h
                lo_ref[k, rows, pl.ds(c * LANES, LANES)] = l

    group = 4

    @pl.loop(0, n_one // group)
    def _(i):
        ks = pl.ds(i * group, group)
        flat = (group * block, 2 * LANES)
        h, l = hi_ref[ks].reshape(flat), lo_ref[ks].reshape(flat)
        r = mm(h, f_hi) + mm(l, f_hi) + mm(h, f_lo)
        turn = phase_ref[ks, pl.ds(pl.multiple_of(base, block), block), :]
        r = times((r[:, :LANES], r[:, LANES:]), sincos(turn.reshape(group * block, LANES)))
        h, l = split(jnp.concatenate(r, axis=1))
        r = mm(h, b_hi) + mm(l, b_hi) + mm(h, b_lo)
        at = pl.ds(pl.multiple_of(i * group * block, block), group * block)
        mid_ref[0, at, :] = r[:, :LANES]
        mid_ref[1, at, :] = r[:, LANES:]

    @pl.loop(0, block // 8)
    def _(i):
        at = pl.ds(pl.multiple_of(base + i * 8, 8), 8)
        v = []
        for k in range(n_one):
            x = tuple(mid_ref[c, pl.ds(pl.multiple_of(k * block + i * 8, 8), 8), :] for c in (0, 1))
            if k:
                x = times(x, (twist_ref[0, k : k + 1, :], -twist_ref[1, k : k + 1, :]))
            v.append(x)
        for a, x in enumerate(fft(v, 1)):
            for c in (0, 1):
                x_ref[c, at, pl.ds(a * LANES, LANES)] = x[c]


def permute_turn(o_ref, mid, turn):
    n_one, count, _ = turn.shape
    half = mid.shape[1]
    some = min(count, LANES)
    part = half // n_one

    @pl.loop(0, count // some)
    def _(i):
        @pl.loop(0, n_one)
        def _(g):
            c, row, j = piece(g, count, o_ref)
            at = pl.ds(pl.multiple_of(row + i * some, some), some)
            x = o_ref[c, at, lanes(j)]
            if some < LANES:
                x = jnp.concatenate([x] * (LANES // some), axis=0)
            per = half // LANES
            mid[g // per, pl.ds(pl.multiple_of(g % per * LANES, LANES), LANES), :] = x.T

        @pl.loop(0, n_one)
        def _(k):
            rows = pl.ds(k, part, stride=n_one)
            x = jnp.concatenate([mid[h, rows, :] for h in range(LANES // part)], axis=0)
            at = pl.ds(pl.multiple_of(i * some, some), some)
            turn[k, at, :] = x.T[:some]


def piece(g, count, o_ref):
    across = o_ref.shape[2] // LANES
    down = o_ref.shape[1] // count
    return g // (across * down), g // across % down * count, g % across


def focus_kernel(
    tiles, length, block,
    raw_ref, scaling_ref, range_ref, azimuth_ref,
    front_ref, twist_ref, fwd_ref, inv_ref, range_twist_ref, table_ref,
    o_ref,
    spec, scaling, turn, phase, dop, ret, tail_out, tail_in, head, hi_ref, lo_ref, mid,
    send_e, recv_e, local_e, send_a, recv_a, local_a, send_b, recv_b, local_b,
    send_c, recv_c, load, load_range,
):
    me = lax.axis_index("tile")
    az = lax.axis_index("az")
    count = dop.shape[1]
    width = o_ref.shape[2]
    pulses = o_ref.shape[1]
    tail = tail_in.shape[2]
    rows_own = raw_ref.shape[1]
    n_one = turn.shape[0]
    blocks = count // block
    early = (blocks - 1) * block
    spans = width // LANES
    cols = tail_out
    m = spec.shape[1] // 4
    q = pulses // 4
    mine = pl.ds(pl.multiple_of(me * width, LANES), width)
    own = pl.ds(pl.multiple_of(me * count, count), count)
    own_pulses = pl.ds(pl.multiple_of(me * rows_own, rows_own), rows_own)

    def remote(src, dst, send, recv, device):
        return pltpu.make_async_remote_copy(
            src_ref=src, dst_ref=dst, send_sem=send, recv_sem=recv,
            device_id=device, device_id_type=pl.DeviceIdType.MESH,
        )

    def echo(j, k):
        to = lax.rem(me + k, tiles)
        return remote(
            raw_ref.at[:, :, lanes(to * spans + j)], cols.at[j, :, own_pulses, :],
            send_e.at[j, k - 1], recv_e.at[j, k - 1], {"tile": to},
        )

    def keep_echo(j):
        return pltpu.make_async_copy(
            raw_ref.at[:, :, lanes(me * spans + j)], cols.at[j, :, own_pulses, :], local_e.at[j]
        )

    def load_piece(g):
        c, row, j = piece(g, count, o_ref)
        return pltpu.make_async_copy(
            range_ref.at[:, lanes(g)],
            o_ref.at[c, pl.ds(pl.multiple_of(row, count), count), lanes(j)],
            load_range.at[g],
        )

    def out_part(i, k, lo, n, slot):
        to = lax.rem(me + k, tiles)
        at = pl.ds(pl.multiple_of(me * width + lo, LANES), n)
        return remote(
            spec.at[:, pl.ds(pl.multiple_of(to * count + i * block, block), block), pl.ds(lo, n)],
            dop.at[:, pl.ds(pl.multiple_of(i * block, block), block), at],
            send_a.at[slot, k - 1], recv_a.at[slot, k - 1], {"tile": to},
        )

    def out(i, k):
        return out_part(i, k, 0, width, i)

    def first_out(k):
        return out_part(0, k, 0, width - LANES, blocks)

    def last_out(k):
        return out_part(0, k, width - LANES, LANES, 0)

    def back_rows(j, k, lo, n, slot):
        to = lax.rem(me + k, tiles)
        return remote(
            dop.at[:, pl.ds(lo, n), lanes(to * spans + j)],
            ret.at[j, :, pl.ds(pl.multiple_of(me * count + lo, 8), n), :],
            send_b.at[slot, k - 1], recv_b.at[slot, k - 1], {"tile": to},
        )

    def first_rows(k):
        return back_rows(0, k, 0, early, spans)

    def last_rows(k):
        return back_rows(0, k, early, count - early, 0)

    def back(j, k):
        return back_rows(j, k, 0, count, j)

    def keep(j):
        return pltpu.make_async_copy(
            dop.at[:, :, lanes(me * spans + j)], ret.at[j, :, own, :], local_b.at[j]
        )

    def onward(j):
        return remote(
            tail_out.at[j, :, pl.ds(0, tail), :], tail_in.at[j], send_c.at[j], recv_c.at[j],
            {"az": lax.rem(az + 1, length)},
        )

    barrier = greet(
        [{"tile": lax.rem(me + k, tiles)} for k in range(1, tiles)]
        + [{"az": lax.rem(az + 1, length)}, {"az": lax.rem(az + length - 1, length)}]
    )
    get_scaling = pltpu.make_async_copy(scaling_ref, scaling, load.at[0])
    get_phase = pltpu.make_async_copy(azimuth_ref, phase, load.at[1])
    pl.semaphore_wait(barrier, tiles + 1)

    @pl.loop(0, spans)
    def _(j):
        for k in range(1, tiles):
            echo(j, k).start()
        keep_echo(j).start()

    @pl.loop(0, n_one)
    def _(g):
        load_piece(g).start()

    get_scaling.start()
    get_phase.start()

    get_scaling.wait()

    @pl.loop(0, spans)
    def _(j):
        @pl.when(j == spans - 1)
        def _():
            for k in range(1, tiles):
                first_out(k).start()

        for k in range(1, tiles):
            echo(j, k).wait_recv()
        keep_echo(j).wait()
        hi, lo = front_ref[0], front_ref[1]
        z = []
        for e in range(4):
            rows = pl.ds(e, q, stride=4)
            s = jnp.concatenate([cols[j, 0, rows, :], cols[j, 1, rows, :]], axis=0)
            s_hi, s_lo = split(s)
            r = mm(hi, s_hi) + mm(hi, s_lo) + mm(lo, s_hi)
            r = (r[:m], r[m:])
            if e:
                r = times(r, (twist_ref[0, e], -twist_ref[1, e]))
            z.append(r)
        for f, x in enumerate(four(z, -1)):
            rows = pl.ds(f * m, m)
            x = times(x, sincos(scaling[rows, lanes(j)]))
            spec[0, rows, lanes(j)] = x[0]
            spec[1, rows, lanes(j)] = x[1]

    for k in range(1, tiles):
        last_out(k).start()

    @pl.loop(1, blocks)
    def _(i):
        for k in range(1, tiles):
            out(i, k).start()

    first = pltpu.make_async_copy(spec.at[:, own, :], dop.at[:, :, mine], local_a)
    first.start()

    @pl.loop(0, n_one)
    def _(g):
        load_piece(g).wait()

    permute_turn(o_ref, mid, turn)
    first.wait()

    @pl.loop(0, blocks)
    def _(i):
        if early:
            @pl.when(i == blocks - 1)
            def _():
                for k in range(1, tiles):
                    first_rows(k).start()

        @pl.when(i == 0)
        def _():
            for k in range(1, tiles):
                first_out(k).wait_recv()
                last_out(k).wait_recv()

        @pl.when(i > 0)
        def _():
            for k in range(1, tiles):
                out(i, k).wait_recv()

        filter_rows(
            dop, i * block, block, fwd_ref, inv_ref, range_twist_ref, turn,
            hi_ref, lo_ref, mid,
        )

    for k in range(1, tiles):
        last_rows(k).start()
    keep(0).start()

    @pl.loop(1, spans)
    def _(j):
        for k in range(1, tiles):
            back(j, k).start()
        keep(j).start()

    get_phase.wait()

    @pl.loop(0, spans)
    def _(j):
        @pl.when(j == 0)
        def _():
            for k in range(1, tiles):
                if early:
                    first_rows(k).wait_recv()
                last_rows(k).wait_recv()

        @pl.when(j > 0)
        def _():
            for k in range(1, tiles):
                back(j, k).wait_recv()

        keep(j).wait()
        hi, lo = table_ref[0], table_ref[1]
        v = []
        for f in range(4):
            rows = pl.ds(f * m, m)
            v.append(times((ret[j, 0, rows, :], ret[j, 1, rows, :]), sincos(phase[rows, lanes(j)])))
        for e, x in enumerate(four(v, 1)):
            if e:
                x = times(x, (twist_ref[0, e], twist_ref[1, e]))
            s_hi, s_lo = split(jnp.concatenate(x, axis=0))
            r = mm(hi, s_hi) + mm(hi, s_lo) + mm(lo, s_hi)
            for c in (0, 1):
                head[c, pl.ds(e, q, stride=4), :] = r[c * m : c * m + q]
                tail_out[j, c, pl.ds(e, m - q, stride=4), :] = r[c * m + q : (c + 1) * m]

        @pl.when(az < length - 1)
        def _():
            onward(j).start()

        o_ref[:, :, lanes(j)] = head[...]

    @pl.when(az > 0)
    def _():
        @pl.loop(0, spans)
        def _(j):
            onward(j).wait_recv()
            o_ref[:, pl.ds(0, tail), lanes(j)] += tail_in[j]

    for k in range(1, tiles):
        first_out(k).wait_send()
        last_out(k).wait_send()

    @pl.loop(1, blocks)
    def _(i):
        for k in range(1, tiles):
            out(i, k).wait_send()

    for k in range(1, tiles):
        if early:
            first_rows(k).wait_send()
        last_rows(k).wait_send()

    @pl.loop(1, spans)
    def _(j):
        for k in range(1, tiles):
            back(j, k).wait_send()

    @pl.loop(0, spans)
    def _(j):
        for k in range(1, tiles):
            echo(j, k).wait_send()

    @pl.when(az < length - 1)
    def _():
        @pl.loop(0, spans)
        def _(j):
            onward(j).wait_send()


def tail_body(raw_echo, phase_scaling, phase_range, phase_azimuth):
    tiles = lax.axis_size("tile")
    length = lax.axis_size("az")
    pulses = raw_echo.shape[1] * tiles
    extent, width = phase_scaling.shape
    count, ranges = phase_range.shape
    m, q, tail = extent // 4, pulses // 4, extent - pulses
    n_one, spans = ranges // LANES, width // LANES
    block = min(64, count)
    rows, lane = np.arange(m), np.arange(LANES)
    vmem = pl.BlockSpec(memory_space=pltpu.VMEM)
    anyspace = pl.BlockSpec(memory_space=pl.ANY)
    dma = pltpu.SemaphoreType.DMA
    c, s = roots(np.arange(n_one), lane, ranges, -1)
    return pl.pallas_call(
        functools.partial(focus_kernel, tiles, length, block),
        out_shape=jax.ShapeDtypeStruct((2, pulses, width), F32),
        in_specs=[anyspace] * 4 + [vmem] * 6,
        out_specs=vmem,
        scratch_shapes=[
            pltpu.VMEM((2, extent, width), F32),
            pltpu.VMEM((extent, width), F32),
            pltpu.VMEM((n_one, count, LANES), F32),
            pltpu.VMEM((extent, width), F32),
            pltpu.VMEM((2, count, ranges), F32),
            pltpu.VMEM((spans, 2, extent, LANES), F32),
            pltpu.VMEM((spans, 2, max(tail, pulses), LANES), F32),
            pltpu.VMEM((spans, 2, tail, LANES), F32),
            pltpu.VMEM((2, pulses, LANES), F32),
            pltpu.VMEM((n_one, block, 2 * LANES), BF16),
            pltpu.VMEM((n_one, block, 2 * LANES), BF16),
            pltpu.VMEM((2, n_one * block, LANES), F32),
            dma((spans, tiles - 1)),
            dma((spans, tiles - 1)),
            dma((spans,)),
            dma((count // block + 1, tiles - 1)),
            dma((count // block + 1, tiles - 1)),
            dma,
            dma((spans + 1, tiles - 1)),
            dma((spans + 1, tiles - 1)),
            dma((spans,)),
            dma((spans,)),
            dma((spans,)),
            dma((2,)),
            dma((n_one,)),
        ],
        compiler_params=pltpu.CompilerParams(
            collective_id=0, has_side_effects=True, vmem_limit_bytes=63 << 20
        ),
    )(
        raw_echo,
        phase_scaling,
        phase_range,
        phase_azimuth,
        left_table(rows, np.arange(q), m, -1),
        twist_table(4, m, extent, 1),
        right_table(lane, lane, LANES, -1),
        right_table(lane, lane, LANES, 1, 1.0 / ranges),
        np.stack([c, s]).astype(np.float32),
        left_table(rows, rows, m, 1, 1.0 / extent),
    )


def pair_front(extent, pulses):
    m = extent // 4
    return np.stack(
        [left_table(2 * np.arange(m // 2) + y, 2 * np.arange(pulses // 2), extent, -1) for y in (0, 1)]
    )


def pair_twists(extent, fine):
    m = extent // 4
    out = np.zeros((m, LANES), np.float32)
    for e in range(1, 4):
        c, s = roots(fine, [e], extent, 1)
        out[:, 2 * e - 2 : 2 * e - 1], out[:, 2 * e - 1 : 2 * e] = c, s
    for t in range(4):
        c, s = roots(2 * np.arange(m // 2) + t // 2 + m * (t % 2), [1], extent, -1)
        out[: m // 2, 6 + 2 * t : 7 + 2 * t], out[: m // 2, 7 + 2 * t : 8 + 2 * t] = c, s
    return out


def filter_block(
    x_ref, base, block, scal_ref, fwd_ref, inv_ref, twist_ref, phase_ref, hi_ref, lo_ref, mid_ref
):
    n_one = phase_ref.shape[0]
    step = 16
    group = max(1, 256 // block)
    f_hi, f_lo = fwd_ref[0], fwd_ref[1]
    b_hi, b_lo = inv_ref[0], inv_ref[1]
    whole = pl.ds(pl.multiple_of(base, block), block)

    @pl.loop(0, n_one)
    def _(a):
        x = times((x_ref[0, whole, lanes(a)], x_ref[1, whole, lanes(a)]), sincos(scal_ref[whole, lanes(a)]))
        x_ref[0, whole, lanes(a)] = x[0]
        x_ref[1, whole, lanes(a)] = x[1]

    @pl.loop(0, block // step)
    def _(i):
        rows = pl.ds(pl.multiple_of(i * step, step), step)
        at = pl.ds(pl.multiple_of(base + i * step, step), step)
        v = [
            tuple(x_ref[c, at, pl.ds(a * LANES, LANES)] for c in (0, 1))
            for a in range(n_one)
        ]
        for k, x in enumerate(fft(v, -1)):
            if k:
                x = times(x, (twist_ref[0, k : k + 1, :], twist_ref[1, k : k + 1, :]))
            for c in (0, 1):
                h, l = split(x[c])
                hi_ref[k, rows, pl.ds(c * LANES, LANES)] = h
                lo_ref[k, rows, pl.ds(c * LANES, LANES)] = l

    @pl.loop(0, n_one // group)
    def _(i):
        ks = pl.ds(i * group, group)
        flat = (group * block, 2 * LANES)
        h, l = hi_ref[ks].reshape(flat), lo_ref[ks].reshape(flat)
        r = mm(h, f_hi) + mm(l, f_hi) + mm(h, f_lo)
        turn = phase_ref[ks, whole, :]
        r = times((r[:, :LANES], r[:, LANES:]), sincos(turn.reshape(group * block, LANES)))
        h, l = split(jnp.concatenate(r, axis=1))
        r = mm(h, b_hi) + mm(l, b_hi) + mm(h, b_lo)
        at = pl.ds(pl.multiple_of(i * group * block, block), group * block)
        mid_ref[0, at, :] = r[:, :LANES]
        mid_ref[1, at, :] = r[:, LANES:]

    @pl.loop(0, block // 8)
    def _(i):
        at = pl.ds(pl.multiple_of(base + i * 8, 8), 8)
        v = []
        for k in range(n_one):
            x = tuple(mid_ref[c, pl.ds(pl.multiple_of(k * block + i * 8, 8), 8), :] for c in (0, 1))
            if k:
                x = times(x, (twist_ref[0, k : k + 1, :], -twist_ref[1, k : k + 1, :]))
            v.append(x)
        for a, x in enumerate(fft(v, 1)):
            for c in (0, 1):
                x_ref[c, at, pl.ds(a * LANES, LANES)] = x[c]


def turn_rows(load, mid, turn, base):
    n_one = turn.shape[0]
    half = n_one * LANES // 2
    part = half // n_one
    per = half // LANES
    at = pl.ds(pl.multiple_of(base, LANES), LANES)

    @pl.loop(0, n_one)
    def _(g):
        mid[g // per, pl.ds(pl.multiple_of(g % per * LANES, LANES), LANES), :] = load(g).T

    @pl.loop(0, n_one)
    def _(k):
        rows = pl.ds(k, part, stride=n_one)
        x = jnp.concatenate([mid[h, rows, :] for h in range(LANES // part)], axis=0)
        turn[k, at, :] = x.T


def pair_kernel(
    n_strip, n_az, block, chunk,
    raw_ref, scaling_ref, range_ref, azimuth_ref, front_ref,
    twists_ref, fwd_ref, inv_ref, range_twist_ref, table_ref,
    o_ref,
    cols, prev, dop, scal, swap, turn, phase, ret, for_chip,
    front, turn_front, twist_ref, head, hi_ref, lo_ref, mid,
    load, load_range, load_echo, load_front, z_send, z_recv, y_send, y_recv, c_send, c_recv, f_send, f_recv,
    s_send, s_recv, p_send, p_recv, az_send, up_send, az_recv, x_send, x_recv,
    w_send, w_recv, w_local, v_send, v_recv, v_local, out_sem,
):
    t = lax.axis_index("tile")
    az = lax.axis_index("az")
    strip = lax.axis_index("strip")
    y, c = t // 2, t % 2
    tiles = 4
    count, ranges = range_ref.shape
    half = count // 2
    extent, width = scaling_ref.shape
    m = extent // 4
    pulses = o_ref.shape[1]
    q = pulses // 4
    rows_own = raw_ref.shape[1]
    spans = width // LANES
    n_one = ranges // LANES
    chunks = n_one // chunk
    blocks = count // block
    part = half // blocks
    whole = blocks // 2 + 1
    partner, across = {"tile": 2 * y + 1 - c}, {"tile": 2 * (1 - y) + c}
    other = pl.ds(pl.multiple_of(2 * (1 - y) * width, LANES), 2 * width)
    mine = pl.ds(pl.multiple_of(t * width, LANES), width)
    slab = strip * n_az + az

    def remote(src, dst, send, recv, device):
        return pltpu.make_async_remote_copy(
            src_ref=src, dst_ref=dst, send_sem=send, recv_sem=recv,
            device_id=device, device_id_type=pl.DeviceIdType.MESH,
        )

    def pulse_rows(tile):
        return pl.ds(pl.multiple_of(tile * rows_own, rows_own), rows_own)

    def groups(j):
        return pl.ds(j * chunk, chunk)

    def onward(a):
        return remote(
            raw_ref.at[:, :, lanes(a)], prev.at[a], z_send.at[a], z_recv.at[a],
            {"az": lax.rem(az + 1, n_az)},
        )

    def own_echo(a):
        return pltpu.make_async_copy(
            raw_ref.at[:, :, lanes(a)], cols.at[a, :, pulse_rows(t), :], load_echo.at[a]
        )

    def range_piece(a, first, rows, stride=None):
        row = a % (extent // count) * count + first
        return phase.at[a // (extent // count), pl.ds(row, rows, stride=stride), :]

    def own_range(a):
        return pltpu.make_async_copy(range_ref.at[:, lanes(a)], range_piece(a, 0, count), load_range.at[a])

    def own_phase(source, j, k):
        return pltpu.make_async_copy(source.at[:, lanes(j)], phase.at[j], load.at[k, j])

    def echo_across(j):
        return remote(
            prev.at[groups(j)], cols.at[groups(j), :, pulse_rows(t), :],
            y_send.at[j], y_recv.at[j], across,
        )

    def echo_core(j):
        at = cols.at[groups(j), :, pulse_rows(t), :]
        return remote(at, at, c_send.at[j], c_recv.at[j], partner)

    def echo_forward(j):
        at = cols.at[groups(j), :, pulse_rows(2 * (1 - y) + c), :]
        return remote(at, at, f_send.at[j], f_recv.at[j], partner)

    def scaling_core():
        return remote(dop.at[0, :, pl.ds(0, width)], scal.at[:, mine], s_send, s_recv, partner)

    def scaling_chip(k):
        to = {"tile": 2 * (1 - y) + lax.rem(c + k, 2)}
        return remote(
            for_chip.at[lax.rem(c + k, 2)],
            scal.at[pl.ds(pl.multiple_of(slab * block, block), block), mine],
            p_send.at[k], p_recv.at[k], to,
        )

    def turn_part(ref, base, z, s):
        first = base + (z * n_strip + s) * part
        return ref.at[:, pl.ds(pl.multiple_of(first, part), part), :]

    def scal_rows(g):
        return scal.at[pl.ds(pl.multiple_of(g * block, block), block), other]

    def range_chip():
        return remote(
            turn_part(swap, 0, az, strip), turn_part(turn, y * half, az, strip),
            p_send.at[2], p_recv.at[2], across,
        )

    def slice_of(z, k):
        if k:
            return turn_part(turn, (1 - y) * half, z, strip)
        return scal_rows(strip * n_az + z)

    def along(d, z, k):
        to = {"az": lax.rem(az + d, n_az)}
        at = slice_of(z, k)
        return remote(at, at, az_send.at[d, k], az_recv.at[z, k], to)

    def up(i, k):
        at = slice_of(az - i, k)
        return remote(at, at, up_send.at[i, k], az_recv.at[az - i, k], {"az": lax.rem(az + 1, n_az)})

    def relay(i):
        @pl.when(az >= i)
        def _():
            for k in (0, 1):
                along(1, az - i, k).wait_recv()
                sideways(az - i, k).start()

                @pl.when(az + 1 < n_az)
                def _():
                    up(i, k).start()

    def sideways(z, k):
        at = slice_of(z, k)
        return remote(at, at, x_send.at[z, k], x_recv.at[z, k], {"strip": 1 - strip})

    def share(k):
        sideways(az, k).start()
        for d in range(n_az - 1, 0, -1):
            @pl.when(az + d >= n_az)
            def _():
                along(d, az, k).start()

    def order(n):
        return jnp.where(az + n < n_az, az + n, n_az - 1 - n)

    def place(n):
        s = jnp.where(lax.rem(n, 2) == 0, y, 1 - y)
        z = order(n // 2)
        base = (s * n_az + z) * block
        row = (2 * s + c) * m + y * half + z * block
        return pl.ds(pl.multiple_of(base, block), block), pl.ds(pl.multiple_of(row, block), block), base

    def back(n, k):
        to = lax.rem(t + k, tiles)
        src, dst, _ = place(n)
        at = pl.ds(pl.multiple_of(to * width, LANES), width)
        return remote(
            dop.at[:, src, at], ret.at[:, dst, :], w_send.at[n, k - 1], w_recv.at[n, k - 1], {"tile": to}
        )

    def keep(n):
        src, dst, _ = place(n)
        return pltpu.make_async_copy(dop.at[:, src, mine], ret.at[:, dst, :], w_local.at[n])

    def back_span(j, n, k):
        to = lax.rem(t + k, tiles)
        src, dst, _ = place(n)
        return remote(
            dop.at[:, src, lanes(to * spans + j)], ret.at[:, dst, lanes(j)],
            v_send.at[j, n - whole, k - 1], v_recv.at[j, n - whole, k - 1], {"tile": to},
        )

    def keep_span(j, n):
        src, dst, _ = place(n)
        return pltpu.make_async_copy(
            dop.at[:, src, lanes(t * spans + j)], ret.at[:, dst, lanes(j)], v_local.at[j, n - whole]
        )

    def put(j):
        slot = lax.rem(j, 2)
        return pltpu.make_async_copy(head.at[slot], o_ref.at[:, :, lanes(j)], out_sem.at[slot])

    get_front = pltpu.make_async_copy(front_ref.at[y], front, load_front)

    @pl.loop(0, spans)
    def _(j):
        own_phase(scaling_ref, j, 0).start()

    @pl.loop(0, n_one)
    def _(a):
        own_echo(a).start()

    get_front.start()
    barrier = greet(
        [{"tile": lax.rem(t + k, tiles)} for k in range(1, tiles)]
        + [{"az": lax.rem(az + k, n_az)} for k in range(1, n_az)]
        + [{"strip": 1 - strip}]
    )
    pl.semaphore_wait(barrier, tiles + n_az - 1)

    @pl.when(az < n_az - 1)
    def _():
        @pl.loop(0, n_one)
        def _(a):
            onward(a).start()

    @pl.when(az == 0)
    def _():
        @pl.loop(0, n_one)
        def _(a):
            prev[a] = jnp.zeros((2, rows_own, LANES), F32)

    @pl.loop(0, spans)
    def _(j):
        own_phase(scaling_ref, j, 0).wait()
        for k in (0, 1):
            first = (2 * strip + k) * m + 2 * az * block + 1 - y
            for_chip[k, :, lanes(j)] = phase[j, pl.ds(first, block, stride=2), :]

    for k in (0, 1):
        scaling_chip(k).start()
    @pl.loop(0, spans)
    def _(j):
        for h in (0, 1):
            rows = pl.ds(h * half, half)
            dop[0, rows, lanes(j)] = phase[j, pl.ds((2 * h + 1 - c) * m + y, half, stride=2), :]
            scal[rows, lanes(t * spans + j)] = phase[j, pl.ds((2 * h + c) * m + y, half, stride=2), :]

    scaling_core().start()

    @pl.loop(0, n_one)
    def _(a):
        own_range(a).start()

    for k in range(6):
        twist_ref[k] = jnp.broadcast_to(twists_ref[:, k : k + 1], (m, LANES))
    for k in (0, 1):
        x = twists_ref[pl.ds(0, half), 6 + k : 7 + k]
        for i in range(1, tiles):
            x = jnp.where(t == i, twists_ref[pl.ds(0, half), 6 + 2 * i + k : 7 + 2 * i + k], x)
        turn_front[k] = jnp.broadcast_to(x, (half, LANES))
    scaling_core().wait_send()
    get_front.wait()
    odd = lax.rem(lax.broadcasted_iota(jnp.int32, (1, pulses), 1), 2) * c
    for k in (0, 1):
        front[k] = (front[k].astype(F32) * (1 - 2 * odd).astype(F32)).astype(BF16)
    sign = (1 - 2 * y).astype(F32)

    @pl.loop(0, chunks + 3)
    def _(j):
        @pl.when(j < chunks)
        def _():
            for i in range(chunk):
                at = j * chunk + i
                own_echo(at).wait()

                @pl.when(az > 0)
                def _():
                    onward(at).wait_recv()

                for k in (0, 1):
                    a = cols[at, k, pulse_rows(t), :]
                    b = prev[at, k] * sign
                    cols[at, k, pulse_rows(t), :] = a + b
                    prev[at, k] = a - b
            echo_across(j).start()
            echo_core(j).start()

        @pl.when(j == 2)
        def _():
            for k in (0, 1):
                scaling_chip(k).wait_recv()
            share(0)

        @pl.when(j == 3)
        def _():
            @pl.loop(0, n_one)
            def _(a):
                own_range(a).wait()

            turn_rows(lambda g: range_piece(g, 1 - y, half, 2)[...], mid, swap, 0)
            range_chip().start()

        @pl.when(j == 5)
        def _():
            turn_rows(lambda g: range_piece(g, y, half, 2)[...], mid, turn, y * half)

            @pl.loop(0, spans)
            def _(i):
                own_phase(azimuth_ref, i, 1).start()

        @pl.when(j == 8)
        def _():
            range_chip().wait_recv()
            share(1)

        @pl.when(j == chunks - 1)
        def _():
            @pl.when(az + 1 < n_az)
            def _():
                for k in (0, 1):
                    up(0, k).start()

        for d in range(1, n_az):
            @pl.when((j == chunks - n_az + d - 1) & (az + d < n_az))
            def _():
                for k in (0, 1):
                    along(n_az - d, az + d, k).wait_recv()
                    sideways(az + d, k).start()

        @pl.when(j >= 3)
        def _():
            now = j - 3
            echo_core(now).wait_recv()
            echo_forward(now).wait_recv()
            r = []
            for e in (0, 1):
                rows = pl.ds(e, pulses // 2, stride=2)
                s = jnp.concatenate(
                    [
                        jnp.concatenate([cols[now * chunk + i, k, rows, :] for k in (0, 1)], axis=0)
                        for i in range(chunk)
                    ],
                    axis=1,
                )
                s_hi, s_lo = split(s)
                hi, lo = front[0], front[1]
                x = mm(hi, s_hi) + mm(hi, s_lo) + mm(lo, s_hi)
                r.append((x[:half], x[half:]))
            w = tuple(jnp.concatenate([turn_front[k]] * chunk, axis=1) for k in (0, 1))
            r[1] = times(r[1], w)
            for k in (0, 1):
                a, b = r[0][k], r[1][k]
                at = pl.ds(pl.multiple_of(now * chunk * LANES, LANES), chunk * LANES)
                dop[k, pl.ds(0, half), at] = a + b
                dop[k, pl.ds(half, half), at] = a - b

        @pl.when((j >= 2) & (j < chunks + 2))
        def _():
            echo_across(j - 2).wait_recv()
            echo_forward(j - 2).start()

        @pl.when(j == chunks + 1)
        def _():
            relay(1)

    scaling_core().wait_recv()

    @pl.loop(0, blocks)
    def _(n):
        for i in range(2, n_az):
            @pl.when(n == 2 * i - 3)
            def _():
                relay(i)

        @pl.when(lax.rem(n, 2) == 0)
        def _():
            for k in (0, 1):
                sideways(order(n // 2), k).wait_recv()

        filter_block(
            dop, place(n)[2], block, scal, fwd_ref, inv_ref, range_twist_ref, turn, hi_ref, lo_ref, mid
        )

        @pl.when(n < whole)
        def _():
            for k in range(tiles - 1, 0, -1):
                back(n, k).start()
            keep(n).start()

    @pl.loop(0, spans)
    def _(j):
        for n in range(whole, blocks):
            for k in range(tiles - 1, 0, -1):
                back_span(j, n, k).start()
            keep_span(j, n).start()

    @pl.loop(0, spans)
    def _(j):
        own_phase(azimuth_ref, j, 1).wait()

    for n in range(whole):
        for k in range(1, tiles):
            back(n, k).wait_recv()
        keep(n).wait()

    @pl.loop(0, spans)
    def _(j):
        for n in range(whole, blocks):
            for k in range(1, tiles):
                back_span(j, n, k).wait_recv()
            keep_span(j, n).wait()
        hi, lo = table_ref[0], table_ref[1]
        slot = lax.rem(j, 2)

        @pl.when(j > 1)
        def _():
            put(j - 2).wait()

        v = []
        for f in range(4):
            rows = pl.ds(f * m, m)
            angle = jnp.concatenate(
                [phase[j, pl.ds(f * m + p, half, stride=2), :] for p in (0, 1)], axis=0
            )
            v.append(times((ret[0, rows, lanes(j)], ret[1, rows, lanes(j)]), sincos(angle)))
        for e, x in enumerate(four(v, 1)):
            if e:
                x = times(x, (twist_ref[2 * e - 2], twist_ref[2 * e - 1]))
            s_hi, s_lo = split(jnp.concatenate(x, axis=0))
            r = mm(hi, s_hi) + mm(hi, s_lo) + mm(lo, s_hi)
            for k in (0, 1):
                head[slot, k, pl.ds(e, q, stride=4), :] = r[k * q : (k + 1) * q]
        put(j).start()

    for j in range(max(0, spans - 2), spans):
        put(j).wait()

    @pl.when(az < n_az - 1)
    def _():
        @pl.loop(0, n_one)
        def _(a):
            onward(a).wait_send()

    @pl.loop(0, chunks)
    def _(j):
        echo_across(j).wait_send()
        echo_core(j).wait_send()
        echo_forward(j).wait_send()

    range_chip().wait_send()
    for k in (0, 1):
        scaling_chip(k).wait_send()
        for d in range(1, n_az):
            @pl.when(az + d >= n_az)
            def _():
                along(d, az, k).wait_send()

            @pl.when((az + 1 < n_az) & (az >= d - 1))
            def _():
                up(d - 1, k).wait_send()
        for z in range(n_az):
            sideways(z, k).wait_send()
    for n in range(whole):
        for k in range(1, tiles):
            back(n, k).wait_send()

    @pl.loop(0, spans)
    def _(j):
        for n in range(whole, blocks):
            for k in range(1, tiles):
                back_span(j, n, k).wait_send()


def pair_body(raw_echo, phase_scaling, phase_range, phase_azimuth):
    tiles = lax.axis_size("tile")
    n_az, n_strip = lax.axis_size("az"), lax.axis_size("strip")
    pulses = raw_echo.shape[1] * tiles
    extent, width = phase_scaling.shape
    count, ranges = phase_range.shape
    m, q, half = extent // 4, pulses // 4, count // 2
    n_one, spans = ranges // LANES, width // LANES
    blocks = n_strip * n_az
    block = count // blocks
    chunk = 2
    chunks = n_one // chunk
    whole = blocks // 2 + 1
    rest = blocks - whole
    fine = np.concatenate([np.arange(0, m, 2), np.arange(1, m, 2)])
    lane = np.arange(LANES)
    vmem = pl.BlockSpec(memory_space=pltpu.VMEM)
    anyspace = pl.BlockSpec(memory_space=pl.ANY)
    dma = pltpu.SemaphoreType.DMA
    c, s = roots(np.arange(n_one), lane, ranges, -1)
    return pl.pallas_call(
        functools.partial(pair_kernel, n_strip, n_az, block, chunk),
        out_shape=jax.ShapeDtypeStruct((2, pulses, width), F32),
        in_specs=[anyspace] * 5 + [vmem] * 5,
        out_specs=anyspace,
        scratch_shapes=[
            pltpu.VMEM((n_one, 2, pulses, LANES), F32),
            pltpu.VMEM((n_one, 2, pulses // tiles, LANES), F32),
            pltpu.VMEM((2, count, ranges), F32),
            pltpu.VMEM((count, ranges), F32),
            pltpu.VMEM((n_one, half, LANES), F32),
            pltpu.VMEM((n_one, count, LANES), F32),
            pltpu.VMEM((spans, extent, LANES), F32),
            pltpu.VMEM((2, extent, width), F32),
            pltpu.VMEM((2, block, width), F32),
            pltpu.VMEM((2, count, pulses), BF16),
            pltpu.VMEM((2, half, LANES), F32),
            pltpu.VMEM((6, m, LANES), F32),
            pltpu.VMEM((2, 2, pulses, LANES), F32),
            pltpu.VMEM((n_one, block, 2 * LANES), BF16),
            pltpu.VMEM((n_one, block, 2 * LANES), BF16),
            pltpu.VMEM((2, n_one * LANES // 2, LANES), F32),
            dma((2, spans)), dma((n_one,)), dma((n_one,)), dma,
            dma((n_one,)), dma((n_one,)),
            dma((chunks,)), dma((chunks,)),
            dma((chunks,)), dma((chunks,)),
            dma((chunks,)), dma((chunks,)),
            dma, dma,
            dma((3,)), dma((3,)),
            dma((n_az, 2)), dma((n_az, 2)), dma((n_az, 2)),
            dma((n_az, 2)), dma((n_az, 2)),
            dma((whole, tiles - 1)), dma((whole, tiles - 1)), dma((whole,)),
            dma((spans, rest, tiles - 1)), dma((spans, rest, tiles - 1)), dma((spans, rest)),
            dma((2,)),
        ],
        compiler_params=pltpu.CompilerParams(
            collective_id=0, has_side_effects=True, vmem_limit_bytes=59 << 20
        ),
    )(
        raw_echo,
        phase_scaling,
        phase_range,
        phase_azimuth,
        pair_front(extent, pulses),
        pair_twists(extent, fine),
        right_table(lane, lane, LANES, -1),
        right_table(lane, lane, LANES, 1, 1.0 / ranges),
        np.stack([c, s]).astype(np.float32),
        left_table(np.arange(q), fine, m, 1, 1.0 / extent),
    )


def paired(raw_echo, phase_scaling, phase_range):
    tiles, n_az, n_strip = (lax.axis_size(a) for a in ("tile", "az", "strip"))
    count = phase_range.shape[0]
    blocks = n_az * n_strip
    return (
        tiles == 4
        and n_strip == 2
        and n_az > 1
        and count == 2 * LANES
        and phase_scaling.shape[0] == 2 * raw_echo.shape[1] * tiles
        and count % (16 * blocks) == 0
        and phase_range.shape[1] % (2 * LANES) == 0
    )


def body(raw_echo, phase_scaling, phase_range, phase_azimuth):
    plan = pair_body if paired(raw_echo, phase_scaling, phase_range) else tail_body
    return plan(raw_echo, phase_scaling, phase_range, phase_azimuth)


def solution(mesh):
    return jax.shard_map(
        body,
        mesh=mesh,
        in_specs=(
            P(None, ("strip", "az", "tile"), None),
            P(None, "tile"),
            P("tile", None),
            P(None, "tile"),
        ),
        out_specs=P(None, ("strip", "az"), "tile"),
        check_vma=False,
    )
```

```python
import functools
import math

import jax
import jax.numpy as jnp
import numpy as np
from jax import lax
from jax.experimental import pallas as pl
from jax.experimental.pallas import tpu as pltpu
from jax.sharding import PartitionSpec as P

F32 = jnp.float32
BF16 = jnp.bfloat16
LANES = 128


def halves(table):
    hi = np.asarray(table, np.float32).astype(jnp.bfloat16)
    lo = (np.asarray(table, np.float64) - hi.astype(np.float64)).astype(jnp.bfloat16)
    return np.stack([hi, lo])


def roots(rows, cols, modulus, direction):
    residue = np.outer(rows, cols) % modulus
    angle = residue * (direction * 2.0 * math.pi / modulus)
    return np.cos(angle), np.sin(angle)


def left_table(rows, cols, modulus, direction, scale=1.0):
    c, s = roots(rows, cols, modulus, direction)
    return halves(np.block([[c, -s], [s, c]]) * scale)


def right_table(rows, cols, modulus, direction, scale=1.0):
    c, s = roots(rows, cols, modulus, direction)
    return halves(np.block([[c, s], [-s, c]]) * scale)


def twist_table(count, length, modulus, direction):
    c, s = roots(np.arange(count), np.arange(length), modulus, direction)
    full = np.stack([c, s]).astype(np.float32)
    return np.ascontiguousarray(np.broadcast_to(full[..., None], full.shape + (LANES,)))


def split(x):
    hi = x.astype(BF16)
    return hi, (x - hi.astype(F32)).astype(BF16)


def mm(a, b):
    return jnp.dot(a, b, preferred_element_type=F32)


def times(a, t):
    return a[0] * t[0] - a[1] * t[1], a[0] * t[1] + a[1] * t[0]


def plus(a, b):
    return a[0] + b[0], a[1] + b[1]


def minus(a, b):
    return a[0] - b[0], a[1] - b[1]


def quarter(a, direction):
    return (-a[1], a[0]) if direction > 0 else (a[1], -a[0])


def four(v, direction):
    a, b = plus(v[0], v[2]), minus(v[0], v[2])
    c, d = plus(v[1], v[3]), quarter(minus(v[1], v[3]), direction)
    return [plus(a, c), plus(b, d), minus(a, c), minus(b, d)]


def fft(v, direction):
    n = len(v)
    if n == 1:
        return v
    if n == 2:
        return [plus(v[0], v[1]), minus(v[0], v[1])]
    if n == 4:
        return four(v, direction)
    parts = [fft(v[e::4], direction) for e in range(4)] if n % 4 == 0 else None
    out = [None] * n
    m = n // 4
    for f in range(m):
        items = []
        for e in range(4):
            x = parts[e][f]
            k = e * f % n
            if k == 0:
                pass
            elif 8 * k == n:
                h = np.float32(math.sqrt(0.5))
                q = quarter(x, direction)
                x = ((x[0] + q[0]) * h, (x[1] + q[1]) * h)
            elif 4 * k == n:
                x = quarter(x, direction)
            elif 8 * k == 3 * n:
                h = np.float32(math.sqrt(0.5))
                q = quarter(x, direction)
                x = ((q[0] - x[0]) * h, (q[1] - x[1]) * h)
            else:
                ang = direction * 2.0 * math.pi * k / n
                x = times(x, (np.float32(math.cos(ang)), np.float32(math.sin(ang))))
            items.append(x)
        got = four(items, direction)
        for j in range(4):
            out[f + j * m] = got[j]
    return out


def sincos(x):
    y = x * 0.5
    z = y * y
    s, c = -1.0 / 39916800, 1.0 / 479001600
    for a, b in ((362880, -3628800), (-5040, 40320), (120, -720), (-6, 24), (1, -2)):
        s = s * z + np.float32(1.0 / a)
        c = c * z + np.float32(1.0 / b)
    s = s * y
    c = c * z + 1.0
    return 1.0 - 2.0 * s * s, 2.0 * s * c


def greet(partners):
    barrier = pltpu.get_barrier_semaphore()
    for device in partners:
        pl.semaphore_signal(barrier, inc=1, device_id=device, device_id_type=pl.DeviceIdType.MESH)
    return barrier


def lanes(j):
    return pl.ds(pl.multiple_of(j * LANES, LANES), LANES)


def filter_rows(x_ref, base, block, fwd_ref, inv_ref, twist_ref, phase_ref, hi_ref, lo_ref, mid_ref):
    n_one = phase_ref.shape[0]
    step = 16
    f_hi, f_lo = fwd_ref[0], fwd_ref[1]
    b_hi, b_lo = inv_ref[0], inv_ref[1]

    @pl.loop(0, block // step)
    def _(i):
        rows = pl.ds(pl.multiple_of(i * step, step), step)
        at = pl.ds(pl.multiple_of(base + i * step, step), step)
        v = [
            tuple(x_ref[c, at, pl.ds(a * LANES, LANES)] for c in (0, 1))
            for a in range(n_one)
        ]
        for k, x in enumerate(fft(v, -1)):
            if k:
                x = times(x, (twist_ref[0, k : k + 1, :], twist_ref[1, k : k + 1, :]))
            for c in (0, 1):
                h, l = split(x[c])
                hi_ref[k, rows, pl.ds(c * LANES, LANES)] = h
                lo_ref[k, rows, pl.ds(c * LANES, LANES)] = l

    group = 4

    @pl.loop(0, n_one // group)
    def _(i):
        ks = pl.ds(i * group, group)
        flat = (group * block, 2 * LANES)
        h, l = hi_ref[ks].reshape(flat), lo_ref[ks].reshape(flat)
        r = mm(h, f_hi) + mm(l, f_hi) + mm(h, f_lo)
        turn = phase_ref[ks, pl.ds(pl.multiple_of(base, block), block), :]
        r = times((r[:, :LANES], r[:, LANES:]), sincos(turn.reshape(group * block, LANES)))
        h, l = split(jnp.concatenate(r, axis=1))
        r = mm(h, b_hi) + mm(l, b_hi) + mm(h, b_lo)
        at = pl.ds(pl.multiple_of(i * group * block, block), group * block)
        mid_ref[0, at, :] = r[:, :LANES]
        mid_ref[1, at, :] = r[:, LANES:]

    @pl.loop(0, block // 8)
    def _(i):
        at = pl.ds(pl.multiple_of(base + i * 8, 8), 8)
        v = []
        for k in range(n_one):
            x = tuple(mid_ref[c, pl.ds(pl.multiple_of(k * block + i * 8, 8), 8), :] for c in (0, 1))
            if k:
                x = times(x, (twist_ref[0, k : k + 1, :], -twist_ref[1, k : k + 1, :]))
            v.append(x)
        for a, x in enumerate(fft(v, 1)):
            for c in (0, 1):
                x_ref[c, at, pl.ds(a * LANES, LANES)] = x[c]


def permute_turn(o_ref, mid, turn):
    n_one, count, _ = turn.shape
    half = mid.shape[1]
    some = min(count, LANES)
    part = half // n_one

    @pl.loop(0, count // some)
    def _(i):
        @pl.loop(0, n_one)
        def _(g):
            c, row, j = piece(g, count, o_ref)
            at = pl.ds(pl.multiple_of(row + i * some, some), some)
            x = o_ref[c, at, lanes(j)]
            if some < LANES:
                x = jnp.concatenate([x] * (LANES // some), axis=0)
            per = half // LANES
            mid[g // per, pl.ds(pl.multiple_of(g % per * LANES, LANES), LANES), :] = x.T

        @pl.loop(0, n_one)
        def _(k):
            rows = pl.ds(k, part, stride=n_one)
            x = jnp.concatenate([mid[h, rows, :] for h in range(LANES // part)], axis=0)
            at = pl.ds(pl.multiple_of(i * some, some), some)
            turn[k, at, :] = x.T[:some]


def piece(g, count, o_ref):
    across = o_ref.shape[2] // LANES
    down = o_ref.shape[1] // count
    return g // (across * down), g // across % down * count, g % across


def focus_kernel(
    tiles, length, block,
    raw_ref, scaling_ref, range_ref, azimuth_ref,
    front_ref, twist_ref, fwd_ref, inv_ref, range_twist_ref, table_ref,
    o_ref,
    spec, scaling, turn, phase, dop, ret, tail_out, tail_in, head, hi_ref, lo_ref, mid,
    send_e, recv_e, local_e, send_a, recv_a, local_a, send_b, recv_b, local_b,
    send_c, recv_c, load, load_range,
):
    me = lax.axis_index("tile")
    az = lax.axis_index("az")
    count = dop.shape[1]
    width = o_ref.shape[2]
    pulses = o_ref.shape[1]
    tail = tail_in.shape[2]
    rows_own = raw_ref.shape[1]
    n_one = turn.shape[0]
    blocks = count // block
    early = (blocks - 1) * block
    spans = width // LANES
    cols = tail_out
    m = spec.shape[1] // 4
    q = pulses // 4
    mine = pl.ds(pl.multiple_of(me * width, LANES), width)
    own = pl.ds(pl.multiple_of(me * count, count), count)
    own_pulses = pl.ds(pl.multiple_of(me * rows_own, rows_own), rows_own)

    def remote(src, dst, send, recv, device):
        return pltpu.make_async_remote_copy(
            src_ref=src, dst_ref=dst, send_sem=send, recv_sem=recv,
            device_id=device, device_id_type=pl.DeviceIdType.MESH,
        )

    def echo(j, k):
        to = lax.rem(me + k, tiles)
        return remote(
            raw_ref.at[:, :, lanes(to * spans + j)], cols.at[j, :, own_pulses, :],
            send_e.at[j, k - 1], recv_e.at[j, k - 1], {"tile": to},
        )

    def keep_echo(j):
        return pltpu.make_async_copy(
            raw_ref.at[:, :, lanes(me * spans + j)], cols.at[j, :, own_pulses, :], local_e.at[j]
        )

    def load_piece(g):
        c, row, j = piece(g, count, o_ref)
        return pltpu.make_async_copy(
            range_ref.at[:, lanes(g)],
            o_ref.at[c, pl.ds(pl.multiple_of(row, count), count), lanes(j)],
            load_range.at[g],
        )

    def out_part(i, k, lo, n, slot):
        to = lax.rem(me + k, tiles)
        at = pl.ds(pl.multiple_of(me * width + lo, LANES), n)
        return remote(
            spec.at[:, pl.ds(pl.multiple_of(to * count + i * block, block), block), pl.ds(lo, n)],
            dop.at[:, pl.ds(pl.multiple_of(i * block, block), block), at],
            send_a.at[slot, k - 1], recv_a.at[slot, k - 1], {"tile": to},
        )

    def out(i, k):
        return out_part(i, k, 0, width, i)

    def first_out(k):
        return out_part(0, k, 0, width - LANES, blocks)

    def last_out(k):
        return out_part(0, k, width - LANES, LANES, 0)

    def back_rows(j, k, lo, n, slot):
        to = lax.rem(me + k, tiles)
        return remote(
            dop.at[:, pl.ds(lo, n), lanes(to * spans + j)],
            ret.at[j, :, pl.ds(pl.multiple_of(me * count + lo, 8), n), :],
            send_b.at[slot, k - 1], recv_b.at[slot, k - 1], {"tile": to},
        )

    def first_rows(k):
        return back_rows(0, k, 0, early, spans)

    def last_rows(k):
        return back_rows(0, k, early, count - early, 0)

    def back(j, k):
        return back_rows(j, k, 0, count, j)

    def keep(j):
        return pltpu.make_async_copy(
            dop.at[:, :, lanes(me * spans + j)], ret.at[j, :, own, :], local_b.at[j]
        )

    def onward(j):
        return remote(
            tail_out.at[j, :, pl.ds(0, tail), :], tail_in.at[j], send_c.at[j], recv_c.at[j],
            {"az": lax.rem(az + 1, length)},
        )

    barrier = greet(
        [{"tile": lax.rem(me + k, tiles)} for k in range(1, tiles)]
        + [{"az": lax.rem(az + 1, length)}, {"az": lax.rem(az + length - 1, length)}]
    )
    get_scaling = pltpu.make_async_copy(scaling_ref, scaling, load.at[0])
    get_phase = pltpu.make_async_copy(azimuth_ref, phase, load.at[1])
    pl.semaphore_wait(barrier, tiles + 1)

    @pl.loop(0, spans)
    def _(j):
        for k in range(1, tiles):
            echo(j, k).start()
        keep_echo(j).start()

    @pl.loop(0, n_one)
    def _(g):
        load_piece(g).start()

    get_scaling.start()
    get_phase.start()

    get_scaling.wait()

    @pl.loop(0, spans)
    def _(j):
        @pl.when(j == spans - 1)
        def _():
            for k in range(1, tiles):
                first_out(k).start()

        for k in range(1, tiles):
            echo(j, k).wait_recv()
        keep_echo(j).wait()
        hi, lo = front_ref[0], front_ref[1]
        z = []
        for e in range(4):
            rows = pl.ds(e, q, stride=4)
            s = jnp.concatenate([cols[j, 0, rows, :], cols[j, 1, rows, :]], axis=0)
            s_hi, s_lo = split(s)
            r = mm(hi, s_hi) + mm(hi, s_lo) + mm(lo, s_hi)
            r = (r[:m], r[m:])
            if e:
                r = times(r, (twist_ref[0, e], -twist_ref[1, e]))
            z.append(r)
        for f, x in enumerate(four(z, -1)):
            rows = pl.ds(f * m, m)
            x = times(x, sincos(scaling[rows, lanes(j)]))
            spec[0, rows, lanes(j)] = x[0]
            spec[1, rows, lanes(j)] = x[1]

    for k in range(1, tiles):
        last_out(k).start()

    @pl.loop(1, blocks)
    def _(i):
        for k in range(1, tiles):
            out(i, k).start()

    first = pltpu.make_async_copy(spec.at[:, own, :], dop.at[:, :, mine], local_a)
    first.start()

    @pl.loop(0, n_one)
    def _(g):
        load_piece(g).wait()

    permute_turn(o_ref, mid, turn)
    first.wait()

    @pl.loop(0, blocks)
    def _(i):
        if early:
            @pl.when(i == blocks - 1)
            def _():
                for k in range(1, tiles):
                    first_rows(k).start()

        @pl.when(i == 0)
        def _():
            for k in range(1, tiles):
                first_out(k).wait_recv()
                last_out(k).wait_recv()

        @pl.when(i > 0)
        def _():
            for k in range(1, tiles):
                out(i, k).wait_recv()

        filter_rows(
            dop, i * block, block, fwd_ref, inv_ref, range_twist_ref, turn,
            hi_ref, lo_ref, mid,
        )

    for k in range(1, tiles):
        last_rows(k).start()
    keep(0).start()

    @pl.loop(1, spans)
    def _(j):
        for k in range(1, tiles):
            back(j, k).start()
        keep(j).start()

    get_phase.wait()

    @pl.loop(0, spans)
    def _(j):
        @pl.when(j == 0)
        def _():
            for k in range(1, tiles):
                if early:
                    first_rows(k).wait_recv()
                last_rows(k).wait_recv()

        @pl.when(j > 0)
        def _():
            for k in range(1, tiles):
                back(j, k).wait_recv()

        keep(j).wait()
        hi, lo = table_ref[0], table_ref[1]
        v = []
        for f in range(4):
            rows = pl.ds(f * m, m)
            v.append(times((ret[j, 0, rows, :], ret[j, 1, rows, :]), sincos(phase[rows, lanes(j)])))
        for e, x in enumerate(four(v, 1)):
            if e:
                x = times(x, (twist_ref[0, e], twist_ref[1, e]))
            s_hi, s_lo = split(jnp.concatenate(x, axis=0))
            r = mm(hi, s_hi) + mm(hi, s_lo) + mm(lo, s_hi)
            for c in (0, 1):
                head[c, pl.ds(e, q, stride=4), :] = r[c * m : c * m + q]
                tail_out[j, c, pl.ds(e, m - q, stride=4), :] = r[c * m + q : (c + 1) * m]

        @pl.when(az < length - 1)
        def _():
            onward(j).start()

        o_ref[:, :, lanes(j)] = head[...]

    @pl.when(az > 0)
    def _():
        @pl.loop(0, spans)
        def _(j):
            onward(j).wait_recv()
            o_ref[:, pl.ds(0, tail), lanes(j)] += tail_in[j]

    for k in range(1, tiles):
        first_out(k).wait_send()
        last_out(k).wait_send()

    @pl.loop(1, blocks)
    def _(i):
        for k in range(1, tiles):
            out(i, k).wait_send()

    for k in range(1, tiles):
        if early:
            first_rows(k).wait_send()
        last_rows(k).wait_send()

    @pl.loop(1, spans)
    def _(j):
        for k in range(1, tiles):
            back(j, k).wait_send()

    @pl.loop(0, spans)
    def _(j):
        for k in range(1, tiles):
            echo(j, k).wait_send()

    @pl.when(az < length - 1)
    def _():
        @pl.loop(0, spans)
        def _(j):
            onward(j).wait_send()


def tail_body(raw_echo, phase_scaling, phase_range, phase_azimuth):
    tiles = lax.axis_size("tile")
    length = lax.axis_size("az")
    pulses = raw_echo.shape[1] * tiles
    extent, width = phase_scaling.shape
    count, ranges = phase_range.shape
    m, q, tail = extent // 4, pulses // 4, extent - pulses
    n_one, spans = ranges // LANES, width // LANES
    block = min(64, count)
    rows, lane = np.arange(m), np.arange(LANES)
    vmem = pl.BlockSpec(memory_space=pltpu.VMEM)
    anyspace = pl.BlockSpec(memory_space=pl.ANY)
    dma = pltpu.SemaphoreType.DMA
    c, s = roots(np.arange(n_one), lane, ranges, -1)
    return pl.pallas_call(
        functools.partial(focus_kernel, tiles, length, block),
        out_shape=jax.ShapeDtypeStruct((2, pulses, width), F32),
        in_specs=[anyspace] * 4 + [vmem] * 6,
        out_specs=vmem,
        scratch_shapes=[
            pltpu.VMEM((2, extent, width), F32),
            pltpu.VMEM((extent, width), F32),
            pltpu.VMEM((n_one, count, LANES), F32),
            pltpu.VMEM((extent, width), F32),
            pltpu.VMEM((2, count, ranges), F32),
            pltpu.VMEM((spans, 2, extent, LANES), F32),
            pltpu.VMEM((spans, 2, max(tail, pulses), LANES), F32),
            pltpu.VMEM((spans, 2, tail, LANES), F32),
            pltpu.VMEM((2, pulses, LANES), F32),
            pltpu.VMEM((n_one, block, 2 * LANES), BF16),
            pltpu.VMEM((n_one, block, 2 * LANES), BF16),
            pltpu.VMEM((2, n_one * block, LANES), F32),
            dma((spans, tiles - 1)),
            dma((spans, tiles - 1)),
            dma((spans,)),
            dma((count // block + 1, tiles - 1)),
            dma((count // block + 1, tiles - 1)),
            dma,
            dma((spans + 1, tiles - 1)),
            dma((spans + 1, tiles - 1)),
            dma((spans,)),
            dma((spans,)),
            dma((spans,)),
            dma((2,)),
            dma((n_one,)),
        ],
        compiler_params=pltpu.CompilerParams(
            collective_id=0, has_side_effects=True, vmem_limit_bytes=63 << 20
        ),
    )(
        raw_echo,
        phase_scaling,
        phase_range,
        phase_azimuth,
        left_table(rows, np.arange(q), m, -1),
        twist_table(4, m, extent, 1),
        right_table(lane, lane, LANES, -1),
        right_table(lane, lane, LANES, 1, 1.0 / ranges),
        np.stack([c, s]).astype(np.float32),
        left_table(rows, rows, m, 1, 1.0 / extent),
    )


def pair_front(extent, pulses):
    m = extent // 4
    return np.stack(
        [left_table(2 * np.arange(m // 2) + y, 2 * np.arange(pulses // 2), extent, -1) for y in (0, 1)]
    )


def pair_twists(extent, fine):
    m = extent // 4
    out = np.zeros((m, LANES), np.float32)
    for e in range(1, 4):
        c, s = roots(fine, [e], extent, 1)
        out[:, 2 * e - 2 : 2 * e - 1], out[:, 2 * e - 1 : 2 * e] = c, s
    for t in range(4):
        c, s = roots(2 * np.arange(m // 2) + t // 2 + m * (t % 2), [1], extent, -1)
        out[: m // 2, 6 + 2 * t : 7 + 2 * t], out[: m // 2, 7 + 2 * t : 8 + 2 * t] = c, s
    return out


def filter_block(
    x_ref, base, block, scal_ref, fwd_ref, inv_ref, twist_ref, phase_ref, hi_ref, lo_ref, mid_ref
):
    n_one = phase_ref.shape[0]
    step = 16
    group = max(1, 256 // block)
    f_hi, f_lo = fwd_ref[0], fwd_ref[1]
    b_hi, b_lo = inv_ref[0], inv_ref[1]
    whole = pl.ds(pl.multiple_of(base, block), block)

    @pl.loop(0, n_one)
    def _(a):
        x = times((x_ref[0, whole, lanes(a)], x_ref[1, whole, lanes(a)]), sincos(scal_ref[whole, lanes(a)]))
        x_ref[0, whole, lanes(a)] = x[0]
        x_ref[1, whole, lanes(a)] = x[1]

    @pl.loop(0, block // step)
    def _(i):
        rows = pl.ds(pl.multiple_of(i * step, step), step)
        at = pl.ds(pl.multiple_of(base + i * step, step), step)
        v = [
            tuple(x_ref[c, at, pl.ds(a * LANES, LANES)] for c in (0, 1))
            for a in range(n_one)
        ]
        for k, x in enumerate(fft(v, -1)):
            if k:
                x = times(x, (twist_ref[0, k : k + 1, :], twist_ref[1, k : k + 1, :]))
            for c in (0, 1):
                h, l = split(x[c])
                hi_ref[k, rows, pl.ds(c * LANES, LANES)] = h
                lo_ref[k, rows, pl.ds(c * LANES, LANES)] = l

    @pl.loop(0, n_one // group)
    def _(i):
        ks = pl.ds(i * group, group)
        flat = (group * block, 2 * LANES)
        h, l = hi_ref[ks].reshape(flat), lo_ref[ks].reshape(flat)
        r = mm(h, f_hi) + mm(l, f_hi) + mm(h, f_lo)
        turn = phase_ref[ks, whole, :]
        r = times((r[:, :LANES], r[:, LANES:]), sincos(turn.reshape(group * block, LANES)))
        h, l = split(jnp.concatenate(r, axis=1))
        r = mm(h, b_hi) + mm(l, b_hi) + mm(h, b_lo)
        at = pl.ds(pl.multiple_of(i * group * block, block), group * block)
        mid_ref[0, at, :] = r[:, :LANES]
        mid_ref[1, at, :] = r[:, LANES:]

    @pl.loop(0, block // 8)
    def _(i):
        at = pl.ds(pl.multiple_of(base + i * 8, 8), 8)
        v = []
        for k in range(n_one):
            x = tuple(mid_ref[c, pl.ds(pl.multiple_of(k * block + i * 8, 8), 8), :] for c in (0, 1))
            if k:
                x = times(x, (twist_ref[0, k : k + 1, :], -twist_ref[1, k : k + 1, :]))
            v.append(x)
        for a, x in enumerate(fft(v, 1)):
            for c in (0, 1):
                x_ref[c, at, pl.ds(a * LANES, LANES)] = x[c]


def turn_rows(load, mid, turn, base):
    n_one = turn.shape[0]
    half = n_one * LANES // 2
    part = half // n_one
    per = half // LANES
    at = pl.ds(pl.multiple_of(base, LANES), LANES)

    @pl.loop(0, n_one)
    def _(g):
        mid[g // per, pl.ds(pl.multiple_of(g % per * LANES, LANES), LANES), :] = load(g).T

    @pl.loop(0, n_one)
    def _(k):
        rows = pl.ds(k, part, stride=n_one)
        x = jnp.concatenate([mid[h, rows, :] for h in range(LANES // part)], axis=0)
        turn[k, at, :] = x.T


def pair_kernel(
    n_strip, n_az, block, chunk,
    raw_ref, scaling_ref, range_ref, azimuth_ref, front_ref,
    twists_ref, fwd_ref, inv_ref, range_twist_ref, table_ref,
    o_ref,
    cols, prev, dop, scal, swap, turn, phase, ret, for_chip,
    front, turn_front, twist_ref, head, hi_ref, lo_ref, mid,
    load, load_range, load_echo, load_front, z_send, z_recv, y_send, y_recv, c_send, c_recv, f_send, f_recv,
    s_send, s_recv, p_send, p_recv, az_send, up_send, az_recv, x_send, x_recv,
    w_send, w_recv, w_local, v_send, v_recv, v_local, out_sem,
):
    t = lax.axis_index("tile")
    az = lax.axis_index("az")
    strip = lax.axis_index("strip")
    y, c = t // 2, t % 2
    tiles = 4
    count, ranges = range_ref.shape
    half = count // 2
    extent, width = scaling_ref.shape
    m = extent // 4
    pulses = o_ref.shape[1]
    q = pulses // 4
    rows_own = raw_ref.shape[1]
    spans = width // LANES
    n_one = ranges // LANES
    chunks = n_one // chunk
    blocks = count // block
    part = half // blocks
    whole = blocks - 2
    lag, steps = 2, 2
    step = block // steps
    partner, across = {"tile": 2 * y + 1 - c}, {"tile": 2 * (1 - y) + c}
    other = pl.ds(pl.multiple_of(2 * (1 - y) * width, LANES), 2 * width)
    mine = pl.ds(pl.multiple_of(t * width, LANES), width)
    slab = strip * n_az + az

    def remote(src, dst, send, recv, device):
        return pltpu.make_async_remote_copy(
            src_ref=src, dst_ref=dst, send_sem=send, recv_sem=recv,
            device_id=device, device_id_type=pl.DeviceIdType.MESH,
        )

    def pulse_rows(tile):
        return pl.ds(pl.multiple_of(tile * rows_own, rows_own), rows_own)

    def groups(j):
        return pl.ds(j * chunk, chunk)

    def onward(a):
        return remote(
            raw_ref.at[:, :, lanes(a)], prev.at[a], z_send.at[a], z_recv.at[a],
            {"az": lax.rem(az + 1, n_az)},
        )

    def own_echo(a):
        return pltpu.make_async_copy(
            raw_ref.at[:, :, lanes(a)], cols.at[a, :, pulse_rows(t), :], load_echo.at[a]
        )

    def range_piece(a, first, rows, stride=None):
        row = a % (extent // count) * count + first
        return phase.at[a // (extent // count), pl.ds(row, rows, stride=stride), :]

    def own_range(a):
        return pltpu.make_async_copy(range_ref.at[:, lanes(a)], range_piece(a, 0, count), load_range.at[a])

    def own_phase(source, j, k):
        return pltpu.make_async_copy(source.at[:, lanes(j)], phase.at[j], load.at[k, j])

    def echo_across(j):
        return remote(
            prev.at[groups(j)], cols.at[groups(j), :, pulse_rows(t), :],
            y_send.at[j], y_recv.at[j], across,
        )

    def echo_core(j):
        at = cols.at[groups(j), :, pulse_rows(t), :]
        return remote(at, at, c_send.at[j], c_recv.at[j], partner)

    def echo_forward(j):
        at = cols.at[groups(j), :, pulse_rows(2 * (1 - y) + c), :]
        return remote(at, at, f_send.at[j], f_recv.at[j], partner)

    def scaling_core():
        return remote(dop.at[0, :, pl.ds(0, width)], scal.at[:, mine], s_send, s_recv, partner)

    def scaling_chip(k):
        to = {"tile": 2 * (1 - y) + lax.rem(c + k, 2)}
        return remote(
            for_chip.at[lax.rem(c + k, 2)],
            scal.at[pl.ds(pl.multiple_of(slab * block, block), block), mine],
            p_send.at[k], p_recv.at[k], to,
        )

    def turn_part(ref, base, z, s):
        first = base + (z * n_strip + s) * part
        return ref.at[:, pl.ds(pl.multiple_of(first, part), part), :]

    def scal_rows(g):
        return scal.at[pl.ds(pl.multiple_of(g * block, block), block), other]

    def range_chip():
        return remote(
            turn_part(swap, 0, az, strip), turn_part(turn, y * half, az, strip),
            p_send.at[2], p_recv.at[2], across,
        )

    def slice_of(z, k):
        if k:
            return turn_part(turn, (1 - y) * half, z, strip)
        return scal_rows(strip * n_az + z)

    def along(d, z, k):
        to = {"az": lax.rem(az + d, n_az)}
        at = slice_of(z, k)
        return remote(at, at, az_send.at[d, k], az_recv.at[z, k], to)

    def up(i, k):
        at = slice_of(az - i, k)
        return remote(at, at, up_send.at[i, k], az_recv.at[az - i, k], {"az": lax.rem(az + 1, n_az)})

    def relay(i):
        @pl.when(az >= i)
        def _():
            for k in (0, 1):
                along(1, az - i, k).wait_recv()
                sideways(az - i, k).start()

                @pl.when(az + 1 < n_az)
                def _():
                    up(i, k).start()

    def sideways(z, k):
        at = slice_of(z, k)
        return remote(at, at, x_send.at[z, k], x_recv.at[z, k], {"strip": 1 - strip})

    def share(k):
        sideways(az, k).start()
        for d in range(n_az - 1, 0, -1):
            @pl.when(az + d >= n_az)
            def _():
                along(d, az, k).start()

    def order(n):
        return jnp.where(az + n < n_az, az + n, n_az - 1 - n)

    def place(n):
        s = jnp.where(lax.rem(n, 2) == 0, y, 1 - y)
        z = order(n // 2)
        base = (s * n_az + z) * block
        row = (2 * s + c) * m + y * half + z * block
        return pl.ds(pl.multiple_of(base, block), block), pl.ds(pl.multiple_of(row, block), block), base, row

    def piece_rows(u):
        _, _, base, row = place(u // steps)
        first = lax.rem(u, steps) * step
        return tuple(pl.ds(pl.multiple_of(x + first, step), step) for x in (base, row))

    def back(u, k):
        to = lax.rem(t + k, tiles)
        src, dst = piece_rows(u)
        at = pl.ds(pl.multiple_of(to * width, LANES), width)
        return remote(
            dop.at[:, src, at], ret.at[:, dst, :], w_send.at[u, k - 1], w_recv.at[u, k - 1], {"tile": to}
        )

    def keep(u):
        src, dst = piece_rows(u)
        return pltpu.make_async_copy(dop.at[:, src, mine], ret.at[:, dst, :], w_local.at[u])

    def back_span(j, n, k):
        to = lax.rem(t + k, tiles)
        src, dst, _, _ = place(n)
        return remote(
            dop.at[:, src, lanes(to * spans + j)], ret.at[:, dst, lanes(j)],
            v_send.at[j, n - whole, k - 1], v_recv.at[j, n - whole, k - 1], {"tile": to},
        )

    def keep_span(j, n):
        src, dst, _, _ = place(n)
        return pltpu.make_async_copy(
            dop.at[:, src, lanes(t * spans + j)], ret.at[:, dst, lanes(j)], v_local.at[j, n - whole]
        )

    def put(j):
        slot = lax.rem(j, 2)
        return pltpu.make_async_copy(head.at[slot], o_ref.at[:, :, lanes(j)], out_sem.at[slot])

    get_front = pltpu.make_async_copy(front_ref.at[y], front, load_front)

    @pl.loop(0, spans)
    def _(j):
        own_phase(scaling_ref, j, 0).start()

    @pl.loop(0, n_one)
    def _(a):
        own_echo(a).start()

    get_front.start()
    barrier = greet(
        [{"tile": lax.rem(t + k, tiles)} for k in range(1, tiles)]
        + [{"az": lax.rem(az + k, n_az)} for k in range(1, n_az)]
        + [{"strip": 1 - strip}]
    )
    pl.semaphore_wait(barrier, tiles + n_az - 1)

    @pl.when(az < n_az - 1)
    def _():
        @pl.loop(0, n_one)
        def _(a):
            onward(a).start()

    @pl.when(az == 0)
    def _():
        @pl.loop(0, n_one)
        def _(a):
            prev[a] = jnp.zeros((2, rows_own, LANES), F32)

    @pl.loop(0, spans)
    def _(j):
        own_phase(scaling_ref, j, 0).wait()
        for k in (0, 1):
            first = (2 * strip + k) * m + 2 * az * block + 1 - y
            for_chip[k, :, lanes(j)] = phase[j, pl.ds(first, block, stride=2), :]

    for k in (0, 1):
        scaling_chip(k).start()
    @pl.loop(0, spans)
    def _(j):
        for h in (0, 1):
            rows = pl.ds(h * half, half)
            dop[0, rows, lanes(j)] = phase[j, pl.ds((2 * h + 1 - c) * m + y, half, stride=2), :]
            scal[rows, lanes(t * spans + j)] = phase[j, pl.ds((2 * h + c) * m + y, half, stride=2), :]

    scaling_core().start()

    @pl.loop(0, n_one)
    def _(a):
        own_range(a).start()

    for k in range(6):
        twist_ref[k] = jnp.broadcast_to(twists_ref[:, k : k + 1], (m, LANES))
    for k in (0, 1):
        x = twists_ref[pl.ds(0, half), 6 + k : 7 + k]
        for i in range(1, tiles):
            x = jnp.where(t == i, twists_ref[pl.ds(0, half), 6 + 2 * i + k : 7 + 2 * i + k], x)
        turn_front[k] = jnp.broadcast_to(x, (half, LANES))
    scaling_core().wait_send()
    get_front.wait()
    odd = lax.rem(lax.broadcasted_iota(jnp.int32, (1, pulses), 1), 2) * c
    for k in (0, 1):
        front[k] = (front[k].astype(F32) * (1 - 2 * odd).astype(F32)).astype(BF16)
    sign = (1 - 2 * y).astype(F32)

    @pl.loop(0, chunks + lag + 1)
    def _(j):
        @pl.when(j < chunks)
        def _():
            for i in range(chunk):
                at = j * chunk + i
                own_echo(at).wait()

                @pl.when(az > 0)
                def _():
                    onward(at).wait_recv()

                for k in (0, 1):
                    a = cols[at, k, pulse_rows(t), :]
                    b = prev[at, k] * sign
                    cols[at, k, pulse_rows(t), :] = a + b
                    prev[at, k] = a - b
            echo_across(j).start()
            echo_core(j).start()

        @pl.when(j == 2)
        def _():
            for k in (0, 1):
                scaling_chip(k).wait_recv()
            share(0)

        @pl.when(j == 3)
        def _():
            @pl.loop(0, n_one)
            def _(a):
                own_range(a).wait()

            turn_rows(lambda g: range_piece(g, 1 - y, half, 2)[...], mid, swap, 0)
            range_chip().start()

        @pl.when(j == 5)
        def _():
            turn_rows(lambda g: range_piece(g, y, half, 2)[...], mid, turn, y * half)

            @pl.loop(0, spans)
            def _(i):
                own_phase(azimuth_ref, i, 1).start()

        @pl.when(j == 8)
        def _():
            range_chip().wait_recv()
            share(1)

        @pl.when(j == chunks - 1)
        def _():
            @pl.when(az + 1 < n_az)
            def _():
                for k in (0, 1):
                    up(0, k).start()

        for d in range(1, n_az):
            @pl.when((j == chunks - n_az + d - 1) & (az + d < n_az))
            def _():
                for k in (0, 1):
                    along(n_az - d, az + d, k).wait_recv()
                    sideways(az + d, k).start()

        @pl.when(j > lag)
        def _():
            now = j - lag - 1
            echo_core(now).wait_recv()
            echo_forward(now).wait_recv()
            r = []
            for e in (0, 1):
                rows = pl.ds(e, pulses // 2, stride=2)
                s = jnp.concatenate(
                    [
                        jnp.concatenate([cols[now * chunk + i, k, rows, :] for k in (0, 1)], axis=0)
                        for i in range(chunk)
                    ],
                    axis=1,
                )
                s_hi, s_lo = split(s)
                hi, lo = front[0], front[1]
                x = mm(hi, s_hi) + mm(hi, s_lo) + mm(lo, s_hi)
                r.append((x[:half], x[half:]))
            w = tuple(jnp.concatenate([turn_front[k]] * chunk, axis=1) for k in (0, 1))
            r[1] = times(r[1], w)
            for k in (0, 1):
                a, b = r[0][k], r[1][k]
                at = pl.ds(pl.multiple_of(now * chunk * LANES, LANES), chunk * LANES)
                dop[k, pl.ds(0, half), at] = a + b
                dop[k, pl.ds(half, half), at] = a - b

        @pl.when((j >= lag) & (j < chunks + lag))
        def _():
            echo_across(j - lag).wait_recv()
            echo_forward(j - lag).start()

        @pl.when(j == chunks + lag - 1)
        def _():
            relay(1)

    scaling_core().wait_recv()

    @pl.loop(0, blocks * steps)
    def _(u):
        for i in range(2, n_az):
            @pl.when(u == steps * (2 * i - 3))
            def _():
                relay(i)

        @pl.when(lax.rem(u, 2 * steps) == 0)
        def _():
            for k in (0, 1):
                sideways(order(u // (2 * steps)), k).wait_recv()

        filter_block(
            dop, place(u // steps)[2] + lax.rem(u, steps) * step, step,
            scal, fwd_ref, inv_ref, range_twist_ref, turn, hi_ref, lo_ref, mid,
        )

        @pl.when(u < whole * steps)
        def _():
            for k in range(tiles - 1, 0, -1):
                back(u, k).start()
            keep(u).start()

    @pl.loop(0, spans)
    def _(j):
        for n in range(whole, blocks):
            for k in range(tiles - 1, 0, -1):
                back_span(j, n, k).start()
            keep_span(j, n).start()

    @pl.loop(0, spans)
    def _(j):
        own_phase(azimuth_ref, j, 1).wait()

    @pl.loop(0, whole * steps)
    def _(u):
        for k in range(1, tiles):
            back(u, k).wait_recv()
        keep(u).wait()

    @pl.loop(0, spans)
    def _(j):
        for n in range(whole, blocks):
            for k in range(1, tiles):
                back_span(j, n, k).wait_recv()
            keep_span(j, n).wait()
        hi, lo = table_ref[0], table_ref[1]
        slot = lax.rem(j, 2)

        @pl.when(j > 1)
        def _():
            put(j - 2).wait()

        v = []
        for f in range(4):
            rows = pl.ds(f * m, m)
            angle = jnp.concatenate(
                [phase[j, pl.ds(f * m + p, half, stride=2), :] for p in (0, 1)], axis=0
            )
            v.append(times((ret[0, rows, lanes(j)], ret[1, rows, lanes(j)]), sincos(angle)))
        for e, x in enumerate(four(v, 1)):
            if e:
                x = times(x, (twist_ref[2 * e - 2], twist_ref[2 * e - 1]))
            s_hi, s_lo = split(jnp.concatenate(x, axis=0))
            r = mm(hi, s_hi) + mm(hi, s_lo) + mm(lo, s_hi)
            for k in (0, 1):
                head[slot, k, pl.ds(e, q, stride=4), :] = r[k * q : (k + 1) * q]
        put(j).start()

    for j in range(max(0, spans - 2), spans):
        put(j).wait()

    @pl.when(az < n_az - 1)
    def _():
        @pl.loop(0, n_one)
        def _(a):
            onward(a).wait_send()

    @pl.loop(0, chunks)
    def _(j):
        echo_across(j).wait_send()
        echo_core(j).wait_send()
        echo_forward(j).wait_send()

    range_chip().wait_send()
    for k in (0, 1):
        scaling_chip(k).wait_send()
        for d in range(1, n_az):
            @pl.when(az + d >= n_az)
            def _():
                along(d, az, k).wait_send()

            @pl.when((az + 1 < n_az) & (az >= d - 1))
            def _():
                up(d - 1, k).wait_send()
        for z in range(n_az):
            sideways(z, k).wait_send()

    @pl.loop(0, whole * steps)
    def _(u):
        for k in range(1, tiles):
            back(u, k).wait_send()

    @pl.loop(0, spans)
    def _(j):
        for n in range(whole, blocks):
            for k in range(1, tiles):
                back_span(j, n, k).wait_send()


def pair_body(raw_echo, phase_scaling, phase_range, phase_azimuth):
    tiles = lax.axis_size("tile")
    n_az, n_strip = lax.axis_size("az"), lax.axis_size("strip")
    pulses = raw_echo.shape[1] * tiles
    extent, width = phase_scaling.shape
    count, ranges = phase_range.shape
    m, q, half = extent // 4, pulses // 4, count // 2
    n_one, spans = ranges // LANES, width // LANES
    blocks = n_strip * n_az
    block = count // blocks
    chunk = 2
    chunks = n_one // chunk
    whole = blocks - 2
    rest = blocks - whole
    fine = np.concatenate([np.arange(0, m, 2), np.arange(1, m, 2)])
    lane = np.arange(LANES)
    vmem = pl.BlockSpec(memory_space=pltpu.VMEM)
    anyspace = pl.BlockSpec(memory_space=pl.ANY)
    dma = pltpu.SemaphoreType.DMA
    c, s = roots(np.arange(n_one), lane, ranges, -1)
    return pl.pallas_call(
        functools.partial(pair_kernel, n_strip, n_az, block, chunk),
        out_shape=pltpu.VMEM((2, pulses, width), F32),
        in_specs=[anyspace] * 5 + [vmem] * 5,
        out_specs=vmem,
        scratch_shapes=[
            pltpu.VMEM((n_one, 2, pulses, LANES), F32),
            pltpu.VMEM((n_one, 2, pulses // tiles, LANES), F32),
            pltpu.VMEM((2, count, ranges), F32),
            pltpu.VMEM((count, ranges), F32),
            pltpu.VMEM((n_one, half, LANES), F32),
            pltpu.VMEM((n_one, count, LANES), F32),
            pltpu.VMEM((spans, extent, LANES), F32),
            pltpu.VMEM((2, extent, width), F32),
            pltpu.VMEM((2, block, width), F32),
            pltpu.VMEM((2, count, pulses), BF16),
            pltpu.VMEM((2, half, LANES), F32),
            pltpu.VMEM((6, m, LANES), F32),
            pltpu.VMEM((2, 2, pulses, LANES), F32),
            pltpu.VMEM((n_one, block // 2, 2 * LANES), BF16),
            pltpu.VMEM((n_one, block // 2, 2 * LANES), BF16),
            pltpu.VMEM((2, n_one * LANES // 2, LANES), F32),
            dma((2, spans)), dma((n_one,)), dma((n_one,)), dma,
            dma((n_one,)), dma((n_one,)),
            dma((chunks,)), dma((chunks,)),
            dma((chunks,)), dma((chunks,)),
            dma((chunks,)), dma((chunks,)),
            dma, dma,
            dma((3,)), dma((3,)),
            dma((n_az, 2)), dma((n_az, 2)), dma((n_az, 2)),
            dma((n_az, 2)), dma((n_az, 2)),
            dma((2 * whole, tiles - 1)), dma((2 * whole, tiles - 1)), dma((2 * whole,)),
            dma((spans, rest, tiles - 1)), dma((spans, rest, tiles - 1)), dma((spans, rest)),
            dma((2,)),
        ],
        compiler_params=pltpu.CompilerParams(
            collective_id=0, has_side_effects=True, vmem_limit_bytes=59 << 20
        ),
    )(
        raw_echo,
        phase_scaling,
        phase_range,
        phase_azimuth,
        pair_front(extent, pulses),
        pair_twists(extent, fine),
        right_table(lane, lane, LANES, -1),
        right_table(lane, lane, LANES, 1, 1.0 / ranges),
        np.stack([c, s]).astype(np.float32),
        left_table(np.arange(q), fine, m, 1, 1.0 / extent),
    )


def paired(raw_echo, phase_scaling, phase_range):
    tiles, n_az, n_strip = (lax.axis_size(a) for a in ("tile", "az", "strip"))
    count = phase_range.shape[0]
    blocks = n_az * n_strip
    return (
        tiles == 4
        and n_strip == 2
        and n_az > 1
        and count == 2 * LANES
        and phase_scaling.shape[0] == 2 * raw_echo.shape[1] * tiles
        and count % (32 * blocks) == 0
        and phase_range.shape[1] % (2 * LANES) == 0
    )


def body(raw_echo, phase_scaling, phase_range, phase_azimuth):
    plan = pair_body if paired(raw_echo, phase_scaling, phase_range) else tail_body
    return plan(raw_echo, phase_scaling, phase_range, phase_azimuth)


def solution(mesh):
    return jax.shard_map(
        body,
        mesh=mesh,
        in_specs=(
            P(None, ("strip", "az", "tile"), None),
            P(None, "tile"),
            P("tile", None),
            P(None, "tile"),
        ),
        out_specs=P(None, ("strip", "az"), "tile"),
        check_vma=False,
    )
```

```python
import functools
import math

import jax
import jax.numpy as jnp
import numpy as np
from jax import lax
from jax.experimental import pallas as pl
from jax.experimental.pallas import tpu as pltpu
from jax.sharding import PartitionSpec as P

F32 = jnp.float32
BF16 = jnp.bfloat16
LANES = 128


def halves(table):
    hi = np.asarray(table, np.float32).astype(jnp.bfloat16)
    lo = (np.asarray(table, np.float64) - hi.astype(np.float64)).astype(jnp.bfloat16)
    return np.stack([hi, lo])


def roots(rows, cols, modulus, direction):
    residue = np.outer(rows, cols) % modulus
    angle = residue * (direction * 2.0 * math.pi / modulus)
    return np.cos(angle), np.sin(angle)


def left_table(rows, cols, modulus, direction, scale=1.0):
    c, s = roots(rows, cols, modulus, direction)
    return halves(np.block([[c, -s], [s, c]]) * scale)


def right_table(rows, cols, modulus, direction, scale=1.0):
    c, s = roots(rows, cols, modulus, direction)
    return halves(np.block([[c, s], [-s, c]]) * scale)


def twist_table(count, length, modulus, direction):
    c, s = roots(np.arange(count), np.arange(length), modulus, direction)
    full = np.stack([c, s]).astype(np.float32)
    return np.ascontiguousarray(np.broadcast_to(full[..., None], full.shape + (LANES,)))


def split(x):
    hi = x.astype(BF16)
    return hi, (x - hi.astype(F32)).astype(BF16)


def mm(a, b):
    return jnp.dot(a, b, preferred_element_type=F32)


def times(a, t):
    return a[0] * t[0] - a[1] * t[1], a[0] * t[1] + a[1] * t[0]


def plus(a, b):
    return a[0] + b[0], a[1] + b[1]


def minus(a, b):
    return a[0] - b[0], a[1] - b[1]


def quarter(a, direction):
    return (-a[1], a[0]) if direction > 0 else (a[1], -a[0])


def four(v, direction):
    a, b = plus(v[0], v[2]), minus(v[0], v[2])
    c, d = plus(v[1], v[3]), quarter(minus(v[1], v[3]), direction)
    return [plus(a, c), plus(b, d), minus(a, c), minus(b, d)]


def fft(v, direction):
    n = len(v)
    if n == 1:
        return v
    if n == 2:
        return [plus(v[0], v[1]), minus(v[0], v[1])]
    if n == 4:
        return four(v, direction)
    parts = [fft(v[e::4], direction) for e in range(4)] if n % 4 == 0 else None
    out = [None] * n
    m = n // 4
    for f in range(m):
        items = []
        for e in range(4):
            x = parts[e][f]
            k = e * f % n
            if k == 0:
                pass
            elif 8 * k == n:
                h = np.float32(math.sqrt(0.5))
                q = quarter(x, direction)
                x = ((x[0] + q[0]) * h, (x[1] + q[1]) * h)
            elif 4 * k == n:
                x = quarter(x, direction)
            elif 8 * k == 3 * n:
                h = np.float32(math.sqrt(0.5))
                q = quarter(x, direction)
                x = ((q[0] - x[0]) * h, (q[1] - x[1]) * h)
            else:
                ang = direction * 2.0 * math.pi * k / n
                x = times(x, (np.float32(math.cos(ang)), np.float32(math.sin(ang))))
            items.append(x)
        got = four(items, direction)
        for j in range(4):
            out[f + j * m] = got[j]
    return out


def sincos(x):
    y = x * 0.5
    z = y * y
    s, c = -1.0 / 39916800, 1.0 / 479001600
    for a, b in ((362880, -3628800), (-5040, 40320), (120, -720), (-6, 24), (1, -2)):
        s = s * z + np.float32(1.0 / a)
        c = c * z + np.float32(1.0 / b)
    s = s * y
    c = c * z + 1.0
    return 1.0 - 2.0 * s * s, 2.0 * s * c


def greet(partners):
    barrier = pltpu.get_barrier_semaphore()
    for device in partners:
        pl.semaphore_signal(barrier, inc=1, device_id=device, device_id_type=pl.DeviceIdType.MESH)
    return barrier


def lanes(j):
    return pl.ds(pl.multiple_of(j * LANES, LANES), LANES)


def filter_rows(x_ref, base, block, fwd_ref, inv_ref, twist_ref, phase_ref, hi_ref, lo_ref, mid_ref):
    n_one = phase_ref.shape[0]
    step = 16
    f_hi, f_lo = fwd_ref[0], fwd_ref[1]
    b_hi, b_lo = inv_ref[0], inv_ref[1]

    @pl.loop(0, block // step)
    def _(i):
        rows = pl.ds(pl.multiple_of(i * step, step), step)
        at = pl.ds(pl.multiple_of(base + i * step, step), step)
        v = [
            tuple(x_ref[c, at, pl.ds(a * LANES, LANES)] for c in (0, 1))
            for a in range(n_one)
        ]
        for k, x in enumerate(fft(v, -1)):
            if k:
                x = times(x, (twist_ref[0, k : k + 1, :], twist_ref[1, k : k + 1, :]))
            for c in (0, 1):
                h, l = split(x[c])
                hi_ref[k, rows, pl.ds(c * LANES, LANES)] = h
                lo_ref[k, rows, pl.ds(c * LANES, LANES)] = l

    group = 4

    @pl.loop(0, n_one // group)
    def _(i):
        ks = pl.ds(i * group, group)
        flat = (group * block, 2 * LANES)
        h, l = hi_ref[ks].reshape(flat), lo_ref[ks].reshape(flat)
        r = mm(h, f_hi) + mm(l, f_hi) + mm(h, f_lo)
        turn = phase_ref[ks, pl.ds(pl.multiple_of(base, block), block), :]
        r = times((r[:, :LANES], r[:, LANES:]), sincos(turn.reshape(group * block, LANES)))
        h, l = split(jnp.concatenate(r, axis=1))
        r = mm(h, b_hi) + mm(l, b_hi) + mm(h, b_lo)
        at = pl.ds(pl.multiple_of(i * group * block, block), group * block)
        mid_ref[0, at, :] = r[:, :LANES]
        mid_ref[1, at, :] = r[:, LANES:]

    @pl.loop(0, block // 8)
    def _(i):
        at = pl.ds(pl.multiple_of(base + i * 8, 8), 8)
        v = []
        for k in range(n_one):
            x = tuple(mid_ref[c, pl.ds(pl.multiple_of(k * block + i * 8, 8), 8), :] for c in (0, 1))
            if k:
                x = times(x, (twist_ref[0, k : k + 1, :], -twist_ref[1, k : k + 1, :]))
            v.append(x)
        for a, x in enumerate(fft(v, 1)):
            for c in (0, 1):
                x_ref[c, at, pl.ds(a * LANES, LANES)] = x[c]


def permute_turn(o_ref, mid, turn):
    n_one, count, _ = turn.shape
    half = mid.shape[1]
    some = min(count, LANES)
    part = half // n_one

    @pl.loop(0, count // some)
    def _(i):
        @pl.loop(0, n_one)
        def _(g):
            c, row, j = piece(g, count, o_ref)
            at = pl.ds(pl.multiple_of(row + i * some, some), some)
            x = o_ref[c, at, lanes(j)]
            if some < LANES:
                x = jnp.concatenate([x] * (LANES // some), axis=0)
            per = half // LANES
            mid[g // per, pl.ds(pl.multiple_of(g % per * LANES, LANES), LANES), :] = x.T

        @pl.loop(0, n_one)
        def _(k):
            rows = pl.ds(k, part, stride=n_one)
            x = jnp.concatenate([mid[h, rows, :] for h in range(LANES // part)], axis=0)
            at = pl.ds(pl.multiple_of(i * some, some), some)
            turn[k, at, :] = x.T[:some]


def piece(g, count, o_ref):
    across = o_ref.shape[2] // LANES
    down = o_ref.shape[1] // count
    return g // (across * down), g // across % down * count, g % across


def focus_kernel(
    tiles, length, block,
    raw_ref, scaling_ref, range_ref, azimuth_ref,
    front_ref, twist_ref, fwd_ref, inv_ref, range_twist_ref, table_ref,
    o_ref,
    spec, scaling, turn, phase, dop, ret, tail_out, tail_in, head, hi_ref, lo_ref, mid,
    send_e, recv_e, local_e, send_a, recv_a, local_a, send_b, recv_b, local_b,
    send_c, recv_c, load, load_range,
):
    me = lax.axis_index("tile")
    az = lax.axis_index("az")
    count = dop.shape[1]
    width = o_ref.shape[2]
    pulses = o_ref.shape[1]
    tail = tail_in.shape[2]
    rows_own = raw_ref.shape[1]
    n_one = turn.shape[0]
    blocks = count // block
    early = (blocks - 1) * block
    spans = width // LANES
    cols = tail_out
    m = spec.shape[1] // 4
    q = pulses // 4
    mine = pl.ds(pl.multiple_of(me * width, LANES), width)
    own = pl.ds(pl.multiple_of(me * count, count), count)
    own_pulses = pl.ds(pl.multiple_of(me * rows_own, rows_own), rows_own)

    def remote(src, dst, send, recv, device):
        return pltpu.make_async_remote_copy(
            src_ref=src, dst_ref=dst, send_sem=send, recv_sem=recv,
            device_id=device, device_id_type=pl.DeviceIdType.MESH,
        )

    def echo(j, k):
        to = lax.rem(me + k, tiles)
        return remote(
            raw_ref.at[:, :, lanes(to * spans + j)], cols.at[j, :, own_pulses, :],
            send_e.at[j, k - 1], recv_e.at[j, k - 1], {"tile": to},
        )

    def keep_echo(j):
        return pltpu.make_async_copy(
            raw_ref.at[:, :, lanes(me * spans + j)], cols.at[j, :, own_pulses, :], local_e.at[j]
        )

    def load_piece(g):
        c, row, j = piece(g, count, o_ref)
        return pltpu.make_async_copy(
            range_ref.at[:, lanes(g)],
            o_ref.at[c, pl.ds(pl.multiple_of(row, count), count), lanes(j)],
            load_range.at[g],
        )

    def out_part(i, k, lo, n, slot):
        to = lax.rem(me + k, tiles)
        at = pl.ds(pl.multiple_of(me * width + lo, LANES), n)
        return remote(
            spec.at[:, pl.ds(pl.multiple_of(to * count + i * block, block), block), pl.ds(lo, n)],
            dop.at[:, pl.ds(pl.multiple_of(i * block, block), block), at],
            send_a.at[slot, k - 1], recv_a.at[slot, k - 1], {"tile": to},
        )

    def out(i, k):
        return out_part(i, k, 0, width, i)

    def first_out(k):
        return out_part(0, k, 0, width - LANES, blocks)

    def last_out(k):
        return out_part(0, k, width - LANES, LANES, 0)

    def back_rows(j, k, lo, n, slot):
        to = lax.rem(me + k, tiles)
        return remote(
            dop.at[:, pl.ds(lo, n), lanes(to * spans + j)],
            ret.at[j, :, pl.ds(pl.multiple_of(me * count + lo, 8), n), :],
            send_b.at[slot, k - 1], recv_b.at[slot, k - 1], {"tile": to},
        )

    def first_rows(k):
        return back_rows(0, k, 0, early, spans)

    def last_rows(k):
        return back_rows(0, k, early, count - early, 0)

    def back(j, k):
        return back_rows(j, k, 0, count, j)

    def keep(j):
        return pltpu.make_async_copy(
            dop.at[:, :, lanes(me * spans + j)], ret.at[j, :, own, :], local_b.at[j]
        )

    def onward(j):
        return remote(
            tail_out.at[j, :, pl.ds(0, tail), :], tail_in.at[j], send_c.at[j], recv_c.at[j],
            {"az": lax.rem(az + 1, length)},
        )

    barrier = greet(
        [{"tile": lax.rem(me + k, tiles)} for k in range(1, tiles)]
        + [{"az": lax.rem(az + 1, length)}, {"az": lax.rem(az + length - 1, length)}]
    )
    get_scaling = pltpu.make_async_copy(scaling_ref, scaling, load.at[0])
    get_phase = pltpu.make_async_copy(azimuth_ref, phase, load.at[1])
    pl.semaphore_wait(barrier, tiles + 1)

    @pl.loop(0, spans)
    def _(j):
        for k in range(1, tiles):
            echo(j, k).start()
        keep_echo(j).start()

    @pl.loop(0, n_one)
    def _(g):
        load_piece(g).start()

    get_scaling.start()
    get_phase.start()

    get_scaling.wait()

    @pl.loop(0, spans)
    def _(j):
        @pl.when(j == spans - 1)
        def _():
            for k in range(1, tiles):
                first_out(k).start()

        for k in range(1, tiles):
            echo(j, k).wait_recv()
        keep_echo(j).wait()
        hi, lo = front_ref[0], front_ref[1]
        z = []
        for e in range(4):
            rows = pl.ds(e, q, stride=4)
            s = jnp.concatenate([cols[j, 0, rows, :], cols[j, 1, rows, :]], axis=0)
            s_hi, s_lo = split(s)
            r = mm(hi, s_hi) + mm(hi, s_lo) + mm(lo, s_hi)
            r = (r[:m], r[m:])
            if e:
                r = times(r, (twist_ref[0, e], -twist_ref[1, e]))
            z.append(r)
        for f, x in enumerate(four(z, -1)):
            rows = pl.ds(f * m, m)
            x = times(x, sincos(scaling[rows, lanes(j)]))
            spec[0, rows, lanes(j)] = x[0]
            spec[1, rows, lanes(j)] = x[1]

    for k in range(1, tiles):
        last_out(k).start()

    @pl.loop(1, blocks)
    def _(i):
        for k in range(1, tiles):
            out(i, k).start()

    first = pltpu.make_async_copy(spec.at[:, own, :], dop.at[:, :, mine], local_a)
    first.start()

    @pl.loop(0, n_one)
    def _(g):
        load_piece(g).wait()

    permute_turn(o_ref, mid, turn)
    first.wait()

    @pl.loop(0, blocks)
    def _(i):
        if early:
            @pl.when(i == blocks - 1)
            def _():
                for k in range(1, tiles):
                    first_rows(k).start()

        @pl.when(i == 0)
        def _():
            for k in range(1, tiles):
                first_out(k).wait_recv()
                last_out(k).wait_recv()

        @pl.when(i > 0)
        def _():
            for k in range(1, tiles):
                out(i, k).wait_recv()

        filter_rows(
            dop, i * block, block, fwd_ref, inv_ref, range_twist_ref, turn,
            hi_ref, lo_ref, mid,
        )

    for k in range(1, tiles):
        last_rows(k).start()
    keep(0).start()

    @pl.loop(1, spans)
    def _(j):
        for k in range(1, tiles):
            back(j, k).start()
        keep(j).start()

    get_phase.wait()

    @pl.loop(0, spans)
    def _(j):
        @pl.when(j == 0)
        def _():
            for k in range(1, tiles):
                if early:
                    first_rows(k).wait_recv()
                last_rows(k).wait_recv()

        @pl.when(j > 0)
        def _():
            for k in range(1, tiles):
                back(j, k).wait_recv()

        keep(j).wait()
        hi, lo = table_ref[0], table_ref[1]
        v = []
        for f in range(4):
            rows = pl.ds(f * m, m)
            v.append(times((ret[j, 0, rows, :], ret[j, 1, rows, :]), sincos(phase[rows, lanes(j)])))
        for e, x in enumerate(four(v, 1)):
            if e:
                x = times(x, (twist_ref[0, e], twist_ref[1, e]))
            s_hi, s_lo = split(jnp.concatenate(x, axis=0))
            r = mm(hi, s_hi) + mm(hi, s_lo) + mm(lo, s_hi)
            for c in (0, 1):
                head[c, pl.ds(e, q, stride=4), :] = r[c * m : c * m + q]
                tail_out[j, c, pl.ds(e, m - q, stride=4), :] = r[c * m + q : (c + 1) * m]

        @pl.when(az < length - 1)
        def _():
            onward(j).start()

        o_ref[:, :, lanes(j)] = head[...]

    @pl.when(az > 0)
    def _():
        @pl.loop(0, spans)
        def _(j):
            onward(j).wait_recv()
            o_ref[:, pl.ds(0, tail), lanes(j)] += tail_in[j]

    for k in range(1, tiles):
        first_out(k).wait_send()
        last_out(k).wait_send()

    @pl.loop(1, blocks)
    def _(i):
        for k in range(1, tiles):
            out(i, k).wait_send()

    for k in range(1, tiles):
        if early:
            first_rows(k).wait_send()
        last_rows(k).wait_send()

    @pl.loop(1, spans)
    def _(j):
        for k in range(1, tiles):
            back(j, k).wait_send()

    @pl.loop(0, spans)
    def _(j):
        for k in range(1, tiles):
            echo(j, k).wait_send()

    @pl.when(az < length - 1)
    def _():
        @pl.loop(0, spans)
        def _(j):
            onward(j).wait_send()


def tail_body(raw_echo, phase_scaling, phase_range, phase_azimuth):
    tiles = lax.axis_size("tile")
    length = lax.axis_size("az")
    pulses = raw_echo.shape[1] * tiles
    extent, width = phase_scaling.shape
    count, ranges = phase_range.shape
    m, q, tail = extent // 4, pulses // 4, extent - pulses
    n_one, spans = ranges // LANES, width // LANES
    block = min(64, count)
    rows, lane = np.arange(m), np.arange(LANES)
    vmem = pl.BlockSpec(memory_space=pltpu.VMEM)
    anyspace = pl.BlockSpec(memory_space=pl.ANY)
    dma = pltpu.SemaphoreType.DMA
    c, s = roots(np.arange(n_one), lane, ranges, -1)
    return pl.pallas_call(
        functools.partial(focus_kernel, tiles, length, block),
        out_shape=jax.ShapeDtypeStruct((2, pulses, width), F32),
        in_specs=[anyspace] * 4 + [vmem] * 6,
        out_specs=vmem,
        scratch_shapes=[
            pltpu.VMEM((2, extent, width), F32),
            pltpu.VMEM((extent, width), F32),
            pltpu.VMEM((n_one, count, LANES), F32),
            pltpu.VMEM((extent, width), F32),
            pltpu.VMEM((2, count, ranges), F32),
            pltpu.VMEM((spans, 2, extent, LANES), F32),
            pltpu.VMEM((spans, 2, max(tail, pulses), LANES), F32),
            pltpu.VMEM((spans, 2, tail, LANES), F32),
            pltpu.VMEM((2, pulses, LANES), F32),
            pltpu.VMEM((n_one, block, 2 * LANES), BF16),
            pltpu.VMEM((n_one, block, 2 * LANES), BF16),
            pltpu.VMEM((2, n_one * block, LANES), F32),
            dma((spans, tiles - 1)),
            dma((spans, tiles - 1)),
            dma((spans,)),
            dma((count // block + 1, tiles - 1)),
            dma((count // block + 1, tiles - 1)),
            dma,
            dma((spans + 1, tiles - 1)),
            dma((spans + 1, tiles - 1)),
            dma((spans,)),
            dma((spans,)),
            dma((spans,)),
            dma((2,)),
            dma((n_one,)),
        ],
        compiler_params=pltpu.CompilerParams(
            collective_id=0, has_side_effects=True, vmem_limit_bytes=63 << 20
        ),
    )(
        raw_echo,
        phase_scaling,
        phase_range,
        phase_azimuth,
        left_table(rows, np.arange(q), m, -1),
        twist_table(4, m, extent, 1),
        right_table(lane, lane, LANES, -1),
        right_table(lane, lane, LANES, 1, 1.0 / ranges),
        np.stack([c, s]).astype(np.float32),
        left_table(rows, rows, m, 1, 1.0 / extent),
    )


def pair_front(extent, pulses):
    m = extent // 4
    return np.stack(
        [left_table(2 * np.arange(m // 2) + y, 2 * np.arange(pulses // 2), extent, -1) for y in (0, 1)]
    )


def pair_twists(extent, fine):
    m = extent // 4
    out = np.zeros((m, LANES), np.float32)
    for e in range(1, 4):
        c, s = roots(fine, [e], extent, 1)
        out[:, 2 * e - 2 : 2 * e - 1], out[:, 2 * e - 1 : 2 * e] = c, s
    for t in range(4):
        c, s = roots(2 * np.arange(m // 2) + t // 2 + m * (t % 2), [1], extent, -1)
        out[: m // 2, 6 + 2 * t : 7 + 2 * t], out[: m // 2, 7 + 2 * t : 8 + 2 * t] = c, s
    return out


def filter_block(
    x_ref, base, block, scal_ref, fwd_ref, inv_ref, twist_ref, phase_ref, hi_ref, lo_ref, mid_ref
):
    n_one = phase_ref.shape[0]
    step = 16
    group = max(1, 256 // block)
    f_hi, f_lo = fwd_ref[0], fwd_ref[1]
    b_hi, b_lo = inv_ref[0], inv_ref[1]
    whole = pl.ds(pl.multiple_of(base, block), block)

    @pl.loop(0, n_one)
    def _(a):
        x = times((x_ref[0, whole, lanes(a)], x_ref[1, whole, lanes(a)]), sincos(scal_ref[whole, lanes(a)]))
        x_ref[0, whole, lanes(a)] = x[0]
        x_ref[1, whole, lanes(a)] = x[1]

    @pl.loop(0, block // step)
    def _(i):
        rows = pl.ds(pl.multiple_of(i * step, step), step)
        at = pl.ds(pl.multiple_of(base + i * step, step), step)
        v = [
            tuple(x_ref[c, at, pl.ds(a * LANES, LANES)] for c in (0, 1))
            for a in range(n_one)
        ]
        for k, x in enumerate(fft(v, -1)):
            if k:
                x = times(x, (twist_ref[0, k : k + 1, :], twist_ref[1, k : k + 1, :]))
            for c in (0, 1):
                h, l = split(x[c])
                hi_ref[k, rows, pl.ds(c * LANES, LANES)] = h
                lo_ref[k, rows, pl.ds(c * LANES, LANES)] = l

    @pl.loop(0, n_one // group)
    def _(i):
        ks = pl.ds(i * group, group)
        flat = (group * block, 2 * LANES)
        h, l = hi_ref[ks].reshape(flat), lo_ref[ks].reshape(flat)
        r = mm(h, f_hi) + mm(l, f_hi) + mm(h, f_lo)
        turn = phase_ref[ks, whole, :]
        r = times((r[:, :LANES], r[:, LANES:]), sincos(turn.reshape(group * block, LANES)))
        h, l = split(jnp.concatenate(r, axis=1))
        r = mm(h, b_hi) + mm(l, b_hi) + mm(h, b_lo)
        at = pl.ds(pl.multiple_of(i * group * block, block), group * block)
        mid_ref[0, at, :] = r[:, :LANES]
        mid_ref[1, at, :] = r[:, LANES:]

    @pl.loop(0, block // 8)
    def _(i):
        at = pl.ds(pl.multiple_of(base + i * 8, 8), 8)
        v = []
        for k in range(n_one):
            x = tuple(mid_ref[c, pl.ds(pl.multiple_of(k * block + i * 8, 8), 8), :] for c in (0, 1))
            if k:
                x = times(x, (twist_ref[0, k : k + 1, :], -twist_ref[1, k : k + 1, :]))
            v.append(x)
        for a, x in enumerate(fft(v, 1)):
            for c in (0, 1):
                x_ref[c, at, pl.ds(a * LANES, LANES)] = x[c]


def turn_in(load, mid, start, stop):
    per = mid.shape[1] // LANES

    @pl.loop(start, stop)
    def _(g):
        mid[g // per, pl.ds(pl.multiple_of(g % per * LANES, LANES), LANES), :] = load(g).T


def turn_out(mid, turn, base, start, stop):
    n_one = turn.shape[0]
    part = mid.shape[1] // n_one
    at = pl.ds(pl.multiple_of(base, LANES), LANES)

    @pl.loop(start, stop)
    def _(k):
        rows = pl.ds(k, part, stride=n_one)
        x = jnp.concatenate([mid[h, rows, :] for h in range(LANES // part)], axis=0)
        turn[k, at, :] = x.T


def pair_kernel(
    n_strip, n_az, block, chunk,
    raw_ref, scaling_ref, range_ref, azimuth_ref, front_ref,
    twists_ref, fwd_ref, inv_ref, range_twist_ref, table_ref,
    o_ref,
    cols, prev, dop, scal, swap, turn, phase, ret, for_chip,
    front, turn_front, twist_ref, head, hi_ref, lo_ref, mid,
    load, load_range, load_echo, load_front, z_send, z_recv, y_send, y_recv, c_send, c_recv, f_send, f_recv,
    s_send, s_recv, p_send, p_recv, az_send, up_send, az_recv, x_send, x_recv,
    w_send, w_recv, w_local, v_send, v_recv, v_local, out_sem,
):
    t = lax.axis_index("tile")
    az = lax.axis_index("az")
    strip = lax.axis_index("strip")
    y, c = t // 2, t % 2
    tiles = 4
    count, ranges = range_ref.shape
    half = count // 2
    extent, width = scaling_ref.shape
    m = extent // 4
    pulses = o_ref.shape[1]
    q = pulses // 4
    rows_own = raw_ref.shape[1]
    spans = width // LANES
    n_one = ranges // LANES
    chunks = n_one // chunk
    blocks = count // block
    part = half // blocks
    parts = chunks // 4
    whole = blocks - 2
    lag, steps = 2, 2
    step = block // steps
    partner, across = {"tile": 2 * y + 1 - c}, {"tile": 2 * (1 - y) + c}
    other = pl.ds(pl.multiple_of(2 * (1 - y) * width, LANES), 2 * width)
    mine = pl.ds(pl.multiple_of(t * width, LANES), width)
    slab = strip * n_az + az

    def remote(src, dst, send, recv, device):
        return pltpu.make_async_remote_copy(
            src_ref=src, dst_ref=dst, send_sem=send, recv_sem=recv,
            device_id=device, device_id_type=pl.DeviceIdType.MESH,
        )

    def pulse_rows(tile):
        return pl.ds(pl.multiple_of(tile * rows_own, rows_own), rows_own)

    def groups(j):
        return pl.ds(j * chunk, chunk)

    def onward(a):
        return remote(
            raw_ref.at[:, :, lanes(a)], prev.at[a], z_send.at[a], z_recv.at[a],
            {"az": lax.rem(az + 1, n_az)},
        )

    def own_echo(a):
        return pltpu.make_async_copy(
            raw_ref.at[:, :, lanes(a)], cols.at[a, :, pulse_rows(t), :], load_echo.at[a]
        )

    def range_piece(a, first, rows, stride=None):
        row = a % (extent // count) * count + first
        return phase.at[a // (extent // count), pl.ds(row, rows, stride=stride), :]

    def own_range(a):
        return pltpu.make_async_copy(range_ref.at[:, lanes(a)], range_piece(a, 0, count), load_range.at[a])

    def own_phase(source, j, k):
        return pltpu.make_async_copy(source.at[:, lanes(j)], phase.at[j], load.at[k, j])

    def echo_across(j):
        return remote(
            prev.at[j], cols.at[j, :, pulse_rows(t), :], y_send.at[j], y_recv.at[j], across,
        )

    def echo_core(j):
        at = cols.at[groups(j), :, pulse_rows(t), :]
        return remote(at, at, c_send.at[j], c_recv.at[j], partner)

    def echo_forward(j):
        at = cols.at[groups(j), :, pulse_rows(2 * (1 - y) + c), :]
        return remote(at, at, f_send.at[j], f_recv.at[j], partner)

    def scaling_core():
        return remote(dop.at[0, :, pl.ds(0, width)], scal.at[:, mine], s_send, s_recv, partner)

    def scaling_chip(k):
        to = {"tile": 2 * (1 - y) + lax.rem(c + k, 2)}
        return remote(
            for_chip.at[lax.rem(c + k, 2)],
            scal.at[pl.ds(pl.multiple_of(slab * block, block), block), mine],
            p_send.at[k], p_recv.at[k], to,
        )

    def turn_part(ref, base, z, s):
        first = base + (z * n_strip + s) * part
        return ref.at[:, pl.ds(pl.multiple_of(first, part), part), :]

    def scal_rows(g):
        return scal.at[pl.ds(pl.multiple_of(g * block, block), block), other]

    def range_chip():
        return remote(
            turn_part(swap, 0, az, strip), turn_part(turn, y * half, az, strip),
            p_send.at[2], p_recv.at[2], across,
        )

    def slice_of(z, k):
        if k:
            return turn_part(turn, (1 - y) * half, z, strip)
        return scal_rows(strip * n_az + z)

    def along(d, z, k):
        to = {"az": lax.rem(az + d, n_az)}
        at = slice_of(z, k)
        return remote(at, at, az_send.at[d, k], az_recv.at[z, k], to)

    def up(i, k):
        at = slice_of(az - i, k)
        return remote(at, at, up_send.at[i, k], az_recv.at[az - i, k], {"az": lax.rem(az + 1, n_az)})

    def relay(i, k):
        @pl.when(az >= i)
        def _():
            along(1, az - i, k).wait_recv()
            sideways(az - i, k).start()

            @pl.when(az + 1 < n_az)
            def _():
                up(i, k).start()

    def hand_over(d, k):
        @pl.when(az + d < n_az)
        def _():
            along(n_az - d, az + d, k).wait_recv()
            sideways(az + d, k).start()

    def sideways(z, k):
        at = slice_of(z, k)
        return remote(at, at, x_send.at[z, k], x_recv.at[z, k], {"strip": 1 - strip})

    def share(k):
        sideways(az, k).start()
        for d in range(n_az - 1, 0, -1):
            @pl.when(az + d >= n_az)
            def _():
                along(d, az, k).start()

    def order(n):
        return jnp.where(az + n < n_az, az + n, n_az - 1 - n)

    def place(n):
        s = jnp.where(n < n_az, y, 1 - y)
        z = order(lax.rem(n, n_az))
        base = (s * n_az + z) * block
        row = (2 * s + c) * m + y * half + z * block
        return pl.ds(pl.multiple_of(base, block), block), pl.ds(pl.multiple_of(row, block), block), base, row

    def piece_rows(u):
        _, _, base, row = place(u // steps)
        first = lax.rem(u, steps) * step
        return tuple(pl.ds(pl.multiple_of(x + first, step), step) for x in (base, row))

    def back(u, k):
        to = lax.rem(t + k, tiles)
        src, dst = piece_rows(u)
        at = pl.ds(pl.multiple_of(to * width, LANES), width)
        return remote(
            dop.at[:, src, at], ret.at[:, dst, :], w_send.at[u, k - 1], w_recv.at[u, k - 1], {"tile": to}
        )

    def keep(u):
        src, dst = piece_rows(u)
        return pltpu.make_async_copy(dop.at[:, src, mine], ret.at[:, dst, :], w_local.at[u])

    def back_span(j, n, k):
        to = lax.rem(t + k, tiles)
        src, dst, _, _ = place(n)
        return remote(
            dop.at[:, src, lanes(to * spans + j)], ret.at[:, dst, lanes(j)],
            v_send.at[j, n - whole, k - 1], v_recv.at[j, n - whole, k - 1], {"tile": to},
        )

    def keep_span(j, n):
        src, dst, _, _ = place(n)
        return pltpu.make_async_copy(
            dop.at[:, src, lanes(t * spans + j)], ret.at[:, dst, lanes(j)], v_local.at[j, n - whole]
        )

    def put(j):
        slot = lax.rem(j, 2)
        return pltpu.make_async_copy(head.at[slot], o_ref.at[:, :, lanes(j)], out_sem.at[slot])

    get_front = pltpu.make_async_copy(front_ref.at[y], front, load_front)

    @pl.loop(0, spans)
    def _(j):
        own_phase(scaling_ref, j, 0).start()

    @pl.loop(0, n_one)
    def _(a):
        own_echo(a).start()

    get_front.start()
    barrier = greet(
        [{"tile": lax.rem(t + k, tiles)} for k in range(1, tiles)]
        + [{"az": lax.rem(az + k, n_az)} for k in range(1, n_az)]
        + [{"strip": 1 - strip}]
    )
    pl.semaphore_wait(barrier, tiles + n_az - 1)

    @pl.when(az < n_az - 1)
    def _():
        @pl.loop(0, n_one)
        def _(a):
            onward(a).start()

    @pl.when(az == 0)
    def _():
        @pl.loop(0, n_one)
        def _(a):
            prev[a] = jnp.zeros((2, rows_own, LANES), F32)

    @pl.loop(0, spans)
    def _(j):
        own_phase(scaling_ref, j, 0).wait()
        for k in (0, 1):
            first = (2 * strip + k) * m + 2 * az * block + 1 - y
            for_chip[k, :, lanes(j)] = phase[j, pl.ds(first, block, stride=2), :]

    for k in (0, 1):
        scaling_chip(k).start()
    @pl.loop(0, spans)
    def _(j):
        for h in (0, 1):
            rows = pl.ds(h * half, half)
            dop[0, rows, lanes(j)] = phase[j, pl.ds((2 * h + 1 - c) * m + y, half, stride=2), :]
            scal[rows, lanes(t * spans + j)] = phase[j, pl.ds((2 * h + c) * m + y, half, stride=2), :]

    scaling_core().start()

    @pl.loop(0, n_one)
    def _(a):
        own_range(a).start()

    for k in range(6):
        twist_ref[k] = jnp.broadcast_to(twists_ref[:, k : k + 1], (m, LANES))
    for k in (0, 1):
        x = twists_ref[pl.ds(0, half), 6 + k : 7 + k]
        for i in range(1, tiles):
            x = jnp.where(t == i, twists_ref[pl.ds(0, half), 6 + 2 * i + k : 7 + 2 * i + k], x)
        turn_front[k] = jnp.broadcast_to(x, (half, LANES))
    scaling_core().wait_send()
    get_front.wait()
    odd = lax.rem(lax.broadcasted_iota(jnp.int32, (1, pulses), 1), 2) * c
    for k in (0, 1):
        front[k] = (front[k].astype(F32) * (1 - 2 * odd).astype(F32)).astype(BF16)
    sign = (1 - 2 * y).astype(F32)

    @pl.loop(0, chunks + lag + 1)
    def _(j):
        @pl.when(j < chunks)
        def _():
            for i in range(chunk):
                at = j * chunk + i
                own_echo(at).wait()

                @pl.when(az > 0)
                def _():
                    onward(at).wait_recv()

                for k in (0, 1):
                    a = cols[at, k, pulse_rows(t), :]
                    b = prev[at, k] * sign
                    cols[at, k, pulse_rows(t), :] = a + b
                    prev[at, k] = a - b
                echo_across(at).start()
            echo_core(j).start()

        @pl.when(j == 2)
        def _():
            for k in (0, 1):
                scaling_chip(k).wait_recv()
            share(0)

        @pl.when(j == 1)
        def _():
            @pl.loop(0, n_one)
            def _(a):
                own_range(a).wait()

        few = n_one // parts

        @pl.when((j >= 1) & (j < 1 + parts))
        def _():
            i = (j - 1) * few
            turn_in(lambda g: range_piece(g, 1 - y, half, 2)[...], mid, i, i + few)

        @pl.when((j >= 1 + parts) & (j < 1 + 2 * parts))
        def _():
            i = (j - 1 - parts) * few
            turn_out(mid, swap, 0, i, i + few)

        @pl.when((j >= 1 + 2 * parts) & (j < 1 + 3 * parts))
        def _():
            i = (j - 1 - 2 * parts) * few
            turn_in(lambda g: range_piece(g, y, half, 2)[...], mid, i, i + few)

        @pl.when((j >= 1 + 3 * parts) & (j < 1 + 4 * parts))
        def _():
            i = (j - 1 - 3 * parts) * few
            turn_out(mid, turn, y * half, i, i + few)

        @pl.when(j == 1 + 4 * parts)
        def _():
            @pl.loop(0, spans)
            def _(i):
                own_phase(azimuth_ref, i, 1).start()

        @pl.when(j == chunks - 1)
        def _():
            range_chip().start()

            @pl.when(az + 1 < n_az)
            def _():
                up(0, 0).start()

        for d in range(1, n_az):
            @pl.when(j == chunks - n_az + d - 1)
            def _():
                hand_over(d, 0)

        @pl.when(j > lag)
        def _():
            now = j - lag - 1
            echo_core(now).wait_recv()
            echo_forward(now).wait_recv()
            r = []
            for e in (0, 1):
                rows = pl.ds(e, pulses // 2, stride=2)
                s = jnp.concatenate(
                    [
                        jnp.concatenate([cols[now * chunk + i, k, rows, :] for k in (0, 1)], axis=0)
                        for i in range(chunk)
                    ],
                    axis=1,
                )
                s_hi, s_lo = split(s)
                hi, lo = front[0], front[1]
                x = mm(hi, s_hi) + mm(hi, s_lo) + mm(lo, s_hi)
                r.append((x[:half], x[half:]))
            w = tuple(jnp.concatenate([turn_front[k]] * chunk, axis=1) for k in (0, 1))
            r[1] = times(r[1], w)
            for k in (0, 1):
                a, b = r[0][k], r[1][k]
                at = pl.ds(pl.multiple_of(now * chunk * LANES, LANES), chunk * LANES)
                dop[k, pl.ds(0, half), at] = a + b
                dop[k, pl.ds(half, half), at] = a - b

        @pl.when((j >= lag) & (j < chunks + lag))
        def _():
            for i in range(chunk):
                echo_across((j - lag) * chunk + i).wait_recv()
            echo_forward(j - lag).start()

        @pl.when(j == chunks + lag - 1)
        def _():
            relay(1, 0)

    scaling_core().wait_recv()

    @pl.loop(0, blocks * steps)
    def _(u):
        for i in range(2, n_az):
            @pl.when(u == steps * (i - 1) - 1)
            def _():
                relay(i, 0)

        @pl.when((lax.rem(u, steps) == 0) & (u < n_az * steps))
        def _():
            sideways(order(u // steps), 0).wait_recv()

        @pl.when(u == 1)
        def _():
            range_chip().wait_recv()
            share(1)

            @pl.when(az + 1 < n_az)
            def _():
                up(0, 1).start()

        @pl.when(u == n_az * steps)
        def _():
            for i in range(1, n_az):
                hand_over(i, 1)
                relay(i, 1)
            for i in range(n_az):
                sideways(order(i), 1).wait_recv()

        filter_block(
            dop, place(u // steps)[2] + lax.rem(u, steps) * step, step,
            scal, fwd_ref, inv_ref, range_twist_ref, turn, hi_ref, lo_ref, mid,
        )

        @pl.when(u < whole * steps)
        def _():
            for k in range(tiles - 1, 0, -1):
                back(u, k).start()
            keep(u).start()

    @pl.loop(0, spans)
    def _(j):
        for n in range(whole, blocks):
            for k in range(tiles - 1, 0, -1):
                back_span(j, n, k).start()
            keep_span(j, n).start()

    @pl.loop(0, spans)
    def _(j):
        own_phase(azimuth_ref, j, 1).wait()

    @pl.loop(0, whole * steps)
    def _(u):
        for k in range(1, tiles):
            back(u, k).wait_recv()
        keep(u).wait()

    @pl.loop(0, spans)
    def _(j):
        for n in range(whole, blocks):
            for k in range(1, tiles):
                back_span(j, n, k).wait_recv()
            keep_span(j, n).wait()
        hi, lo = table_ref[0], table_ref[1]
        slot = lax.rem(j, 2)

        @pl.when(j > 1)
        def _():
            put(j - 2).wait()

        v = []
        for f in range(4):
            rows = pl.ds(f * m, m)
            angle = jnp.concatenate(
                [phase[j, pl.ds(f * m + p, half, stride=2), :] for p in (0, 1)], axis=0
            )
            v.append(times((ret[0, rows, lanes(j)], ret[1, rows, lanes(j)]), sincos(angle)))
        for e, x in enumerate(four(v, 1)):
            if e:
                x = times(x, (twist_ref[2 * e - 2], twist_ref[2 * e - 1]))
            s_hi, s_lo = split(jnp.concatenate(x, axis=0))
            r = mm(hi, s_hi) + mm(hi, s_lo) + mm(lo, s_hi)
            for k in (0, 1):
                head[slot, k, pl.ds(e, q, stride=4), :] = r[k * q : (k + 1) * q]
        put(j).start()

    for j in range(max(0, spans - 2), spans):
        put(j).wait()

    @pl.when(az < n_az - 1)
    def _():
        @pl.loop(0, n_one)
        def _(a):
            onward(a).wait_send()

    @pl.loop(0, chunks)
    def _(j):
        for i in range(chunk):
            echo_across(j * chunk + i).wait_send()
        echo_core(j).wait_send()
        echo_forward(j).wait_send()

    range_chip().wait_send()
    for k in (0, 1):
        scaling_chip(k).wait_send()
        for d in range(1, n_az):
            @pl.when(az + d >= n_az)
            def _():
                along(d, az, k).wait_send()

            @pl.when((az + 1 < n_az) & (az >= d - 1))
            def _():
                up(d - 1, k).wait_send()
        for z in range(n_az):
            sideways(z, k).wait_send()

    @pl.loop(0, whole * steps)
    def _(u):
        for k in range(1, tiles):
            back(u, k).wait_send()

    @pl.loop(0, spans)
    def _(j):
        for n in range(whole, blocks):
            for k in range(1, tiles):
                back_span(j, n, k).wait_send()


def pair_body(raw_echo, phase_scaling, phase_range, phase_azimuth):
    tiles = lax.axis_size("tile")
    n_az, n_strip = lax.axis_size("az"), lax.axis_size("strip")
    pulses = raw_echo.shape[1] * tiles
    extent, width = phase_scaling.shape
    count, ranges = phase_range.shape
    m, q, half = extent // 4, pulses // 4, count // 2
    n_one, spans = ranges // LANES, width // LANES
    blocks = n_strip * n_az
    block = count // blocks
    chunk = 2
    chunks = n_one // chunk
    whole = blocks - 2
    rest = blocks - whole
    fine = np.concatenate([np.arange(0, m, 2), np.arange(1, m, 2)])
    lane = np.arange(LANES)
    vmem = pl.BlockSpec(memory_space=pltpu.VMEM)
    anyspace = pl.BlockSpec(memory_space=pl.ANY)
    dma = pltpu.SemaphoreType.DMA
    c, s = roots(np.arange(n_one), lane, ranges, -1)
    return pl.pallas_call(
        functools.partial(pair_kernel, n_strip, n_az, block, chunk),
        out_shape=pltpu.VMEM((2, pulses, width), F32),
        in_specs=[anyspace] * 5 + [vmem] * 5,
        out_specs=vmem,
        scratch_shapes=[
            pltpu.VMEM((n_one, 2, pulses, LANES), F32),
            pltpu.VMEM((n_one, 2, pulses // tiles, LANES), F32),
            pltpu.VMEM((2, count, ranges), F32),
            pltpu.VMEM((count, ranges), F32),
            pltpu.VMEM((n_one, half, LANES), F32),
            pltpu.VMEM((n_one, count, LANES), F32),
            pltpu.VMEM((spans, extent, LANES), F32),
            pltpu.VMEM((2, extent, width), F32),
            pltpu.VMEM((2, block, width), F32),
            pltpu.VMEM((2, count, pulses), BF16),
            pltpu.VMEM((2, half, LANES), F32),
            pltpu.VMEM((6, m, LANES), F32),
            pltpu.VMEM((2, 2, pulses, LANES), F32),
            pltpu.VMEM((n_one, block // 2, 2 * LANES), BF16),
            pltpu.VMEM((n_one, block // 2, 2 * LANES), BF16),
            pltpu.VMEM((2, n_one * LANES // 2, LANES), F32),
            dma((2, spans)), dma((n_one,)), dma((n_one,)), dma,
            dma((n_one,)), dma((n_one,)),
            dma((n_one,)), dma((n_one,)),
            dma((chunks,)), dma((chunks,)),
            dma((chunks,)), dma((chunks,)),
            dma, dma,
            dma((3,)), dma((3,)),
            dma((n_az, 2)), dma((n_az, 2)), dma((n_az, 2)),
            dma((n_az, 2)), dma((n_az, 2)),
            dma((2 * whole, tiles - 1)), dma((2 * whole, tiles - 1)), dma((2 * whole,)),
            dma((spans, rest, tiles - 1)), dma((spans, rest, tiles - 1)), dma((spans, rest)),
            dma((2,)),
        ],
        compiler_params=pltpu.CompilerParams(
            collective_id=0, has_side_effects=True, vmem_limit_bytes=59 << 20
        ),
    )(
        raw_echo,
        phase_scaling,
        phase_range,
        phase_azimuth,
        pair_front(extent, pulses),
        pair_twists(extent, fine),
        right_table(lane, lane, LANES, -1),
        right_table(lane, lane, LANES, 1, 1.0 / ranges),
        np.stack([c, s]).astype(np.float32),
        left_table(np.arange(q), fine, m, 1, 1.0 / extent),
    )


def paired(raw_echo, phase_scaling, phase_range):
    tiles, n_az, n_strip = (lax.axis_size(a) for a in ("tile", "az", "strip"))
    count = phase_range.shape[0]
    blocks = n_az * n_strip
    return (
        tiles == 4
        and n_strip == 2
        and n_az > 1
        and count == 2 * LANES
        and phase_scaling.shape[0] == 2 * raw_echo.shape[1] * tiles
        and count % (32 * blocks) == 0
        and phase_range.shape[1] % (8 * LANES) == 0
    )


def body(raw_echo, phase_scaling, phase_range, phase_azimuth):
    plan = pair_body if paired(raw_echo, phase_scaling, phase_range) else tail_body
    return plan(raw_echo, phase_scaling, phase_range, phase_azimuth)


def solution(mesh):
    return jax.shard_map(
        body,
        mesh=mesh,
        in_specs=(
            P(None, ("strip", "az", "tile"), None),
            P(None, "tile"),
            P("tile", None),
            P(None, "tile"),
        ),
        out_specs=P(None, ("strip", "az"), "tile"),
        check_vma=False,
    )
```

```python
import functools
import math

import jax
import jax.numpy as jnp
import numpy as np
from jax import lax
from jax.experimental import pallas as pl
from jax.experimental.pallas import tpu as pltpu
from jax.sharding import PartitionSpec as P

F32 = jnp.float32
BF16 = jnp.bfloat16
LANES = 128


def halves(table):
    hi = np.asarray(table, np.float32).astype(jnp.bfloat16)
    lo = (np.asarray(table, np.float64) - hi.astype(np.float64)).astype(jnp.bfloat16)
    return np.stack([hi, lo])


def roots(rows, cols, modulus, direction):
    residue = np.outer(rows, cols) % modulus
    angle = residue * (direction * 2.0 * math.pi / modulus)
    return np.cos(angle), np.sin(angle)


def left_table(rows, cols, modulus, direction, scale=1.0):
    c, s = roots(rows, cols, modulus, direction)
    return halves(np.block([[c, -s], [s, c]]) * scale)


def right_table(rows, cols, modulus, direction, scale=1.0):
    c, s = roots(rows, cols, modulus, direction)
    return halves(np.block([[c, s], [-s, c]]) * scale)


def twist_table(count, length, modulus, direction):
    c, s = roots(np.arange(count), np.arange(length), modulus, direction)
    full = np.stack([c, s]).astype(np.float32)
    return np.ascontiguousarray(np.broadcast_to(full[..., None], full.shape + (LANES,)))


def split(x):
    hi = x.astype(BF16)
    return hi, (x - hi.astype(F32)).astype(BF16)


def mm(a, b):
    return jnp.dot(a, b, preferred_element_type=F32)


def times(a, t):
    return a[0] * t[0] - a[1] * t[1], a[0] * t[1] + a[1] * t[0]


def plus(a, b):
    return a[0] + b[0], a[1] + b[1]


def minus(a, b):
    return a[0] - b[0], a[1] - b[1]


def quarter(a, direction):
    return (-a[1], a[0]) if direction > 0 else (a[1], -a[0])


def four(v, direction):
    a, b = plus(v[0], v[2]), minus(v[0], v[2])
    c, d = plus(v[1], v[3]), quarter(minus(v[1], v[3]), direction)
    return [plus(a, c), plus(b, d), minus(a, c), minus(b, d)]


def fft(v, direction):
    n = len(v)
    if n == 1:
        return v
    if n == 2:
        return [plus(v[0], v[1]), minus(v[0], v[1])]
    if n == 4:
        return four(v, direction)
    parts = [fft(v[e::4], direction) for e in range(4)] if n % 4 == 0 else None
    out = [None] * n
    m = n // 4
    for f in range(m):
        items = []
        for e in range(4):
            x = parts[e][f]
            k = e * f % n
            if k == 0:
                pass
            elif 8 * k == n:
                h = np.float32(math.sqrt(0.5))
                q = quarter(x, direction)
                x = ((x[0] + q[0]) * h, (x[1] + q[1]) * h)
            elif 4 * k == n:
                x = quarter(x, direction)
            elif 8 * k == 3 * n:
                h = np.float32(math.sqrt(0.5))
                q = quarter(x, direction)
                x = ((q[0] - x[0]) * h, (q[1] - x[1]) * h)
            else:
                ang = direction * 2.0 * math.pi * k / n
                x = times(x, (np.float32(math.cos(ang)), np.float32(math.sin(ang))))
            items.append(x)
        got = four(items, direction)
        for j in range(4):
            out[f + j * m] = got[j]
    return out


def sincos(x):
    y = x * 0.5
    z = y * y
    s, c = -1.0 / 39916800, 1.0 / 479001600
    for a, b in ((362880, -3628800), (-5040, 40320), (120, -720), (-6, 24), (1, -2)):
        s = s * z + np.float32(1.0 / a)
        c = c * z + np.float32(1.0 / b)
    s = s * y
    c = c * z + 1.0
    return 1.0 - 2.0 * s * s, 2.0 * s * c


def greet(partners):
    barrier = pltpu.get_barrier_semaphore()
    for device in partners:
        pl.semaphore_signal(barrier, inc=1, device_id=device, device_id_type=pl.DeviceIdType.MESH)
    return barrier


def lanes(j):
    return pl.ds(pl.multiple_of(j * LANES, LANES), LANES)


def filter_rows(x_ref, base, block, fwd_ref, inv_ref, twist_ref, phase_ref, hi_ref, lo_ref, mid_ref):
    n_one = phase_ref.shape[0]
    step = 16
    f_hi, f_lo = fwd_ref[0], fwd_ref[1]
    b_hi, b_lo = inv_ref[0], inv_ref[1]

    @pl.loop(0, block // step)
    def _(i):
        rows = pl.ds(pl.multiple_of(i * step, step), step)
        at = pl.ds(pl.multiple_of(base + i * step, step), step)
        v = [
            tuple(x_ref[c, at, pl.ds(a * LANES, LANES)] for c in (0, 1))
            for a in range(n_one)
        ]
        for k, x in enumerate(fft(v, -1)):
            if k:
                x = times(x, (twist_ref[0, k : k + 1, :], twist_ref[1, k : k + 1, :]))
            for c in (0, 1):
                h, l = split(x[c])
                hi_ref[k, rows, pl.ds(c * LANES, LANES)] = h
                lo_ref[k, rows, pl.ds(c * LANES, LANES)] = l

    group = 4

    @pl.loop(0, n_one // group)
    def _(i):
        ks = pl.ds(i * group, group)
        flat = (group * block, 2 * LANES)
        h, l = hi_ref[ks].reshape(flat), lo_ref[ks].reshape(flat)
        r = mm(h, f_hi) + mm(l, f_hi) + mm(h, f_lo)
        turn = phase_ref[ks, pl.ds(pl.multiple_of(base, block), block), :]
        r = times((r[:, :LANES], r[:, LANES:]), sincos(turn.reshape(group * block, LANES)))
        h, l = split(jnp.concatenate(r, axis=1))
        r = mm(h, b_hi) + mm(l, b_hi) + mm(h, b_lo)
        at = pl.ds(pl.multiple_of(i * group * block, block), group * block)
        mid_ref[0, at, :] = r[:, :LANES]
        mid_ref[1, at, :] = r[:, LANES:]

    @pl.loop(0, block // 8)
    def _(i):
        at = pl.ds(pl.multiple_of(base + i * 8, 8), 8)
        v = []
        for k in range(n_one):
            x = tuple(mid_ref[c, pl.ds(pl.multiple_of(k * block + i * 8, 8), 8), :] for c in (0, 1))
            if k:
                x = times(x, (twist_ref[0, k : k + 1, :], -twist_ref[1, k : k + 1, :]))
            v.append(x)
        for a, x in enumerate(fft(v, 1)):
            for c in (0, 1):
                x_ref[c, at, pl.ds(a * LANES, LANES)] = x[c]


def permute_turn(o_ref, mid, turn):
    n_one, count, _ = turn.shape
    half = mid.shape[1]
    some = min(count, LANES)
    part = half // n_one

    @pl.loop(0, count // some)
    def _(i):
        @pl.loop(0, n_one)
        def _(g):
            c, row, j = piece(g, count, o_ref)
            at = pl.ds(pl.multiple_of(row + i * some, some), some)
            x = o_ref[c, at, lanes(j)]
            if some < LANES:
                x = jnp.concatenate([x] * (LANES // some), axis=0)
            per = half // LANES
            mid[g // per, pl.ds(pl.multiple_of(g % per * LANES, LANES), LANES), :] = x.T

        @pl.loop(0, n_one)
        def _(k):
            rows = pl.ds(k, part, stride=n_one)
            x = jnp.concatenate([mid[h, rows, :] for h in range(LANES // part)], axis=0)
            at = pl.ds(pl.multiple_of(i * some, some), some)
            turn[k, at, :] = x.T[:some]


def piece(g, count, o_ref):
    across = o_ref.shape[2] // LANES
    down = o_ref.shape[1] // count
    return g // (across * down), g // across % down * count, g % across


def focus_kernel(
    tiles, length, block,
    raw_ref, scaling_ref, range_ref, azimuth_ref,
    front_ref, twist_ref, fwd_ref, inv_ref, range_twist_ref, table_ref,
    o_ref,
    spec, scaling, turn, phase, dop, ret, tail_out, tail_in, head, hi_ref, lo_ref, mid,
    send_e, recv_e, local_e, send_a, recv_a, local_a, send_b, recv_b, local_b,
    send_c, recv_c, load, load_range,
):
    me = lax.axis_index("tile")
    az = lax.axis_index("az")
    count = dop.shape[1]
    width = o_ref.shape[2]
    pulses = o_ref.shape[1]
    tail = tail_in.shape[2]
    rows_own = raw_ref.shape[1]
    n_one = turn.shape[0]
    blocks = count // block
    early = (blocks - 1) * block
    spans = width // LANES
    cols = tail_out
    m = spec.shape[1] // 4
    q = pulses // 4
    mine = pl.ds(pl.multiple_of(me * width, LANES), width)
    own = pl.ds(pl.multiple_of(me * count, count), count)
    own_pulses = pl.ds(pl.multiple_of(me * rows_own, rows_own), rows_own)

    def remote(src, dst, send, recv, device):
        return pltpu.make_async_remote_copy(
            src_ref=src, dst_ref=dst, send_sem=send, recv_sem=recv,
            device_id=device, device_id_type=pl.DeviceIdType.MESH,
        )

    def echo(j, k):
        to = lax.rem(me + k, tiles)
        return remote(
            raw_ref.at[:, :, lanes(to * spans + j)], cols.at[j, :, own_pulses, :],
            send_e.at[j, k - 1], recv_e.at[j, k - 1], {"tile": to},
        )

    def keep_echo(j):
        return pltpu.make_async_copy(
            raw_ref.at[:, :, lanes(me * spans + j)], cols.at[j, :, own_pulses, :], local_e.at[j]
        )

    def load_piece(g):
        c, row, j = piece(g, count, o_ref)
        return pltpu.make_async_copy(
            range_ref.at[:, lanes(g)],
            o_ref.at[c, pl.ds(pl.multiple_of(row, count), count), lanes(j)],
            load_range.at[g],
        )

    def out_part(i, k, lo, n, slot):
        to = lax.rem(me + k, tiles)
        at = pl.ds(pl.multiple_of(me * width + lo, LANES), n)
        return remote(
            spec.at[:, pl.ds(pl.multiple_of(to * count + i * block, block), block), pl.ds(lo, n)],
            dop.at[:, pl.ds(pl.multiple_of(i * block, block), block), at],
            send_a.at[slot, k - 1], recv_a.at[slot, k - 1], {"tile": to},
        )

    def out(i, k):
        return out_part(i, k, 0, width, i)

    def first_out(k):
        return out_part(0, k, 0, width - LANES, blocks)

    def last_out(k):
        return out_part(0, k, width - LANES, LANES, 0)

    def back_rows(j, k, lo, n, slot):
        to = lax.rem(me + k, tiles)
        return remote(
            dop.at[:, pl.ds(lo, n), lanes(to * spans + j)],
            ret.at[j, :, pl.ds(pl.multiple_of(me * count + lo, 8), n), :],
            send_b.at[slot, k - 1], recv_b.at[slot, k - 1], {"tile": to},
        )

    def first_rows(k):
        return back_rows(0, k, 0, early, spans)

    def last_rows(k):
        return back_rows(0, k, early, count - early, 0)

    def back(j, k):
        return back_rows(j, k, 0, count, j)

    def keep(j):
        return pltpu.make_async_copy(
            dop.at[:, :, lanes(me * spans + j)], ret.at[j, :, own, :], local_b.at[j]
        )

    def onward(j):
        return remote(
            tail_out.at[j, :, pl.ds(0, tail), :], tail_in.at[j], send_c.at[j], recv_c.at[j],
            {"az": lax.rem(az + 1, length)},
        )

    barrier = greet(
        [{"tile": lax.rem(me + k, tiles)} for k in range(1, tiles)]
        + [{"az": lax.rem(az + 1, length)}, {"az": lax.rem(az + length - 1, length)}]
    )
    get_scaling = pltpu.make_async_copy(scaling_ref, scaling, load.at[0])
    get_phase = pltpu.make_async_copy(azimuth_ref, phase, load.at[1])
    pl.semaphore_wait(barrier, tiles + 1)

    @pl.loop(0, spans)
    def _(j):
        for k in range(1, tiles):
            echo(j, k).start()
        keep_echo(j).start()

    @pl.loop(0, n_one)
    def _(g):
        load_piece(g).start()

    get_scaling.start()
    get_phase.start()

    get_scaling.wait()

    @pl.loop(0, spans)
    def _(j):
        @pl.when(j == spans - 1)
        def _():
            for k in range(1, tiles):
                first_out(k).start()

        for k in range(1, tiles):
            echo(j, k).wait_recv()
        keep_echo(j).wait()
        hi, lo = front_ref[0], front_ref[1]
        z = []
        for e in range(4):
            rows = pl.ds(e, q, stride=4)
            s = jnp.concatenate([cols[j, 0, rows, :], cols[j, 1, rows, :]], axis=0)
            s_hi, s_lo = split(s)
            r = mm(hi, s_hi) + mm(hi, s_lo) + mm(lo, s_hi)
            r = (r[:m], r[m:])
            if e:
                r = times(r, (twist_ref[0, e], -twist_ref[1, e]))
            z.append(r)
        for f, x in enumerate(four(z, -1)):
            rows = pl.ds(f * m, m)
            x = times(x, sincos(scaling[rows, lanes(j)]))
            spec[0, rows, lanes(j)] = x[0]
            spec[1, rows, lanes(j)] = x[1]

    for k in range(1, tiles):
        last_out(k).start()

    @pl.loop(1, blocks)
    def _(i):
        for k in range(1, tiles):
            out(i, k).start()

    first = pltpu.make_async_copy(spec.at[:, own, :], dop.at[:, :, mine], local_a)
    first.start()

    @pl.loop(0, n_one)
    def _(g):
        load_piece(g).wait()

    permute_turn(o_ref, mid, turn)
    first.wait()

    @pl.loop(0, blocks)
    def _(i):
        if early:
            @pl.when(i == blocks - 1)
            def _():
                for k in range(1, tiles):
                    first_rows(k).start()

        @pl.when(i == 0)
        def _():
            for k in range(1, tiles):
                first_out(k).wait_recv()
                last_out(k).wait_recv()

        @pl.when(i > 0)
        def _():
            for k in range(1, tiles):
                out(i, k).wait_recv()

        filter_rows(
            dop, i * block, block, fwd_ref, inv_ref, range_twist_ref, turn,
            hi_ref, lo_ref, mid,
        )

    for k in range(1, tiles):
        last_rows(k).start()
    keep(0).start()

    @pl.loop(1, spans)
    def _(j):
        for k in range(1, tiles):
            back(j, k).start()
        keep(j).start()

    get_phase.wait()

    @pl.loop(0, spans)
    def _(j):
        @pl.when(j == 0)
        def _():
            for k in range(1, tiles):
                if early:
                    first_rows(k).wait_recv()
                last_rows(k).wait_recv()

        @pl.when(j > 0)
        def _():
            for k in range(1, tiles):
                back(j, k).wait_recv()

        keep(j).wait()
        hi, lo = table_ref[0], table_ref[1]
        v = []
        for f in range(4):
            rows = pl.ds(f * m, m)
            v.append(times((ret[j, 0, rows, :], ret[j, 1, rows, :]), sincos(phase[rows, lanes(j)])))
        for e, x in enumerate(four(v, 1)):
            if e:
                x = times(x, (twist_ref[0, e], twist_ref[1, e]))
            s_hi, s_lo = split(jnp.concatenate(x, axis=0))
            r = mm(hi, s_hi) + mm(hi, s_lo) + mm(lo, s_hi)
            for c in (0, 1):
                head[c, pl.ds(e, q, stride=4), :] = r[c * m : c * m + q]
                tail_out[j, c, pl.ds(e, m - q, stride=4), :] = r[c * m + q : (c + 1) * m]

        @pl.when(az < length - 1)
        def _():
            onward(j).start()

        o_ref[:, :, lanes(j)] = head[...]

    @pl.when(az > 0)
    def _():
        @pl.loop(0, spans)
        def _(j):
            onward(j).wait_recv()
            o_ref[:, pl.ds(0, tail), lanes(j)] += tail_in[j]

    for k in range(1, tiles):
        first_out(k).wait_send()
        last_out(k).wait_send()

    @pl.loop(1, blocks)
    def _(i):
        for k in range(1, tiles):
            out(i, k).wait_send()

    for k in range(1, tiles):
        if early:
            first_rows(k).wait_send()
        last_rows(k).wait_send()

    @pl.loop(1, spans)
    def _(j):
        for k in range(1, tiles):
            back(j, k).wait_send()

    @pl.loop(0, spans)
    def _(j):
        for k in range(1, tiles):
            echo(j, k).wait_send()

    @pl.when(az < length - 1)
    def _():
        @pl.loop(0, spans)
        def _(j):
            onward(j).wait_send()


def tail_body(raw_echo, phase_scaling, phase_range, phase_azimuth):
    tiles = lax.axis_size("tile")
    length = lax.axis_size("az")
    pulses = raw_echo.shape[1] * tiles
    extent, width = phase_scaling.shape
    count, ranges = phase_range.shape
    m, q, tail = extent // 4, pulses // 4, extent - pulses
    n_one, spans = ranges // LANES, width // LANES
    block = min(64, count)
    rows, lane = np.arange(m), np.arange(LANES)
    vmem = pl.BlockSpec(memory_space=pltpu.VMEM)
    anyspace = pl.BlockSpec(memory_space=pl.ANY)
    dma = pltpu.SemaphoreType.DMA
    c, s = roots(np.arange(n_one), lane, ranges, -1)
    return pl.pallas_call(
        functools.partial(focus_kernel, tiles, length, block),
        out_shape=jax.ShapeDtypeStruct((2, pulses, width), F32),
        in_specs=[anyspace] * 4 + [vmem] * 6,
        out_specs=vmem,
        scratch_shapes=[
            pltpu.VMEM((2, extent, width), F32),
            pltpu.VMEM((extent, width), F32),
            pltpu.VMEM((n_one, count, LANES), F32),
            pltpu.VMEM((extent, width), F32),
            pltpu.VMEM((2, count, ranges), F32),
            pltpu.VMEM((spans, 2, extent, LANES), F32),
            pltpu.VMEM((spans, 2, max(tail, pulses), LANES), F32),
            pltpu.VMEM((spans, 2, tail, LANES), F32),
            pltpu.VMEM((2, pulses, LANES), F32),
            pltpu.VMEM((n_one, block, 2 * LANES), BF16),
            pltpu.VMEM((n_one, block, 2 * LANES), BF16),
            pltpu.VMEM((2, n_one * block, LANES), F32),
            dma((spans, tiles - 1)),
            dma((spans, tiles - 1)),
            dma((spans,)),
            dma((count // block + 1, tiles - 1)),
            dma((count // block + 1, tiles - 1)),
            dma,
            dma((spans + 1, tiles - 1)),
            dma((spans + 1, tiles - 1)),
            dma((spans,)),
            dma((spans,)),
            dma((spans,)),
            dma((2,)),
            dma((n_one,)),
        ],
        compiler_params=pltpu.CompilerParams(
            collective_id=0, has_side_effects=True, vmem_limit_bytes=63 << 20
        ),
    )(
        raw_echo,
        phase_scaling,
        phase_range,
        phase_azimuth,
        left_table(rows, np.arange(q), m, -1),
        twist_table(4, m, extent, 1),
        right_table(lane, lane, LANES, -1),
        right_table(lane, lane, LANES, 1, 1.0 / ranges),
        np.stack([c, s]).astype(np.float32),
        left_table(rows, rows, m, 1, 1.0 / extent),
    )


def pair_front(extent, pulses):
    m = extent // 4
    return np.stack(
        [left_table(2 * np.arange(m // 2) + y, 2 * np.arange(pulses // 2), extent, -1) for y in (0, 1)]
    )


def pair_twists(extent, fine):
    m = extent // 4
    out = np.zeros((m, LANES), np.float32)
    for e in range(1, 4):
        c, s = roots(fine, [e], extent, 1)
        out[:, 2 * e - 2 : 2 * e - 1], out[:, 2 * e - 1 : 2 * e] = c, s
    for t in range(4):
        c, s = roots(2 * np.arange(m // 2) + t // 2 + m * (t % 2), [1], extent, -1)
        out[: m // 2, 6 + 2 * t : 7 + 2 * t], out[: m // 2, 7 + 2 * t : 8 + 2 * t] = c, s
    return out


def filter_block(
    x_ref, base, block, scal_ref, fwd_ref, inv_ref, twist_ref, phase_ref, hi_ref, lo_ref, mid_ref
):
    n_one = phase_ref.shape[0]
    step = 16
    group = max(1, 256 // block)
    f_hi, f_lo = fwd_ref[0], fwd_ref[1]
    b_hi, b_lo = inv_ref[0], inv_ref[1]
    whole = pl.ds(pl.multiple_of(base, block), block)

    @pl.loop(0, n_one)
    def _(a):
        x = times((x_ref[0, whole, lanes(a)], x_ref[1, whole, lanes(a)]), sincos(scal_ref[whole, lanes(a)]))
        x_ref[0, whole, lanes(a)] = x[0]
        x_ref[1, whole, lanes(a)] = x[1]

    @pl.loop(0, block // step)
    def _(i):
        rows = pl.ds(pl.multiple_of(i * step, step), step)
        at = pl.ds(pl.multiple_of(base + i * step, step), step)
        v = [
            tuple(x_ref[c, at, pl.ds(a * LANES, LANES)] for c in (0, 1))
            for a in range(n_one)
        ]
        for k, x in enumerate(fft(v, -1)):
            if k:
                x = times(x, (twist_ref[0, k : k + 1, :], twist_ref[1, k : k + 1, :]))
            for c in (0, 1):
                h, l = split(x[c])
                hi_ref[k, rows, pl.ds(c * LANES, LANES)] = h
                lo_ref[k, rows, pl.ds(c * LANES, LANES)] = l

    @pl.loop(0, n_one // group)
    def _(i):
        ks = pl.ds(i * group, group)
        flat = (group * block, 2 * LANES)
        h, l = hi_ref[ks].reshape(flat), lo_ref[ks].reshape(flat)
        r = mm(h, f_hi) + mm(l, f_hi) + mm(h, f_lo)
        turn = phase_ref[ks, whole, :]
        r = times((r[:, :LANES], r[:, LANES:]), sincos(turn.reshape(group * block, LANES)))
        h, l = split(jnp.concatenate(r, axis=1))
        r = mm(h, b_hi) + mm(l, b_hi) + mm(h, b_lo)
        at = pl.ds(pl.multiple_of(i * group * block, block), group * block)
        mid_ref[0, at, :] = r[:, :LANES]
        mid_ref[1, at, :] = r[:, LANES:]

    @pl.loop(0, block // 8)
    def _(i):
        at = pl.ds(pl.multiple_of(base + i * 8, 8), 8)
        v = []
        for k in range(n_one):
            x = tuple(mid_ref[c, pl.ds(pl.multiple_of(k * block + i * 8, 8), 8), :] for c in (0, 1))
            if k:
                x = times(x, (twist_ref[0, k : k + 1, :], -twist_ref[1, k : k + 1, :]))
            v.append(x)
        for a, x in enumerate(fft(v, 1)):
            for c in (0, 1):
                x_ref[c, at, pl.ds(a * LANES, LANES)] = x[c]


def turn_in(load, mid, start, stop):
    per = mid.shape[1] // LANES

    @pl.loop(start, stop)
    def _(g):
        mid[g // per, pl.ds(pl.multiple_of(g % per * LANES, LANES), LANES), :] = load(g).T


def turn_out(mid, turn, base, start, stop):
    n_one = turn.shape[0]
    part = mid.shape[1] // n_one
    at = pl.ds(pl.multiple_of(base, LANES), LANES)

    @pl.loop(start, stop)
    def _(k):
        rows = pl.ds(k, part, stride=n_one)
        x = jnp.concatenate([mid[h, rows, :] for h in range(LANES // part)], axis=0)
        turn[k, at, :] = x.T


def pair_kernel(
    n_strip, n_az, block, chunk,
    raw_ref, scaling_ref, range_ref, azimuth_ref, front_ref,
    twists_any, fwd_any, inv_any, range_twist_any, table_any,
    o_ref,
    twists_ref, fwd_ref, inv_ref, range_twist_ref, table_ref,
    cols, prev, dop, scal, swap, turn, phase, ret, for_chip,
    front, turn_front, twist_ref, spin, head, hi_ref, lo_ref, mid,
    load, load_range, load_echo, load_front, load_table, z_send, z_recv, y_send, y_recv, c_send, c_recv, f_send, f_recv,
    s_send, s_recv, p_send, p_recv, down_send, up_send, az_recv, x_send, x_recv,
    w_send, w_recv, w_local, v_send, v_recv, v_local, out_sem,
):
    t = lax.axis_index("tile")
    az = lax.axis_index("az")
    strip = lax.axis_index("strip")
    y, c = t // 2, t % 2
    tiles = 4
    count, ranges = range_ref.shape
    half = count // 2
    extent, width = scaling_ref.shape
    m = extent // 4
    pulses = o_ref.shape[1]
    q = pulses // 4
    rows_own = raw_ref.shape[1]
    spans = width // LANES
    n_one = ranges // LANES
    chunks = n_one // chunk
    blocks = count // block
    part = half // blocks
    parts = chunks // 4
    whole = blocks - 2
    lag, steps = 2, 2
    step = block // steps
    partner, across = {"tile": 2 * y + 1 - c}, {"tile": 2 * (1 - y) + c}
    other = pl.ds(pl.multiple_of(2 * (1 - y) * width, LANES), 2 * width)
    mine = pl.ds(pl.multiple_of(t * width, LANES), width)
    slab = strip * n_az + az

    def remote(src, dst, send, recv, device):
        return pltpu.make_async_remote_copy(
            src_ref=src, dst_ref=dst, send_sem=send, recv_sem=recv,
            device_id=device, device_id_type=pl.DeviceIdType.MESH,
        )

    def pulse_rows(tile):
        return pl.ds(pl.multiple_of(tile * rows_own, rows_own), rows_own)

    def groups(j):
        return pl.ds(j * chunk, chunk)

    def onward(a):
        return remote(
            raw_ref.at[:, :, lanes(a)], prev.at[a], z_send.at[a], z_recv.at[a],
            {"az": lax.rem(az + 1, n_az)},
        )

    def own_echo(a):
        return pltpu.make_async_copy(
            raw_ref.at[:, :, lanes(a)], cols.at[a, :, pulse_rows(t), :], load_echo.at[a]
        )

    def range_piece(a, first, rows, stride=None):
        row = a % (extent // count) * count + first
        return phase.at[a // (extent // count), pl.ds(row, rows, stride=stride), :]

    def own_range(a):
        return pltpu.make_async_copy(range_ref.at[:, lanes(a)], range_piece(a, 0, count), load_range.at[a])

    def own_phase(source, j, k):
        return pltpu.make_async_copy(source.at[:, lanes(j)], phase.at[j], load.at[k, j])

    def echo_across(j):
        return remote(
            prev.at[j], cols.at[j, :, pulse_rows(t), :], y_send.at[j], y_recv.at[j], across,
        )

    def echo_core(j):
        at = cols.at[groups(j), :, pulse_rows(t), :]
        return remote(at, at, c_send.at[j], c_recv.at[j], partner)

    def echo_forward(j):
        at = cols.at[groups(j), :, pulse_rows(2 * (1 - y) + c), :]
        return remote(at, at, f_send.at[j], f_recv.at[j], partner)

    def scaling_core():
        return remote(dop.at[0, :, pl.ds(0, width)], scal.at[:, mine], s_send, s_recv, partner)

    def scaling_chip(k):
        to = {"tile": 2 * (1 - y) + lax.rem(c + k, 2)}
        return remote(
            for_chip.at[lax.rem(c + k, 2)],
            scal.at[pl.ds(pl.multiple_of(slab * block, block), block), mine],
            p_send.at[k], p_recv.at[k], to,
        )

    def turn_part(ref, base, z, s):
        first = base + (z * n_strip + s) * part
        return ref.at[:, pl.ds(pl.multiple_of(first, part), part), :]

    def scal_rows(g):
        return scal.at[pl.ds(pl.multiple_of(g * block, block), block), other]

    def range_chip():
        return remote(
            turn_part(swap, 0, az, strip), turn_part(turn, y * half, az, strip),
            p_send.at[2], p_recv.at[2], across,
        )

    def slice_of(z, k):
        if k:
            return turn_part(turn, (1 - y) * half, z, strip)
        return scal_rows(strip * n_az + z)

    def up(i, k):
        at = slice_of(az - i, k)
        return remote(at, at, up_send.at[i, k], az_recv.at[az - i, k], {"az": lax.rem(az + 1, n_az)})

    def arrived(z, k):
        at = slice_of(z, k)
        remote(at, at, up_send.at[0, k], az_recv.at[z, k], {"az": lax.rem(az + 1, n_az)}).wait_recv()

    def down(i, k):
        at = slice_of(az + i, k)
        return remote(
            at, at, down_send.at[i, k], az_recv.at[az + i, k], {"az": lax.rem(az + n_az - 1, n_az)}
        )

    def relay(i, k):
        @pl.when(az >= i)
        def _():
            arrived(az - i, k)
            sideways(az - i, k).start()

            @pl.when(az + 1 < n_az)
            def _():
                up(i, k).start()

    def hand_over(d, k):
        @pl.when(az + d < n_az)
        def _():
            arrived(az + d, k)
            sideways(az + d, k).start()

            @pl.when(az > 0)
            def _():
                down(d, k).start()

    def sideways(z, k):
        at = slice_of(z, k)
        return remote(at, at, x_send.at[z, k], x_recv.at[z, k], {"strip": 1 - strip})

    def share(k):
        sideways(az, k).start()

        @pl.when(az > 0)
        def _():
            down(0, k).start()

    def order(n):
        return jnp.where(az + n < n_az, az + n, n_az - 1 - n)

    def place(n):
        s = jnp.where(n < n_az, y, 1 - y)
        z = order(lax.rem(n, n_az))
        base = (s * n_az + z) * block
        row = (2 * s + c) * m + y * half + z * block
        return pl.ds(pl.multiple_of(base, block), block), pl.ds(pl.multiple_of(row, block), block), base, row

    def piece_rows(u):
        _, _, base, row = place(u // steps)
        first = lax.rem(u, steps) * step
        return tuple(pl.ds(pl.multiple_of(x + first, step), step) for x in (base, row))

    def back(u, k):
        to = lax.rem(t + k, tiles)
        src, dst = piece_rows(u)
        at = pl.ds(pl.multiple_of(to * width, LANES), width)
        return remote(
            dop.at[:, src, at], ret.at[:, dst, :], w_send.at[u, k - 1], w_recv.at[u, k - 1], {"tile": to}
        )

    def keep(u):
        src, dst = piece_rows(u)
        return pltpu.make_async_copy(dop.at[:, src, mine], ret.at[:, dst, :], w_local.at[u])

    def back_span(j, n, k):
        to = lax.rem(t + k, tiles)
        src, dst, _, _ = place(n)
        return remote(
            dop.at[:, src, lanes(to * spans + j)], ret.at[:, dst, lanes(j)],
            v_send.at[j, n - whole, k - 1], v_recv.at[j, n - whole, k - 1], {"tile": to},
        )

    def keep_span(j, n):
        src, dst, _, _ = place(n)
        return pltpu.make_async_copy(
            dop.at[:, src, lanes(t * spans + j)], ret.at[:, dst, lanes(j)], v_local.at[j, n - whole]
        )

    def put(j):
        slot = lax.rem(j, 2)
        return pltpu.make_async_copy(head.at[slot], o_ref.at[:, :, lanes(j)], out_sem.at[slot])

    get_front = pltpu.make_async_copy(front_ref.at[y], front, load_front)
    get_tables = [
        pltpu.make_async_copy(source, target, load_table.at[i])
        for i, (source, target) in enumerate(
            (
                (twists_any, twists_ref),
                (fwd_any, fwd_ref),
                (inv_any, inv_ref),
                (range_twist_any, range_twist_ref),
                (table_any, table_ref),
            )
        )
    ]
    barrier = greet(
        [{"tile": lax.rem(t + k, tiles)} for k in range(1, tiles)]
        + [{"strip": 1 - strip}]
    )
    neighbours = ((az + 1, az + 1 < n_az), (az + n_az - 1, az > 0))
    for to, there in neighbours:
        @pl.when(there)
        def _():
            pl.semaphore_signal(
                barrier, inc=1, device_id={"az": lax.rem(to, n_az)}, device_id_type=pl.DeviceIdType.MESH
            )


    @pl.loop(0, spans)
    def _(j):
        own_phase(scaling_ref, j, 0).start()

    @pl.when(az == 0)
    def _():
        @pl.loop(0, n_one)
        def _(a):
            prev[a] = jnp.zeros((2, rows_own, LANES), F32)

    @pl.loop(0, spans)
    def _(j):
        own_phase(scaling_ref, j, 0).wait()
        for k in (0, 1):
            first = (2 * strip + k) * m + 2 * az * block + 1 - y
            for_chip[k, :, lanes(j)] = phase[j, pl.ds(first, block, stride=2), :]

    pl.semaphore_wait(barrier, tiles + sum(there.astype(jnp.int32) for _, there in neighbours))
    for k in (0, 1):
        scaling_chip(k).start()

    @pl.when(az < n_az - 1)
    def _():
        @pl.loop(0, n_one)
        def _(a):
            onward(a).start()

    @pl.loop(0, n_one)
    def _(a):
        own_echo(a).start()

    get_front.start()
    for copy in get_tables:
        copy.start()

    @pl.loop(0, spans)
    def _(j):
        for h in (0, 1):
            rows = pl.ds(h * half, half)
            dop[0, rows, lanes(j)] = phase[j, pl.ds((2 * h + 1 - c) * m + y, half, stride=2), :]
            scal[rows, lanes(t * spans + j)] = phase[j, pl.ds((2 * h + c) * m + y, half, stride=2), :]

    scaling_core().start()

    @pl.loop(0, n_one)
    def _(a):
        own_range(a).start()

    get_tables[0].wait()
    for k in range(6):
        twist_ref[k] = jnp.broadcast_to(twists_ref[:, k : k + 1], (m, LANES))
    for k in (0, 1):
        x = twists_ref[pl.ds(0, half), 6 + k : 7 + k]
        for i in range(1, tiles):
            x = jnp.where(t == i, twists_ref[pl.ds(0, half), 6 + 2 * i + k : 7 + 2 * i + k], x)
        turn_front[k] = jnp.broadcast_to(x, (half, LANES))
    scaling_core().wait_send()
    get_front.wait()
    odd = lax.rem(lax.broadcasted_iota(jnp.int32, (1, pulses), 1), 2) * c
    for k in (0, 1):
        front[k] = (front[k].astype(F32) * (1 - 2 * odd).astype(F32)).astype(BF16)
    sign = (1 - 2 * y).astype(F32)

    @pl.loop(0, chunks + lag + 1)
    def _(j):
        @pl.when(j < chunks)
        def _():
            for i in range(chunk):
                at = j * chunk + i
                own_echo(at).wait()

                @pl.when(az > 0)
                def _():
                    onward(at).wait_recv()

                for k in (0, 1):
                    a = cols[at, k, pulse_rows(t), :]
                    b = prev[at, k] * sign
                    cols[at, k, pulse_rows(t), :] = a + b
                    prev[at, k] = a - b
                echo_across(at).start()
            echo_core(j).start()

        @pl.when(j == 2)
        def _():
            for k in (0, 1):
                scaling_chip(k).wait_recv()
            share(0)

        @pl.when(j == 1)
        def _():
            @pl.loop(0, n_one)
            def _(a):
                own_range(a).wait()

        few = n_one // parts

        @pl.when((j >= 1) & (j < 1 + parts))
        def _():
            i = (j - 1) * few
            turn_in(lambda g: range_piece(g, 1 - y, half, 2)[...], mid, i, i + few)

        @pl.when((j >= 1 + parts) & (j < 1 + 2 * parts))
        def _():
            i = (j - 1 - parts) * few
            turn_out(mid, swap, 0, i, i + few)

        @pl.when((j >= 1 + 2 * parts) & (j < 1 + 3 * parts))
        def _():
            i = (j - 1 - 2 * parts) * few
            turn_in(lambda g: range_piece(g, y, half, 2)[...], mid, i, i + few)

        @pl.when((j >= 1 + 3 * parts) & (j < 1 + 4 * parts))
        def _():
            i = (j - 1 - 3 * parts) * few
            turn_out(mid, turn, y * half, i, i + few)

        @pl.when(j == 1 + 4 * parts)
        def _():
            @pl.loop(0, spans)
            def _(i):
                own_phase(azimuth_ref, i, 1).start()

        @pl.when(j == chunks - 1)
        def _():
            range_chip().start()

            @pl.when(az + 1 < n_az)
            def _():
                up(0, 0).start()

        for d in range(1, n_az):
            @pl.when(j == 2 + chunks * d // n_az)
            def _():
                hand_over(d, 0)

        @pl.when(j > lag)
        def _():
            now = j - lag - 1
            echo_core(now).wait_recv()
            echo_forward(now).wait_recv()
            r = []
            for e in (0, 1):
                rows = pl.ds(e, pulses // 2, stride=2)
                s = jnp.concatenate(
                    [
                        jnp.concatenate([cols[now * chunk + i, k, rows, :] for k in (0, 1)], axis=0)
                        for i in range(chunk)
                    ],
                    axis=1,
                )
                s_hi, s_lo = split(s)
                hi, lo = front[0], front[1]
                x = mm(hi, s_hi) + mm(hi, s_lo) + mm(lo, s_hi)
                r.append((x[:half], x[half:]))
            w = tuple(jnp.concatenate([turn_front[k]] * chunk, axis=1) for k in (0, 1))
            r[1] = times(r[1], w)
            for k in (0, 1):
                a, b = r[0][k], r[1][k]
                at = pl.ds(pl.multiple_of(now * chunk * LANES, LANES), chunk * LANES)
                dop[k, pl.ds(0, half), at] = a + b
                dop[k, pl.ds(half, half), at] = a - b

        @pl.when((j >= lag) & (j < chunks + lag))
        def _():
            for i in range(chunk):
                echo_across((j - lag) * chunk + i).wait_recv()
            echo_forward(j - lag).start()

    relay(1, 0)
    scaling_core().wait_recv()
    for copy in get_tables[1:]:
        copy.wait()

    @pl.loop(0, blocks * steps)
    def _(u):
        for i in range(2, n_az):
            @pl.when(u == steps * (i - 1) - 1)
            def _():
                relay(i, 0)

        @pl.when((lax.rem(u, steps) == 0) & (u < n_az * steps))
        def _():
            sideways(order(u // steps), 0).wait_recv()

        @pl.when(u == 1)
        def _():
            range_chip().wait_recv()
            share(1)

            @pl.when(az + 1 < n_az)
            def _():
                up(0, 1).start()

        for i in range(1, n_az):
            @pl.when(u == steps * (i + 1))
            def _():
                hand_over(i, 1)
                relay(i, 1)

        @pl.when(u == n_az * steps)
        def _():
            for i in range(n_az):
                sideways(order(i), 1).wait_recv()

        filter_block(
            dop, place(u // steps)[2] + lax.rem(u, steps) * step, step,
            scal, fwd_ref, inv_ref, range_twist_ref, turn, hi_ref, lo_ref, mid,
        )

        @pl.when(u < whole * steps)
        def _():
            for k in range(tiles - 1, 0, -1):
                back(u, k).start()
            keep(u).start()

    @pl.loop(0, spans)
    def _(j):
        for n in range(whole, blocks):
            for k in range(tiles - 1, 0, -1):
                back_span(j, n, k).start()
            keep_span(j, n).start()

    @pl.loop(0, spans)
    def _(j):
        own_phase(azimuth_ref, j, 1).wait()

    @pl.loop(0, whole * steps)
    def _(u):
        for k in range(1, tiles):
            back(u, k).wait_recv()
        keep(u).wait()

    @pl.loop(0, spans)
    def _(j):
        for f in range(4):
            angle = jnp.concatenate(
                [phase[j, pl.ds(f * m + p, half, stride=2), :] for p in (0, 1)], axis=0
            )
            spin[0, f], spin[1, f] = sincos(angle)
        for n in range(whole, blocks):
            for k in range(1, tiles):
                back_span(j, n, k).wait_recv()
            keep_span(j, n).wait()
        hi, lo = table_ref[0], table_ref[1]
        slot = lax.rem(j, 2)

        @pl.when(j > 1)
        def _():
            put(j - 2).wait()

        v = []
        for f in range(4):
            rows = pl.ds(f * m, m)
            v.append(times((ret[0, rows, lanes(j)], ret[1, rows, lanes(j)]), (spin[0, f], spin[1, f])))
        for e, x in enumerate(four(v, 1)):
            if e:
                x = times(x, (twist_ref[2 * e - 2], twist_ref[2 * e - 1]))
            s_hi, s_lo = split(jnp.concatenate(x, axis=0))
            r = mm(hi, s_hi) + mm(hi, s_lo) + mm(lo, s_hi)
            for k in (0, 1):
                head[slot, k, pl.ds(e, q, stride=4), :] = r[k * q : (k + 1) * q]
        put(j).start()

    for j in range(max(0, spans - 2), spans):
        put(j).wait()

    @pl.when(az < n_az - 1)
    def _():
        @pl.loop(0, n_one)
        def _(a):
            onward(a).wait_send()

    @pl.loop(0, chunks)
    def _(j):
        for i in range(chunk):
            echo_across(j * chunk + i).wait_send()
        echo_core(j).wait_send()
        echo_forward(j).wait_send()

    range_chip().wait_send()
    for k in (0, 1):
        scaling_chip(k).wait_send()
        for d in range(1, n_az):
            @pl.when((az > 0) & (az + d - 1 < n_az))
            def _():
                down(d - 1, k).wait_send()

            @pl.when((az + 1 < n_az) & (az >= d - 1))
            def _():
                up(d - 1, k).wait_send()
        for z in range(n_az):
            sideways(z, k).wait_send()

    @pl.loop(0, whole * steps)
    def _(u):
        for k in range(1, tiles):
            back(u, k).wait_send()

    @pl.loop(0, spans)
    def _(j):
        for n in range(whole, blocks):
            for k in range(1, tiles):
                back_span(j, n, k).wait_send()


def pair_body(raw_echo, phase_scaling, phase_range, phase_azimuth):
    tiles = lax.axis_size("tile")
    n_az, n_strip = lax.axis_size("az"), lax.axis_size("strip")
    pulses = raw_echo.shape[1] * tiles
    extent, width = phase_scaling.shape
    count, ranges = phase_range.shape
    m, q, half = extent // 4, pulses // 4, count // 2
    n_one, spans = ranges // LANES, width // LANES
    blocks = n_strip * n_az
    block = count // blocks
    chunk = 2
    chunks = n_one // chunk
    whole = blocks - 2
    rest = blocks - whole
    fine = np.concatenate([np.arange(0, m, 2), np.arange(1, m, 2)])
    lane = np.arange(LANES)
    vmem = pl.BlockSpec(memory_space=pltpu.VMEM)
    anyspace = pl.BlockSpec(memory_space=pl.ANY)
    dma = pltpu.SemaphoreType.DMA
    c, s = roots(np.arange(n_one), lane, ranges, -1)
    return pl.pallas_call(
        functools.partial(pair_kernel, n_strip, n_az, block, chunk),
        out_shape=pltpu.VMEM((2, pulses, width), F32),
        in_specs=[anyspace] * 10,
        out_specs=vmem,
        scratch_shapes=[
            pltpu.VMEM((m, LANES), F32),
            pltpu.VMEM((2, 2 * LANES, 2 * LANES), BF16),
            pltpu.VMEM((2, 2 * LANES, 2 * LANES), BF16),
            pltpu.VMEM((2, n_one, LANES), F32),
            pltpu.VMEM((2, 2 * q, 2 * m), BF16),
            pltpu.VMEM((n_one, 2, pulses, LANES), F32),
            pltpu.VMEM((n_one, 2, pulses // tiles, LANES), F32),
            pltpu.VMEM((2, count, ranges), F32),
            pltpu.VMEM((count, ranges), F32),
            pltpu.VMEM((n_one, half, LANES), F32),
            pltpu.VMEM((n_one, count, LANES), F32),
            pltpu.VMEM((spans, extent, LANES), F32),
            pltpu.VMEM((2, extent, width), F32),
            pltpu.VMEM((2, block, width), F32),
            pltpu.VMEM((2, count, pulses), BF16),
            pltpu.VMEM((2, half, LANES), F32),
            pltpu.VMEM((6, m, LANES), F32),
            pltpu.VMEM((2, 4, m, LANES), F32),
            pltpu.VMEM((2, 2, pulses, LANES), F32),
            pltpu.VMEM((n_one, block // 2, 2 * LANES), BF16),
            pltpu.VMEM((n_one, block // 2, 2 * LANES), BF16),
            pltpu.VMEM((2, n_one * LANES // 2, LANES), F32),
            dma((2, spans)), dma((n_one,)), dma((n_one,)), dma, dma((5,)),
            dma((n_one,)), dma((n_one,)),
            dma((n_one,)), dma((n_one,)),
            dma((chunks,)), dma((chunks,)),
            dma((chunks,)), dma((chunks,)),
            dma, dma,
            dma((3,)), dma((3,)),
            dma((n_az, 2)), dma((n_az, 2)), dma((n_az, 2)),
            dma((n_az, 2)), dma((n_az, 2)),
            dma((2 * whole, tiles - 1)), dma((2 * whole, tiles - 1)), dma((2 * whole,)),
            dma((spans, rest, tiles - 1)), dma((spans, rest, tiles - 1)), dma((spans, rest)),
            dma((2,)),
        ],
        compiler_params=pltpu.CompilerParams(
            collective_id=0, has_side_effects=True, vmem_limit_bytes=59 << 20
        ),
    )(
        raw_echo,
        phase_scaling,
        phase_range,
        phase_azimuth,
        pair_front(extent, pulses),
        pair_twists(extent, fine),
        right_table(lane, lane, LANES, -1),
        right_table(lane, lane, LANES, 1, 1.0 / ranges),
        np.stack([c, s]).astype(np.float32),
        left_table(np.arange(q), fine, m, 1, 1.0 / extent),
    )


def paired(raw_echo, phase_scaling, phase_range):
    tiles, n_az, n_strip = (lax.axis_size(a) for a in ("tile", "az", "strip"))
    count = phase_range.shape[0]
    blocks = n_az * n_strip
    return (
        tiles == 4
        and n_strip == 2
        and n_az > 1
        and count == 2 * LANES
        and phase_scaling.shape[0] == 2 * raw_echo.shape[1] * tiles
        and count % (32 * blocks) == 0
        and phase_range.shape[1] % (8 * LANES) == 0
    )


def body(raw_echo, phase_scaling, phase_range, phase_azimuth):
    plan = pair_body if paired(raw_echo, phase_scaling, phase_range) else tail_body
    return plan(raw_echo, phase_scaling, phase_range, phase_azimuth)


def solution(mesh):
    return jax.shard_map(
        body,
        mesh=mesh,
        in_specs=(
            P(None, ("strip", "az", "tile"), None),
            P(None, "tile"),
            P("tile", None),
            P(None, "tile"),
        ),
        out_specs=P(None, ("strip", "az"), "tile"),
        check_vma=False,
    )
```

```python
import functools
import math

import jax
import jax.numpy as jnp
import numpy as np
from jax import lax
from jax.experimental import pallas as pl
from jax.experimental.pallas import tpu as pltpu
from jax.sharding import PartitionSpec as P

F32 = jnp.float32
BF16 = jnp.bfloat16
LANES = 128


def halves(table):
    hi = np.asarray(table, np.float32).astype(jnp.bfloat16)
    lo = (np.asarray(table, np.float64) - hi.astype(np.float64)).astype(jnp.bfloat16)
    return np.stack([hi, lo])


def roots(rows, cols, modulus, direction):
    residue = np.outer(rows, cols) % modulus
    angle = residue * (direction * 2.0 * math.pi / modulus)
    return np.cos(angle), np.sin(angle)


def left_table(rows, cols, modulus, direction, scale=1.0):
    c, s = roots(rows, cols, modulus, direction)
    return halves(np.block([[c, -s], [s, c]]) * scale)


def right_table(rows, cols, modulus, direction, scale=1.0):
    c, s = roots(rows, cols, modulus, direction)
    return halves(np.block([[c, s], [-s, c]]) * scale)


def twist_table(count, length, modulus, direction):
    c, s = roots(np.arange(count), np.arange(length), modulus, direction)
    full = np.stack([c, s]).astype(np.float32)
    return np.ascontiguousarray(np.broadcast_to(full[..., None], full.shape + (LANES,)))


def split(x):
    hi = x.astype(BF16)
    return hi, (x - hi.astype(F32)).astype(BF16)


def mm(a, b):
    return jnp.dot(a, b, preferred_element_type=F32)


def times(a, t):
    return a[0] * t[0] - a[1] * t[1], a[0] * t[1] + a[1] * t[0]


def plus(a, b):
    return a[0] + b[0], a[1] + b[1]


def minus(a, b):
    return a[0] - b[0], a[1] - b[1]


def quarter(a, direction):
    return (-a[1], a[0]) if direction > 0 else (a[1], -a[0])


def four(v, direction):
    a, b = plus(v[0], v[2]), minus(v[0], v[2])
    c, d = plus(v[1], v[3]), quarter(minus(v[1], v[3]), direction)
    return [plus(a, c), plus(b, d), minus(a, c), minus(b, d)]


def fft(v, direction):
    n = len(v)
    if n == 1:
        return v
    if n == 2:
        return [plus(v[0], v[1]), minus(v[0], v[1])]
    if n == 4:
        return four(v, direction)
    parts = [fft(v[e::4], direction) for e in range(4)] if n % 4 == 0 else None
    out = [None] * n
    m = n // 4
    for f in range(m):
        items = []
        for e in range(4):
            x = parts[e][f]
            k = e * f % n
            if k == 0:
                pass
            elif 8 * k == n:
                h = np.float32(math.sqrt(0.5))
                q = quarter(x, direction)
                x = ((x[0] + q[0]) * h, (x[1] + q[1]) * h)
            elif 4 * k == n:
                x = quarter(x, direction)
            elif 8 * k == 3 * n:
                h = np.float32(math.sqrt(0.5))
                q = quarter(x, direction)
                x = ((q[0] - x[0]) * h, (q[1] - x[1]) * h)
            else:
                ang = direction * 2.0 * math.pi * k / n
                x = times(x, (np.float32(math.cos(ang)), np.float32(math.sin(ang))))
            items.append(x)
        got = four(items, direction)
        for j in range(4):
            out[f + j * m] = got[j]
    return out


def sincos(x):
    y = x * 0.5
    z = y * y
    s, c = -1.0 / 39916800, 1.0 / 479001600
    for a, b in ((362880, -3628800), (-5040, 40320), (120, -720), (-6, 24), (1, -2)):
        s = s * z + np.float32(1.0 / a)
        c = c * z + np.float32(1.0 / b)
    s = s * y
    c = c * z + 1.0
    return 1.0 - 2.0 * s * s, 2.0 * s * c


def greet(partners):
    barrier = pltpu.get_barrier_semaphore()
    for device in partners:
        pl.semaphore_signal(barrier, inc=1, device_id=device, device_id_type=pl.DeviceIdType.MESH)
    return barrier


def lanes(j):
    return pl.ds(pl.multiple_of(j * LANES, LANES), LANES)


def filter_rows(x_ref, base, block, fwd_ref, inv_ref, twist_ref, phase_ref, hi_ref, lo_ref, mid_ref):
    n_one = phase_ref.shape[0]
    step = 16
    f_hi, f_lo = fwd_ref[0], fwd_ref[1]
    b_hi, b_lo = inv_ref[0], inv_ref[1]

    @pl.loop(0, block // step)
    def _(i):
        rows = pl.ds(pl.multiple_of(i * step, step), step)
        at = pl.ds(pl.multiple_of(base + i * step, step), step)
        v = [
            tuple(x_ref[c, at, pl.ds(a * LANES, LANES)] for c in (0, 1))
            for a in range(n_one)
        ]
        for k, x in enumerate(fft(v, -1)):
            if k:
                x = times(x, (twist_ref[0, k : k + 1, :], twist_ref[1, k : k + 1, :]))
            for c in (0, 1):
                h, l = split(x[c])
                hi_ref[k, rows, pl.ds(c * LANES, LANES)] = h
                lo_ref[k, rows, pl.ds(c * LANES, LANES)] = l

    group = 4

    @pl.loop(0, n_one // group)
    def _(i):
        ks = pl.ds(i * group, group)
        flat = (group * block, 2 * LANES)
        h, l = hi_ref[ks].reshape(flat), lo_ref[ks].reshape(flat)
        r = mm(h, f_hi) + mm(l, f_hi) + mm(h, f_lo)
        turn = phase_ref[ks, pl.ds(pl.multiple_of(base, block), block), :]
        r = times((r[:, :LANES], r[:, LANES:]), sincos(turn.reshape(group * block, LANES)))
        h, l = split(jnp.concatenate(r, axis=1))
        r = mm(h, b_hi) + mm(l, b_hi) + mm(h, b_lo)
        at = pl.ds(pl.multiple_of(i * group * block, block), group * block)
        mid_ref[0, at, :] = r[:, :LANES]
        mid_ref[1, at, :] = r[:, LANES:]

    @pl.loop(0, block // 8)
    def _(i):
        at = pl.ds(pl.multiple_of(base + i * 8, 8), 8)
        v = []
        for k in range(n_one):
            x = tuple(mid_ref[c, pl.ds(pl.multiple_of(k * block + i * 8, 8), 8), :] for c in (0, 1))
            if k:
                x = times(x, (twist_ref[0, k : k + 1, :], -twist_ref[1, k : k + 1, :]))
            v.append(x)
        for a, x in enumerate(fft(v, 1)):
            for c in (0, 1):
                x_ref[c, at, pl.ds(a * LANES, LANES)] = x[c]


def permute_turn(o_ref, mid, turn):
    n_one, count, _ = turn.shape
    half = mid.shape[1]
    some = min(count, LANES)
    part = half // n_one

    @pl.loop(0, count // some)
    def _(i):
        @pl.loop(0, n_one)
        def _(g):
            c, row, j = piece(g, count, o_ref)
            at = pl.ds(pl.multiple_of(row + i * some, some), some)
            x = o_ref[c, at, lanes(j)]
            if some < LANES:
                x = jnp.concatenate([x] * (LANES // some), axis=0)
            per = half // LANES
            mid[g // per, pl.ds(pl.multiple_of(g % per * LANES, LANES), LANES), :] = x.T

        @pl.loop(0, n_one)
        def _(k):
            rows = pl.ds(k, part, stride=n_one)
            x = jnp.concatenate([mid[h, rows, :] for h in range(LANES // part)], axis=0)
            at = pl.ds(pl.multiple_of(i * some, some), some)
            turn[k, at, :] = x.T[:some]


def piece(g, count, o_ref):
    across = o_ref.shape[2] // LANES
    down = o_ref.shape[1] // count
    return g // (across * down), g // across % down * count, g % across


def focus_kernel(
    tiles, length, block,
    raw_ref, scaling_ref, range_ref, azimuth_ref,
    front_ref, twist_ref, fwd_ref, inv_ref, range_twist_ref, table_ref,
    o_ref,
    spec, scaling, turn, phase, dop, ret, tail_out, tail_in, head, hi_ref, lo_ref, mid,
    send_e, recv_e, local_e, send_a, recv_a, local_a, send_b, recv_b, local_b,
    send_c, recv_c, load, load_range,
):
    me = lax.axis_index("tile")
    az = lax.axis_index("az")
    count = dop.shape[1]
    width = o_ref.shape[2]
    pulses = o_ref.shape[1]
    tail = tail_in.shape[2]
    rows_own = raw_ref.shape[1]
    n_one = turn.shape[0]
    blocks = count // block
    early = (blocks - 1) * block
    spans = width // LANES
    cols = tail_out
    m = spec.shape[1] // 4
    q = pulses // 4
    mine = pl.ds(pl.multiple_of(me * width, LANES), width)
    own = pl.ds(pl.multiple_of(me * count, count), count)
    own_pulses = pl.ds(pl.multiple_of(me * rows_own, rows_own), rows_own)

    def remote(src, dst, send, recv, device):
        return pltpu.make_async_remote_copy(
            src_ref=src, dst_ref=dst, send_sem=send, recv_sem=recv,
            device_id=device, device_id_type=pl.DeviceIdType.MESH,
        )

    def echo(j, k):
        to = lax.rem(me + k, tiles)
        return remote(
            raw_ref.at[:, :, lanes(to * spans + j)], cols.at[j, :, own_pulses, :],
            send_e.at[j, k - 1], recv_e.at[j, k - 1], {"tile": to},
        )

    def keep_echo(j):
        return pltpu.make_async_copy(
            raw_ref.at[:, :, lanes(me * spans + j)], cols.at[j, :, own_pulses, :], local_e.at[j]
        )

    def load_piece(g):
        c, row, j = piece(g, count, o_ref)
        return pltpu.make_async_copy(
            range_ref.at[:, lanes(g)],
            o_ref.at[c, pl.ds(pl.multiple_of(row, count), count), lanes(j)],
            load_range.at[g],
        )

    def out_part(i, k, lo, n, slot):
        to = lax.rem(me + k, tiles)
        at = pl.ds(pl.multiple_of(me * width + lo, LANES), n)
        return remote(
            spec.at[:, pl.ds(pl.multiple_of(to * count + i * block, block), block), pl.ds(lo, n)],
            dop.at[:, pl.ds(pl.multiple_of(i * block, block), block), at],
            send_a.at[slot, k - 1], recv_a.at[slot, k - 1], {"tile": to},
        )

    def out(i, k):
        return out_part(i, k, 0, width, i)

    def first_out(k):
        return out_part(0, k, 0, width - LANES, blocks)

    def last_out(k):
        return out_part(0, k, width - LANES, LANES, 0)

    def back_rows(j, k, lo, n, slot):
        to = lax.rem(me + k, tiles)
        return remote(
            dop.at[:, pl.ds(lo, n), lanes(to * spans + j)],
            ret.at[j, :, pl.ds(pl.multiple_of(me * count + lo, 8), n), :],
            send_b.at[slot, k - 1], recv_b.at[slot, k - 1], {"tile": to},
        )

    def first_rows(k):
        return back_rows(0, k, 0, early, spans)

    def last_rows(k):
        return back_rows(0, k, early, count - early, 0)

    def back(j, k):
        return back_rows(j, k, 0, count, j)

    def keep(j):
        return pltpu.make_async_copy(
            dop.at[:, :, lanes(me * spans + j)], ret.at[j, :, own, :], local_b.at[j]
        )

    def onward(j):
        return remote(
            tail_out.at[j, :, pl.ds(0, tail), :], tail_in.at[j], send_c.at[j], recv_c.at[j],
            {"az": lax.rem(az + 1, length)},
        )

    barrier = greet(
        [{"tile": lax.rem(me + k, tiles)} for k in range(1, tiles)]
        + [{"az": lax.rem(az + 1, length)}, {"az": lax.rem(az + length - 1, length)}]
    )
    get_scaling = pltpu.make_async_copy(scaling_ref, scaling, load.at[0])
    get_phase = pltpu.make_async_copy(azimuth_ref, phase, load.at[1])
    pl.semaphore_wait(barrier, tiles + 1)

    @pl.loop(0, spans)
    def _(j):
        for k in range(1, tiles):
            echo(j, k).start()
        keep_echo(j).start()

    @pl.loop(0, n_one)
    def _(g):
        load_piece(g).start()

    get_scaling.start()
    get_phase.start()

    get_scaling.wait()

    @pl.loop(0, spans)
    def _(j):
        @pl.when(j == spans - 1)
        def _():
            for k in range(1, tiles):
                first_out(k).start()

        for k in range(1, tiles):
            echo(j, k).wait_recv()
        keep_echo(j).wait()
        hi, lo = front_ref[0], front_ref[1]
        z = []
        for e in range(4):
            rows = pl.ds(e, q, stride=4)
            s = jnp.concatenate([cols[j, 0, rows, :], cols[j, 1, rows, :]], axis=0)
            s_hi, s_lo = split(s)
            r = mm(hi, s_hi) + mm(hi, s_lo) + mm(lo, s_hi)
            r = (r[:m], r[m:])
            if e:
                r = times(r, (twist_ref[0, e], -twist_ref[1, e]))
            z.append(r)
        for f, x in enumerate(four(z, -1)):
            rows = pl.ds(f * m, m)
            x = times(x, sincos(scaling[rows, lanes(j)]))
            spec[0, rows, lanes(j)] = x[0]
            spec[1, rows, lanes(j)] = x[1]

    for k in range(1, tiles):
        last_out(k).start()

    @pl.loop(1, blocks)
    def _(i):
        for k in range(1, tiles):
            out(i, k).start()

    first = pltpu.make_async_copy(spec.at[:, own, :], dop.at[:, :, mine], local_a)
    first.start()

    @pl.loop(0, n_one)
    def _(g):
        load_piece(g).wait()

    permute_turn(o_ref, mid, turn)
    first.wait()

    @pl.loop(0, blocks)
    def _(i):
        if early:
            @pl.when(i == blocks - 1)
            def _():
                for k in range(1, tiles):
                    first_rows(k).start()

        @pl.when(i == 0)
        def _():
            for k in range(1, tiles):
                first_out(k).wait_recv()
                last_out(k).wait_recv()

        @pl.when(i > 0)
        def _():
            for k in range(1, tiles):
                out(i, k).wait_recv()

        filter_rows(
            dop, i * block, block, fwd_ref, inv_ref, range_twist_ref, turn,
            hi_ref, lo_ref, mid,
        )

    for k in range(1, tiles):
        last_rows(k).start()
    keep(0).start()

    @pl.loop(1, spans)
    def _(j):
        for k in range(1, tiles):
            back(j, k).start()
        keep(j).start()

    get_phase.wait()

    @pl.loop(0, spans)
    def _(j):
        @pl.when(j == 0)
        def _():
            for k in range(1, tiles):
                if early:
                    first_rows(k).wait_recv()
                last_rows(k).wait_recv()

        @pl.when(j > 0)
        def _():
            for k in range(1, tiles):
                back(j, k).wait_recv()

        keep(j).wait()
        hi, lo = table_ref[0], table_ref[1]
        v = []
        for f in range(4):
            rows = pl.ds(f * m, m)
            v.append(times((ret[j, 0, rows, :], ret[j, 1, rows, :]), sincos(phase[rows, lanes(j)])))
        for e, x in enumerate(four(v, 1)):
            if e:
                x = times(x, (twist_ref[0, e], twist_ref[1, e]))
            s_hi, s_lo = split(jnp.concatenate(x, axis=0))
            r = mm(hi, s_hi) + mm(hi, s_lo) + mm(lo, s_hi)
            for c in (0, 1):
                head[c, pl.ds(e, q, stride=4), :] = r[c * m : c * m + q]
                tail_out[j, c, pl.ds(e, m - q, stride=4), :] = r[c * m + q : (c + 1) * m]

        @pl.when(az < length - 1)
        def _():
            onward(j).start()

        o_ref[:, :, lanes(j)] = head[...]

    @pl.when(az > 0)
    def _():
        @pl.loop(0, spans)
        def _(j):
            onward(j).wait_recv()
            o_ref[:, pl.ds(0, tail), lanes(j)] += tail_in[j]

    for k in range(1, tiles):
        first_out(k).wait_send()
        last_out(k).wait_send()

    @pl.loop(1, blocks)
    def _(i):
        for k in range(1, tiles):
            out(i, k).wait_send()

    for k in range(1, tiles):
        if early:
            first_rows(k).wait_send()
        last_rows(k).wait_send()

    @pl.loop(1, spans)
    def _(j):
        for k in range(1, tiles):
            back(j, k).wait_send()

    @pl.loop(0, spans)
    def _(j):
        for k in range(1, tiles):
            echo(j, k).wait_send()

    @pl.when(az < length - 1)
    def _():
        @pl.loop(0, spans)
        def _(j):
            onward(j).wait_send()


def tail_body(raw_echo, phase_scaling, phase_range, phase_azimuth):
    tiles = lax.axis_size("tile")
    length = lax.axis_size("az")
    pulses = raw_echo.shape[1] * tiles
    extent, width = phase_scaling.shape
    count, ranges = phase_range.shape
    m, q, tail = extent // 4, pulses // 4, extent - pulses
    n_one, spans = ranges // LANES, width // LANES
    block = min(64, count)
    rows, lane = np.arange(m), np.arange(LANES)
    vmem = pl.BlockSpec(memory_space=pltpu.VMEM)
    anyspace = pl.BlockSpec(memory_space=pl.ANY)
    dma = pltpu.SemaphoreType.DMA
    c, s = roots(np.arange(n_one), lane, ranges, -1)
    return pl.pallas_call(
        functools.partial(focus_kernel, tiles, length, block),
        out_shape=jax.ShapeDtypeStruct((2, pulses, width), F32),
        in_specs=[anyspace] * 4 + [vmem] * 6,
        out_specs=vmem,
        scratch_shapes=[
            pltpu.VMEM((2, extent, width), F32),
            pltpu.VMEM((extent, width), F32),
            pltpu.VMEM((n_one, count, LANES), F32),
            pltpu.VMEM((extent, width), F32),
            pltpu.VMEM((2, count, ranges), F32),
            pltpu.VMEM((spans, 2, extent, LANES), F32),
            pltpu.VMEM((spans, 2, max(tail, pulses), LANES), F32),
            pltpu.VMEM((spans, 2, tail, LANES), F32),
            pltpu.VMEM((2, pulses, LANES), F32),
            pltpu.VMEM((n_one, block, 2 * LANES), BF16),
            pltpu.VMEM((n_one, block, 2 * LANES), BF16),
            pltpu.VMEM((2, n_one * block, LANES), F32),
            dma((spans, tiles - 1)),
            dma((spans, tiles - 1)),
            dma((spans,)),
            dma((count // block + 1, tiles - 1)),
            dma((count // block + 1, tiles - 1)),
            dma,
            dma((spans + 1, tiles - 1)),
            dma((spans + 1, tiles - 1)),
            dma((spans,)),
            dma((spans,)),
            dma((spans,)),
            dma((2,)),
            dma((n_one,)),
        ],
        compiler_params=pltpu.CompilerParams(
            collective_id=0, has_side_effects=True, vmem_limit_bytes=63 << 20
        ),
    )(
        raw_echo,
        phase_scaling,
        phase_range,
        phase_azimuth,
        left_table(rows, np.arange(q), m, -1),
        twist_table(4, m, extent, 1),
        right_table(lane, lane, LANES, -1),
        right_table(lane, lane, LANES, 1, 1.0 / ranges),
        np.stack([c, s]).astype(np.float32),
        left_table(rows, rows, m, 1, 1.0 / extent),
    )


def pair_front(extent, pulses):
    m = extent // 4
    return np.stack(
        [left_table(2 * np.arange(m // 2) + y, 2 * np.arange(pulses // 2), extent, -1) for y in (0, 1)]
    )


def pair_twists(extent, fine):
    m = extent // 4
    out = np.zeros((m, LANES), np.float32)
    for e in range(1, 4):
        c, s = roots(fine, [e], extent, 1)
        out[:, 2 * e - 2 : 2 * e - 1], out[:, 2 * e - 1 : 2 * e] = c, s
    for t in range(4):
        c, s = roots(2 * np.arange(m // 2) + t // 2 + m * (t % 2), [1], extent, -1)
        out[: m // 2, 6 + 2 * t : 7 + 2 * t], out[: m // 2, 7 + 2 * t : 8 + 2 * t] = c, s
    return out


def filter_block(
    x_ref, base, block, scal_ref, fwd_ref, inv_ref, twist_ref, phase_ref, hi_ref, lo_ref, mid_ref
):
    n_one = phase_ref.shape[0]
    step = 16
    group = max(1, 256 // block)
    f_hi, f_lo = fwd_ref[0], fwd_ref[1]
    b_hi, b_lo = inv_ref[0], inv_ref[1]
    whole = pl.ds(pl.multiple_of(base, block), block)

    wide = 8 * LANES

    @pl.loop(0, n_one * LANES // wide)
    def _(a):
        at = pl.ds(pl.multiple_of(a * wide, wide), wide)
        x = times((x_ref[0, whole, at], x_ref[1, whole, at]), sincos(scal_ref[whole, at]))
        x_ref[0, whole, at] = x[0]
        x_ref[1, whole, at] = x[1]

    @pl.loop(0, block // step)
    def _(i):
        rows = pl.ds(pl.multiple_of(i * step, step), step)
        at = pl.ds(pl.multiple_of(base + i * step, step), step)
        v = [
            tuple(x_ref[c, at, pl.ds(a * LANES, LANES)] for c in (0, 1))
            for a in range(n_one)
        ]
        for k, x in enumerate(fft(v, -1)):
            if k:
                x = times(x, (twist_ref[0, k : k + 1, :], twist_ref[1, k : k + 1, :]))
            for c in (0, 1):
                h, l = split(x[c])
                hi_ref[k, rows, pl.ds(c * LANES, LANES)] = h
                lo_ref[k, rows, pl.ds(c * LANES, LANES)] = l

    @pl.loop(0, n_one // group)
    def _(i):
        ks = pl.ds(i * group, group)
        flat = (group * block, 2 * LANES)
        h, l = hi_ref[ks].reshape(flat), lo_ref[ks].reshape(flat)
        r = mm(h, f_hi) + mm(l, f_hi) + mm(h, f_lo)
        turn = phase_ref[ks, whole, :]
        r = times((r[:, :LANES], r[:, LANES:]), sincos(turn.reshape(group * block, LANES)))
        h, l = split(jnp.concatenate(r, axis=1))
        r = mm(h, b_hi) + mm(l, b_hi) + mm(h, b_lo)
        at = pl.ds(pl.multiple_of(i * group * block, block), group * block)
        mid_ref[0, at, :] = r[:, :LANES]
        mid_ref[1, at, :] = r[:, LANES:]

    @pl.loop(0, block // 8)
    def _(i):
        at = pl.ds(pl.multiple_of(base + i * 8, 8), 8)
        v = []
        for k in range(n_one):
            x = tuple(mid_ref[c, pl.ds(pl.multiple_of(k * block + i * 8, 8), 8), :] for c in (0, 1))
            if k:
                x = times(x, (twist_ref[0, k : k + 1, :], -twist_ref[1, k : k + 1, :]))
            v.append(x)
        for a, x in enumerate(fft(v, 1)):
            for c in (0, 1):
                x_ref[c, at, pl.ds(a * LANES, LANES)] = x[c]


def turn_in(load, mid, start, stop):
    per = mid.shape[1] // LANES

    @pl.loop(start, stop)
    def _(g):
        mid[g // per, pl.ds(pl.multiple_of(g % per * LANES, LANES), LANES), :] = load(g).T


def turn_out(mid, turn, base, start, stop):
    n_one = turn.shape[0]
    part = mid.shape[1] // n_one
    at = pl.ds(pl.multiple_of(base, LANES), LANES)

    @pl.loop(start, stop)
    def _(k):
        rows = pl.ds(k, part, stride=n_one)
        x = jnp.concatenate([mid[h, rows, :] for h in range(LANES // part)], axis=0)
        turn[k, at, :] = x.T


def pair_kernel(
    n_strip, n_az, block, chunk,
    raw_ref, scaling_ref, range_ref, azimuth_ref, front_ref,
    twists_any, fwd_any, inv_any, range_twist_any, table_any,
    o_ref,
    twists_ref, fwd_ref, inv_ref, range_twist_ref, table_ref,
    cols, prev, dop, scal, swap, turn, phase, ret, for_chip,
    front, turn_front, twist_ref, spin, head, hi_ref, lo_ref, mid,
    load, load_range, load_echo, load_front, load_table, z_send, z_recv, y_send, y_recv, c_send, c_recv, f_send, f_recv,
    s_send, s_recv, p_send, p_recv, down_send, up_send, az_recv, swap_send, swap_recv, x_send, x_recv,
    w_send, w_recv, w_local, v_send, v_recv, v_local,
):
    t = lax.axis_index("tile")
    az = lax.axis_index("az")
    strip = lax.axis_index("strip")
    y, c = t // 2, t % 2
    tiles = 4
    count, ranges = range_ref.shape
    half = count // 2
    extent, width = scaling_ref.shape
    m = extent // 4
    pulses = o_ref.shape[1]
    q = pulses // 4
    rows_own = raw_ref.shape[1]
    spans = width // LANES
    n_one = ranges // LANES
    chunks = n_one // chunk
    blocks = count // block
    part = half // blocks
    parts = chunks // 4
    whole = blocks - 2
    lag, steps = 2, 2
    step = block // steps
    partner, across = {"tile": 2 * y + 1 - c}, {"tile": 2 * (1 - y) + c}
    other = pl.ds(pl.multiple_of(2 * (1 - y) * width, LANES), 2 * width)
    mine = pl.ds(pl.multiple_of(t * width, LANES), width)
    slab = strip * n_az + az

    def remote(src, dst, send, recv, device):
        return pltpu.make_async_remote_copy(
            src_ref=src, dst_ref=dst, send_sem=send, recv_sem=recv,
            device_id=device, device_id_type=pl.DeviceIdType.MESH,
        )

    def pulse_rows(tile):
        return pl.ds(pl.multiple_of(tile * rows_own, rows_own), rows_own)

    def groups(j):
        return pl.ds(j * chunk, chunk)

    def onward(a):
        return remote(
            raw_ref.at[:, :, lanes(a)], prev.at[a], z_send.at[a], z_recv.at[a],
            {"az": lax.rem(az + 1, n_az)},
        )

    def own_echo(a):
        return pltpu.make_async_copy(
            raw_ref.at[:, :, lanes(a)], cols.at[a, :, pulse_rows(t), :], load_echo.at[a]
        )

    def range_piece(a, first, rows, stride=None):
        row = a % (extent // count) * count + first
        return phase.at[a // (extent // count), pl.ds(row, rows, stride=stride), :]

    def own_range(a):
        return pltpu.make_async_copy(range_ref.at[:, lanes(a)], range_piece(a, 0, count), load_range.at[a])

    def own_phase(source, j, k):
        return pltpu.make_async_copy(source.at[:, lanes(j)], phase.at[j], load.at[k, j])

    def echo_across(j):
        return remote(
            prev.at[j], cols.at[j, :, pulse_rows(t), :], y_send.at[j], y_recv.at[j], across,
        )

    def echo_core(j):
        at = cols.at[groups(j), :, pulse_rows(t), :]
        return remote(at, at, c_send.at[j], c_recv.at[j], partner)

    def echo_forward(j):
        at = cols.at[groups(j), :, pulse_rows(2 * (1 - y) + c), :]
        return remote(at, at, f_send.at[j], f_recv.at[j], partner)

    def scaling_core():
        return remote(dop.at[0, :, pl.ds(0, width)], scal.at[:, mine], s_send, s_recv, partner)

    def scaling_chip(k):
        to = {"tile": 2 * (1 - y) + lax.rem(c + k, 2)}
        return remote(
            for_chip.at[lax.rem(c + k, 2)],
            scal.at[pl.ds(pl.multiple_of(slab * block, block), block), mine],
            p_send.at[k], p_recv.at[k], to,
        )

    def turn_part(ref, base, z, s):
        first = base + (z * n_strip + s) * part
        return ref.at[:, pl.ds(pl.multiple_of(first, part), part), :]

    def scal_rows(g):
        return scal.at[pl.ds(pl.multiple_of(g * block, block), block), other]

    def range_chip():
        return remote(
            turn_part(swap, 0, az, strip), turn_part(turn, y * half, az, strip),
            p_send.at[2], p_recv.at[2], across,
        )

    def slice_of(z, k):
        if k == 1:
            return turn_part(turn, (1 - y) * half, z, strip)
        return scal_rows((y if k == 0 else 1 - y) * n_az + z)

    def swap_scaling():
        at = scal_rows(slab)
        return remote(at, at, swap_send, swap_recv, {"strip": 1 - strip})

    def up(i, k):
        at = slice_of(az - i, k)
        return remote(at, at, up_send.at[i, k], az_recv.at[az - i, k], {"az": lax.rem(az + 1, n_az)})

    def arrived(z, k):
        at = slice_of(z, k)
        remote(at, at, up_send.at[0, k], az_recv.at[z, k], {"az": lax.rem(az + 1, n_az)}).wait_recv()

    def down(i, k):
        at = slice_of(az + i, k)
        return remote(
            at, at, down_send.at[i, k], az_recv.at[az + i, k], {"az": lax.rem(az + n_az - 1, n_az)}
        )

    def relay(i, k):
        @pl.when(az >= i)
        def _():
            arrived(az - i, k)
            if k == 1:
                sideways(az - i).start()

            @pl.when(az + 1 < n_az)
            def _():
                up(i, k).start()

    def hand_over(d, k):
        @pl.when(az + d < n_az)
        def _():
            arrived(az + d, k)
            if k == 1:
                sideways(az + d).start()

            @pl.when(az > 0)
            def _():
                down(d, k).start()

    def sideways(z):
        at = slice_of(z, 1)
        return remote(at, at, x_send.at[z], x_recv.at[z], {"strip": 1 - strip})

    def order(n):
        return jnp.where(az + n < n_az, az + n, n_az - 1 - n)

    def place(n):
        s = jnp.where(n < n_az, y, 1 - y)
        z = order(lax.rem(n, n_az))
        base = (s * n_az + z) * block
        row = (2 * s + c) * m + y * half + z * block
        return pl.ds(pl.multiple_of(base, block), block), pl.ds(pl.multiple_of(row, block), block), base, row

    def piece_rows(u):
        _, _, base, row = place(u // steps)
        first = lax.rem(u, steps) * step
        return tuple(pl.ds(pl.multiple_of(x + first, step), step) for x in (base, row))

    def back(u, k):
        to = lax.rem(t + k, tiles)
        src, dst = piece_rows(u)
        at = pl.ds(pl.multiple_of(to * width, LANES), width)
        return remote(
            dop.at[:, src, at], ret.at[:, dst, :], w_send.at[u, k - 1], w_recv.at[u, k - 1], {"tile": to}
        )

    def keep(u):
        src, dst = piece_rows(u)
        return pltpu.make_async_copy(dop.at[:, src, mine], ret.at[:, dst, :], w_local.at[u])

    def back_span(j, n, k):
        to = lax.rem(t + k, tiles)
        src, dst, _, _ = place(n)
        return remote(
            dop.at[:, src, lanes(to * spans + j)], ret.at[:, dst, lanes(j)],
            v_send.at[j, n - whole, k - 1], v_recv.at[j, n - whole, k - 1], {"tile": to},
        )

    def keep_span(j, n):
        src, dst, _, _ = place(n)
        return pltpu.make_async_copy(
            dop.at[:, src, lanes(t * spans + j)], ret.at[:, dst, lanes(j)], v_local.at[j, n - whole]
        )

    get_front = pltpu.make_async_copy(front_ref.at[y], front, load_front)
    get_tables = [
        pltpu.make_async_copy(source, target, load_table.at[i])
        for i, (source, target) in enumerate(
            (
                (twists_any, twists_ref),
                (fwd_any, fwd_ref),
                (inv_any, inv_ref),
                (range_twist_any, range_twist_ref),
                (table_any, table_ref),
            )
        )
    ]
    barrier = greet(
        [{"tile": lax.rem(t + k, tiles)} for k in range(1, tiles)]
        + [{"strip": 1 - strip}]
    )
    neighbours = ((az + 1, az + 1 < n_az), (az + n_az - 1, az > 0))
    for to, there in neighbours:
        @pl.when(there)
        def _():
            pl.semaphore_signal(
                barrier, inc=1, device_id={"az": lax.rem(to, n_az)}, device_id_type=pl.DeviceIdType.MESH
            )


    @pl.loop(0, spans)
    def _(j):
        own_phase(scaling_ref, j, 0).start()

    @pl.when(az == 0)
    def _():
        @pl.loop(0, n_one)
        def _(a):
            prev[a] = jnp.zeros((2, rows_own, LANES), F32)

    @pl.loop(0, spans)
    def _(j):
        own_phase(scaling_ref, j, 0).wait()
        for k in (0, 1):
            first = (2 * strip + k) * m + 2 * az * block + 1 - y
            for_chip[k, :, lanes(j)] = phase[j, pl.ds(first, block, stride=2), :]

    pl.semaphore_wait(barrier, tiles + sum(there.astype(jnp.int32) for _, there in neighbours))
    for k in (0, 1):
        scaling_chip(k).start()

    @pl.when(az < n_az - 1)
    def _():
        @pl.loop(0, n_one)
        def _(a):
            onward(a).start()

    @pl.loop(0, n_one)
    def _(a):
        own_echo(a).start()

    get_front.start()
    for copy in get_tables:
        copy.start()

    sign = (1 - 2 * y).astype(F32)

    @pl.loop(0, chunks + lag + 1)
    def _(j):
        @pl.when(j < chunks)
        def _():
            for i in range(chunk):
                at = j * chunk + i
                own_echo(at).wait()

                @pl.when(az > 0)
                def _():
                    onward(at).wait_recv()

                for k in (0, 1):
                    a = cols[at, k, pulse_rows(t), :]
                    b = prev[at, k] * sign
                    cols[at, k, pulse_rows(t), :] = a + b
                    prev[at, k] = a - b
                echo_across(at).start()
            echo_core(j).start()

        @pl.when(j == 0)
        def _():
            @pl.loop(0, spans)
            def _(i):
                for h in (0, 1):
                    rows = pl.ds(h * half, half)
                    dop[0, rows, lanes(i)] = phase[i, pl.ds((2 * h + 1 - c) * m + y, half, stride=2), :]
                    scal[rows, lanes(t * spans + i)] = phase[i, pl.ds((2 * h + c) * m + y, half, stride=2), :]

            scaling_core().start()

            @pl.loop(0, n_one)
            def _(a):
                own_range(a).start()

            get_tables[0].wait()
            for k in range(6):
                twist_ref[k] = jnp.broadcast_to(twists_ref[:, k : k + 1], (m, LANES))
            for k in (0, 1):
                x = twists_ref[pl.ds(0, half), 6 + k : 7 + k]
                for i in range(1, tiles):
                    x = jnp.where(t == i, twists_ref[pl.ds(0, half), 6 + 2 * i + k : 7 + 2 * i + k], x)
                turn_front[k] = jnp.broadcast_to(x, (half, LANES))

        @pl.when(j == 1)
        def _():
            scaling_core().wait_send()
            get_front.wait()
            odd = lax.rem(lax.broadcasted_iota(jnp.int32, (1, pulses), 1), 2) * c
            for k in (0, 1):
                front[k] = (front[k].astype(F32) * (1 - 2 * odd).astype(F32)).astype(BF16)

        @pl.when(j == 2)
        def _():
            for k in (0, 1):
                scaling_chip(k).wait_recv()
            swap_scaling().start()

        @pl.when(j == 4)
        def _():
            swap_scaling().wait_recv()

            @pl.when(az > 0)
            def _():
                for k in (0, 2):
                    down(0, k).start()

        @pl.when(j == 1)
        def _():
            @pl.loop(0, n_one)
            def _(a):
                own_range(a).wait()

        few = n_one // parts

        @pl.when((j >= 1) & (j < 1 + parts))
        def _():
            i = (j - 1) * few
            turn_in(lambda g: range_piece(g, 1 - y, half, 2)[...], mid, i, i + few)

        @pl.when((j >= 1 + parts) & (j < 1 + 2 * parts))
        def _():
            i = (j - 1 - parts) * few
            turn_out(mid, swap, 0, i, i + few)

        @pl.when((j >= 1 + 2 * parts) & (j < 1 + 3 * parts))
        def _():
            i = (j - 1 - 2 * parts) * few
            turn_in(lambda g: range_piece(g, y, half, 2)[...], mid, i, i + few)

        @pl.when((j >= 1 + 3 * parts) & (j < 1 + 4 * parts))
        def _():
            i = (j - 1 - 3 * parts) * few
            turn_out(mid, turn, y * half, i, i + few)

        @pl.when(j == 1 + 4 * parts)
        def _():
            @pl.loop(0, spans)
            def _(i):
                own_phase(azimuth_ref, i, 1).start()

        @pl.when(j == chunks - 1)
        def _():
            range_chip().start()

            @pl.when(az + 1 < n_az)
            def _():
                up(0, 0).start()

        for d in range(1, n_az):
            for k in (0, 2):
                @pl.when(j == 2 + chunks * d // n_az + k // 2)
                def _():
                    hand_over(d, k)

        @pl.when(j > lag)
        def _():
            now = j - lag - 1
            echo_core(now).wait_recv()
            echo_forward(now).wait_recv()
            r = []
            for e in (0, 1):
                rows = pl.ds(e, pulses // 2, stride=2)
                s = jnp.concatenate(
                    [
                        jnp.concatenate([cols[now * chunk + i, k, rows, :] for k in (0, 1)], axis=0)
                        for i in range(chunk)
                    ],
                    axis=1,
                )
                s_hi, s_lo = split(s)
                hi, lo = front[0], front[1]
                x = mm(hi, s_hi) + mm(hi, s_lo) + mm(lo, s_hi)
                r.append((x[:half], x[half:]))
            w = tuple(jnp.concatenate([turn_front[k]] * chunk, axis=1) for k in (0, 1))
            r[1] = times(r[1], w)
            for k in (0, 1):
                a, b = r[0][k], r[1][k]
                at = pl.ds(pl.multiple_of(now * chunk * LANES, LANES), chunk * LANES)
                dop[k, pl.ds(0, half), at] = a + b
                dop[k, pl.ds(half, half), at] = a - b

        @pl.when((j >= lag) & (j < chunks + lag))
        def _():
            for i in range(chunk):
                echo_across((j - lag) * chunk + i).wait_recv()
            echo_forward(j - lag).start()

    relay(1, 0)
    scaling_core().wait_recv()
    for copy in get_tables[1:]:
        copy.wait()

    @pl.loop(0, blocks * steps)
    def _(u):
        @pl.when(u == 1)
        def _():
            range_chip().wait_recv()
            sideways(az).start()

            @pl.when(az > 0)
            def _():
                down(0, 1).start()

            @pl.when(az + 1 < n_az)
            def _():
                up(0, 1).start()
                up(0, 2).start()

        for i in range(2, n_az):
            @pl.when(u == steps * i)
            def _():
                relay(i, 0)

        for i in range(1, n_az):
            @pl.when(u == steps * (i + 1))
            def _():
                hand_over(i, 1)
                relay(i, 1)

            @pl.when(u == steps * (n_az + i - 1))
            def _():
                relay(i, 2)

        @pl.when(u == n_az * steps)
        def _():
            for i in range(n_az):
                sideways(order(i)).wait_recv()

        filter_block(
            dop, place(u // steps)[2] + lax.rem(u, steps) * step, step,
            scal, fwd_ref, inv_ref, range_twist_ref, turn, hi_ref, lo_ref, mid,
        )

        @pl.when(u < whole * steps)
        def _():
            for k in range(tiles - 1, 0, -1):
                back(u, k).start()
            keep(u).start()

    @pl.loop(0, spans)
    def _(j):
        for n in range(whole, blocks):
            for k in range(tiles - 1, 0, -1):
                back_span(j, n, k).start()
            keep_span(j, n).start()

    @pl.loop(0, spans)
    def _(j):
        own_phase(azimuth_ref, j, 1).wait()

    @pl.loop(0, whole * steps)
    def _(u):
        for k in range(1, tiles):
            back(u, k).wait_recv()
        keep(u).wait()

    @pl.loop(0, spans)
    def _(j):
        for f in range(4):
            angle = jnp.concatenate(
                [phase[j, pl.ds(f * m + p, half, stride=2), :] for p in (0, 1)], axis=0
            )
            spin[0, f], spin[1, f] = sincos(angle)
        for n in range(whole, blocks):
            for k in range(1, tiles):
                back_span(j, n, k).wait_recv()
            keep_span(j, n).wait()
        hi, lo = table_ref[0], table_ref[1]
        v = []
        for f in range(4):
            rows = pl.ds(f * m, m)
            v.append(times((ret[0, rows, lanes(j)], ret[1, rows, lanes(j)]), (spin[0, f], spin[1, f])))
        for e, x in enumerate(four(v, 1)):
            if e:
                x = times(x, (twist_ref[2 * e - 2], twist_ref[2 * e - 1]))
            s_hi, s_lo = split(jnp.concatenate(x, axis=0))
            r = mm(hi, s_hi) + mm(hi, s_lo) + mm(lo, s_hi)
            for k in (0, 1):
                head[k, pl.ds(e, q, stride=4), :] = r[k * q : (k + 1) * q]
        o_ref[:, :, lanes(j)] = head[...]

    @pl.when(az < n_az - 1)
    def _():
        @pl.loop(0, n_one)
        def _(a):
            onward(a).wait_send()

    @pl.loop(0, chunks)
    def _(j):
        for i in range(chunk):
            echo_across(j * chunk + i).wait_send()
        echo_core(j).wait_send()
        echo_forward(j).wait_send()

    range_chip().wait_send()
    for k in (0, 1):
        scaling_chip(k).wait_send()
    swap_scaling().wait_send()
    for z in range(n_az):
        sideways(z).wait_send()
    for k in (0, 1, 2):
        for d in range(n_az - 1):
            @pl.when((az > 0) & (az + d < n_az))
            def _():
                down(d, k).wait_send()

            @pl.when((az + 1 < n_az) & (az >= d))
            def _():
                up(d, k).wait_send()

    @pl.loop(0, whole * steps)
    def _(u):
        for k in range(1, tiles):
            back(u, k).wait_send()

    @pl.loop(0, spans)
    def _(j):
        for n in range(whole, blocks):
            for k in range(1, tiles):
                back_span(j, n, k).wait_send()


def pair_body(raw_echo, phase_scaling, phase_range, phase_azimuth):
    tiles = lax.axis_size("tile")
    n_az, n_strip = lax.axis_size("az"), lax.axis_size("strip")
    pulses = raw_echo.shape[1] * tiles
    extent, width = phase_scaling.shape
    count, ranges = phase_range.shape
    m, q, half = extent // 4, pulses // 4, count // 2
    n_one, spans = ranges // LANES, width // LANES
    blocks = n_strip * n_az
    block = count // blocks
    chunk = 2
    chunks = n_one // chunk
    whole = blocks - 2
    rest = blocks - whole
    fine = np.concatenate([np.arange(0, m, 2), np.arange(1, m, 2)])
    lane = np.arange(LANES)
    vmem = pl.BlockSpec(memory_space=pltpu.VMEM)
    anyspace = pl.BlockSpec(memory_space=pl.ANY)
    dma = pltpu.SemaphoreType.DMA
    c, s = roots(np.arange(n_one), lane, ranges, -1)
    return pl.pallas_call(
        functools.partial(pair_kernel, n_strip, n_az, block, chunk),
        out_shape=pltpu.VMEM((2, pulses, width), F32),
        in_specs=[anyspace] * 10,
        out_specs=vmem,
        scratch_shapes=[
            pltpu.VMEM((m, LANES), F32),
            pltpu.VMEM((2, 2 * LANES, 2 * LANES), BF16),
            pltpu.VMEM((2, 2 * LANES, 2 * LANES), BF16),
            pltpu.VMEM((2, n_one, LANES), F32),
            pltpu.VMEM((2, 2 * q, 2 * m), BF16),
            pltpu.VMEM((n_one, 2, pulses, LANES), F32),
            pltpu.VMEM((n_one, 2, pulses // tiles, LANES), F32),
            pltpu.VMEM((2, count, ranges), F32),
            pltpu.VMEM((count, ranges), F32),
            pltpu.VMEM((n_one, half, LANES), F32),
            pltpu.VMEM((n_one, count, LANES), F32),
            pltpu.VMEM((spans, extent, LANES), F32),
            pltpu.VMEM((2, extent, width), F32),
            pltpu.VMEM((2, block, width), F32),
            pltpu.VMEM((2, count, pulses), BF16),
            pltpu.VMEM((2, half, LANES), F32),
            pltpu.VMEM((6, m, LANES), F32),
            pltpu.VMEM((2, 4, m, LANES), F32),
            pltpu.VMEM((2, pulses, LANES), F32),
            pltpu.VMEM((n_one, block // 2, 2 * LANES), BF16),
            pltpu.VMEM((n_one, block // 2, 2 * LANES), BF16),
            pltpu.VMEM((2, n_one * LANES // 2, LANES), F32),
            dma((2, spans)), dma((n_one,)), dma((n_one,)), dma, dma((5,)),
            dma((n_one,)), dma((n_one,)),
            dma((n_one,)), dma((n_one,)),
            dma((chunks,)), dma((chunks,)),
            dma((chunks,)), dma((chunks,)),
            dma, dma,
            dma((3,)), dma((3,)),
            dma((n_az, 3)), dma((n_az, 3)), dma((n_az, 3)),
            dma, dma,
            dma((n_az,)), dma((n_az,)),
            dma((2 * whole, tiles - 1)), dma((2 * whole, tiles - 1)), dma((2 * whole,)),
            dma((spans, rest, tiles - 1)), dma((spans, rest, tiles - 1)), dma((spans, rest)),
        ],
        compiler_params=pltpu.CompilerParams(
            collective_id=0, has_side_effects=True, vmem_limit_bytes=59 << 20
        ),
    )(
        raw_echo,
        phase_scaling,
        phase_range,
        phase_azimuth,
        pair_front(extent, pulses),
        pair_twists(extent, fine),
        right_table(lane, lane, LANES, -1),
        right_table(lane, lane, LANES, 1, 1.0 / ranges),
        np.stack([c, s]).astype(np.float32),
        left_table(np.arange(q), fine, m, 1, 1.0 / extent),
    )


def paired(raw_echo, phase_scaling, phase_range):
    tiles, n_az, n_strip = (lax.axis_size(a) for a in ("tile", "az", "strip"))
    count = phase_range.shape[0]
    blocks = n_az * n_strip
    return (
        tiles == 4
        and n_strip == 2
        and n_az > 1
        and count == 2 * LANES
        and phase_scaling.shape[0] == 2 * raw_echo.shape[1] * tiles
        and count % (32 * blocks) == 0
        and phase_range.shape[1] % (8 * LANES) == 0
    )


def body(raw_echo, phase_scaling, phase_range, phase_azimuth):
    plan = pair_body if paired(raw_echo, phase_scaling, phase_range) else tail_body
    return plan(raw_echo, phase_scaling, phase_range, phase_azimuth)


def solution(mesh):
    return jax.shard_map(
        body,
        mesh=mesh,
        in_specs=(
            P(None, ("strip", "az", "tile"), None),
            P(None, "tile"),
            P("tile", None),
            P(None, "tile"),
        ),
        out_specs=P(None, ("strip", "az"), "tile"),
        check_vma=False,
    )
```

```python
import functools
import math

import jax
import jax.numpy as jnp
import numpy as np
from jax import lax
from jax.experimental import pallas as pl
from jax.experimental.pallas import tpu as pltpu
from jax.sharding import PartitionSpec as P

F32 = jnp.float32
BF16 = jnp.bfloat16
LANES = 128


def halves(table):
    hi = np.asarray(table, np.float32).astype(jnp.bfloat16)
    lo = (np.asarray(table, np.float64) - hi.astype(np.float64)).astype(jnp.bfloat16)
    return np.stack([hi, lo])


def roots(rows, cols, modulus, direction):
    residue = np.outer(rows, cols) % modulus
    angle = residue * (direction * 2.0 * math.pi / modulus)
    return np.cos(angle), np.sin(angle)


def left_table(rows, cols, modulus, direction, scale=1.0):
    c, s = roots(rows, cols, modulus, direction)
    return halves(np.block([[c, -s], [s, c]]) * scale)


def right_table(rows, cols, modulus, direction, scale=1.0):
    c, s = roots(rows, cols, modulus, direction)
    return halves(np.block([[c, s], [-s, c]]) * scale)


def twist_table(count, length, modulus, direction):
    c, s = roots(np.arange(count), np.arange(length), modulus, direction)
    full = np.stack([c, s]).astype(np.float32)
    return np.ascontiguousarray(np.broadcast_to(full[..., None], full.shape + (LANES,)))


def split(x):
    hi = x.astype(BF16)
    return hi, (x - hi.astype(F32)).astype(BF16)


def mm(a, b):
    return jnp.dot(a, b, preferred_element_type=F32)


def times(a, t):
    return a[0] * t[0] - a[1] * t[1], a[0] * t[1] + a[1] * t[0]


def plus(a, b):
    return a[0] + b[0], a[1] + b[1]


def minus(a, b):
    return a[0] - b[0], a[1] - b[1]


def quarter(a, direction):
    return (-a[1], a[0]) if direction > 0 else (a[1], -a[0])


def four(v, direction):
    a, b = plus(v[0], v[2]), minus(v[0], v[2])
    c, d = plus(v[1], v[3]), quarter(minus(v[1], v[3]), direction)
    return [plus(a, c), plus(b, d), minus(a, c), minus(b, d)]


def fft(v, direction):
    n = len(v)
    if n == 1:
        return v
    if n == 2:
        return [plus(v[0], v[1]), minus(v[0], v[1])]
    if n == 4:
        return four(v, direction)
    parts = [fft(v[e::4], direction) for e in range(4)] if n % 4 == 0 else None
    out = [None] * n
    m = n // 4
    for f in range(m):
        items = []
        for e in range(4):
            x = parts[e][f]
            k = e * f % n
            if k == 0:
                pass
            elif 8 * k == n:
                h = np.float32(math.sqrt(0.5))
                q = quarter(x, direction)
                x = ((x[0] + q[0]) * h, (x[1] + q[1]) * h)
            elif 4 * k == n:
                x = quarter(x, direction)
            elif 8 * k == 3 * n:
                h = np.float32(math.sqrt(0.5))
                q = quarter(x, direction)
                x = ((q[0] - x[0]) * h, (q[1] - x[1]) * h)
            else:
                ang = direction * 2.0 * math.pi * k / n
                x = times(x, (np.float32(math.cos(ang)), np.float32(math.sin(ang))))
            items.append(x)
        got = four(items, direction)
        for j in range(4):
            out[f + j * m] = got[j]
    return out


def sincos(x):
    y = x * 0.5
    z = y * y
    s, c = -1.0 / 39916800, 1.0 / 479001600
    for a, b in ((362880, -3628800), (-5040, 40320), (120, -720), (-6, 24), (1, -2)):
        s = s * z + np.float32(1.0 / a)
        c = c * z + np.float32(1.0 / b)
    s = s * y
    c = c * z + 1.0
    return 1.0 - 2.0 * s * s, 2.0 * s * c


def greet(partners):
    barrier = pltpu.get_barrier_semaphore()
    for device in partners:
        pl.semaphore_signal(barrier, inc=1, device_id=device, device_id_type=pl.DeviceIdType.MESH)
    return barrier


def lanes(j):
    return pl.ds(pl.multiple_of(j * LANES, LANES), LANES)


def filter_rows(x_ref, base, block, fwd_ref, inv_ref, twist_ref, phase_ref, hi_ref, lo_ref, mid_ref):
    n_one = phase_ref.shape[0]
    step = 16
    f_hi, f_lo = fwd_ref[0], fwd_ref[1]
    b_hi, b_lo = inv_ref[0], inv_ref[1]

    @pl.loop(0, block // step)
    def _(i):
        rows = pl.ds(pl.multiple_of(i * step, step), step)
        at = pl.ds(pl.multiple_of(base + i * step, step), step)
        v = [
            tuple(x_ref[c, at, pl.ds(a * LANES, LANES)] for c in (0, 1))
            for a in range(n_one)
        ]
        for k, x in enumerate(fft(v, -1)):
            if k:
                x = times(x, (twist_ref[0, k : k + 1, :], twist_ref[1, k : k + 1, :]))
            for c in (0, 1):
                h, l = split(x[c])
                hi_ref[k, rows, pl.ds(c * LANES, LANES)] = h
                lo_ref[k, rows, pl.ds(c * LANES, LANES)] = l

    group = 4

    @pl.loop(0, n_one // group)
    def _(i):
        ks = pl.ds(i * group, group)
        flat = (group * block, 2 * LANES)
        h, l = hi_ref[ks].reshape(flat), lo_ref[ks].reshape(flat)
        r = mm(h, f_hi) + mm(l, f_hi) + mm(h, f_lo)
        turn = phase_ref[ks, pl.ds(pl.multiple_of(base, block), block), :]
        r = times((r[:, :LANES], r[:, LANES:]), sincos(turn.reshape(group * block, LANES)))
        h, l = split(jnp.concatenate(r, axis=1))
        r = mm(h, b_hi) + mm(l, b_hi) + mm(h, b_lo)
        at = pl.ds(pl.multiple_of(i * group * block, block), group * block)
        mid_ref[0, at, :] = r[:, :LANES]
        mid_ref[1, at, :] = r[:, LANES:]

    @pl.loop(0, block // 8)
    def _(i):
        at = pl.ds(pl.multiple_of(base + i * 8, 8), 8)
        v = []
        for k in range(n_one):
            x = tuple(mid_ref[c, pl.ds(pl.multiple_of(k * block + i * 8, 8), 8), :] for c in (0, 1))
            if k:
                x = times(x, (twist_ref[0, k : k + 1, :], -twist_ref[1, k : k + 1, :]))
            v.append(x)
        for a, x in enumerate(fft(v, 1)):
            for c in (0, 1):
                x_ref[c, at, pl.ds(a * LANES, LANES)] = x[c]


def permute_turn(o_ref, mid, turn):
    n_one, count, _ = turn.shape
    half = mid.shape[1]
    some = min(count, LANES)
    part = half // n_one

    @pl.loop(0, count // some)
    def _(i):
        @pl.loop(0, n_one)
        def _(g):
            c, row, j = piece(g, count, o_ref)
            at = pl.ds(pl.multiple_of(row + i * some, some), some)
            x = o_ref[c, at, lanes(j)]
            if some < LANES:
                x = jnp.concatenate([x] * (LANES // some), axis=0)
            per = half // LANES
            mid[g // per, pl.ds(pl.multiple_of(g % per * LANES, LANES), LANES), :] = x.T

        @pl.loop(0, n_one)
        def _(k):
            rows = pl.ds(k, part, stride=n_one)
            x = jnp.concatenate([mid[h, rows, :] for h in range(LANES // part)], axis=0)
            at = pl.ds(pl.multiple_of(i * some, some), some)
            turn[k, at, :] = x.T[:some]


def piece(g, count, o_ref):
    across = o_ref.shape[2] // LANES
    down = o_ref.shape[1] // count
    return g // (across * down), g // across % down * count, g % across


def focus_kernel(
    tiles, length, block,
    raw_ref, scaling_ref, range_ref, azimuth_ref,
    front_ref, twist_ref, fwd_ref, inv_ref, range_twist_ref, table_ref,
    o_ref,
    spec, scaling, turn, phase, dop, ret, tail_out, tail_in, head, hi_ref, lo_ref, mid,
    send_e, recv_e, local_e, send_a, recv_a, local_a, send_b, recv_b, local_b,
    send_c, recv_c, load, load_range,
):
    me = lax.axis_index("tile")
    az = lax.axis_index("az")
    count = dop.shape[1]
    width = o_ref.shape[2]
    pulses = o_ref.shape[1]
    tail = tail_in.shape[2]
    rows_own = raw_ref.shape[1]
    n_one = turn.shape[0]
    blocks = count // block
    early = (blocks - 1) * block
    spans = width // LANES
    cols = tail_out
    m = spec.shape[1] // 4
    q = pulses // 4
    mine = pl.ds(pl.multiple_of(me * width, LANES), width)
    own = pl.ds(pl.multiple_of(me * count, count), count)
    own_pulses = pl.ds(pl.multiple_of(me * rows_own, rows_own), rows_own)

    def remote(src, dst, send, recv, device):
        return pltpu.make_async_remote_copy(
            src_ref=src, dst_ref=dst, send_sem=send, recv_sem=recv,
            device_id=device, device_id_type=pl.DeviceIdType.MESH,
        )

    def echo(j, k):
        to = lax.rem(me + k, tiles)
        return remote(
            raw_ref.at[:, :, lanes(to * spans + j)], cols.at[j, :, own_pulses, :],
            send_e.at[j, k - 1], recv_e.at[j, k - 1], {"tile": to},
        )

    def keep_echo(j):
        return pltpu.make_async_copy(
            raw_ref.at[:, :, lanes(me * spans + j)], cols.at[j, :, own_pulses, :], local_e.at[j]
        )

    def load_piece(g):
        c, row, j = piece(g, count, o_ref)
        return pltpu.make_async_copy(
            range_ref.at[:, lanes(g)],
            o_ref.at[c, pl.ds(pl.multiple_of(row, count), count), lanes(j)],
            load_range.at[g],
        )

    def out_part(i, k, lo, n, slot):
        to = lax.rem(me + k, tiles)
        at = pl.ds(pl.multiple_of(me * width + lo, LANES), n)
        return remote(
            spec.at[:, pl.ds(pl.multiple_of(to * count + i * block, block), block), pl.ds(lo, n)],
            dop.at[:, pl.ds(pl.multiple_of(i * block, block), block), at],
            send_a.at[slot, k - 1], recv_a.at[slot, k - 1], {"tile": to},
        )

    def out(i, k):
        return out_part(i, k, 0, width, i)

    def first_out(k):
        return out_part(0, k, 0, width - LANES, blocks)

    def last_out(k):
        return out_part(0, k, width - LANES, LANES, 0)

    def back_rows(j, k, lo, n, slot):
        to = lax.rem(me + k, tiles)
        return remote(
            dop.at[:, pl.ds(lo, n), lanes(to * spans + j)],
            ret.at[j, :, pl.ds(pl.multiple_of(me * count + lo, 8), n), :],
            send_b.at[slot, k - 1], recv_b.at[slot, k - 1], {"tile": to},
        )

    def first_rows(k):
        return back_rows(0, k, 0, early, spans)

    def last_rows(k):
        return back_rows(0, k, early, count - early, 0)

    def back(j, k):
        return back_rows(j, k, 0, count, j)

    def keep(j):
        return pltpu.make_async_copy(
            dop.at[:, :, lanes(me * spans + j)], ret.at[j, :, own, :], local_b.at[j]
        )

    def onward(j):
        return remote(
            tail_out.at[j, :, pl.ds(0, tail), :], tail_in.at[j], send_c.at[j], recv_c.at[j],
            {"az": lax.rem(az + 1, length)},
        )

    barrier = greet(
        [{"tile": lax.rem(me + k, tiles)} for k in range(1, tiles)]
        + [{"az": lax.rem(az + 1, length)}, {"az": lax.rem(az + length - 1, length)}]
    )
    get_scaling = pltpu.make_async_copy(scaling_ref, scaling, load.at[0])
    get_phase = pltpu.make_async_copy(azimuth_ref, phase, load.at[1])
    pl.semaphore_wait(barrier, tiles + 1)

    @pl.loop(0, spans)
    def _(j):
        for k in range(1, tiles):
            echo(j, k).start()
        keep_echo(j).start()

    @pl.loop(0, n_one)
    def _(g):
        load_piece(g).start()

    get_scaling.start()
    get_phase.start()

    get_scaling.wait()

    @pl.loop(0, spans)
    def _(j):
        @pl.when(j == spans - 1)
        def _():
            for k in range(1, tiles):
                first_out(k).start()

        for k in range(1, tiles):
            echo(j, k).wait_recv()
        keep_echo(j).wait()
        hi, lo = front_ref[0], front_ref[1]
        z = []
        for e in range(4):
            rows = pl.ds(e, q, stride=4)
            s = jnp.concatenate([cols[j, 0, rows, :], cols[j, 1, rows, :]], axis=0)
            s_hi, s_lo = split(s)
            r = mm(hi, s_hi) + mm(hi, s_lo) + mm(lo, s_hi)
            r = (r[:m], r[m:])
            if e:
                r = times(r, (twist_ref[0, e], -twist_ref[1, e]))
            z.append(r)
        for f, x in enumerate(four(z, -1)):
            rows = pl.ds(f * m, m)
            x = times(x, sincos(scaling[rows, lanes(j)]))
            spec[0, rows, lanes(j)] = x[0]
            spec[1, rows, lanes(j)] = x[1]

    for k in range(1, tiles):
        last_out(k).start()

    @pl.loop(1, blocks)
    def _(i):
        for k in range(1, tiles):
            out(i, k).start()

    first = pltpu.make_async_copy(spec.at[:, own, :], dop.at[:, :, mine], local_a)
    first.start()

    @pl.loop(0, n_one)
    def _(g):
        load_piece(g).wait()

    permute_turn(o_ref, mid, turn)
    first.wait()

    @pl.loop(0, blocks)
    def _(i):
        if early:
            @pl.when(i == blocks - 1)
            def _():
                for k in range(1, tiles):
                    first_rows(k).start()

        @pl.when(i == 0)
        def _():
            for k in range(1, tiles):
                first_out(k).wait_recv()
                last_out(k).wait_recv()

        @pl.when(i > 0)
        def _():
            for k in range(1, tiles):
                out(i, k).wait_recv()

        filter_rows(
            dop, i * block, block, fwd_ref, inv_ref, range_twist_ref, turn,
            hi_ref, lo_ref, mid,
        )

    for k in range(1, tiles):
        last_rows(k).start()
    keep(0).start()

    @pl.loop(1, spans)
    def _(j):
        for k in range(1, tiles):
            back(j, k).start()
        keep(j).start()

    get_phase.wait()

    @pl.loop(0, spans)
    def _(j):
        @pl.when(j == 0)
        def _():
            for k in range(1, tiles):
                if early:
                    first_rows(k).wait_recv()
                last_rows(k).wait_recv()

        @pl.when(j > 0)
        def _():
            for k in range(1, tiles):
                back(j, k).wait_recv()

        keep(j).wait()
        hi, lo = table_ref[0], table_ref[1]
        v = []
        for f in range(4):
            rows = pl.ds(f * m, m)
            v.append(times((ret[j, 0, rows, :], ret[j, 1, rows, :]), sincos(phase[rows, lanes(j)])))
        for e, x in enumerate(four(v, 1)):
            if e:
                x = times(x, (twist_ref[0, e], twist_ref[1, e]))
            s_hi, s_lo = split(jnp.concatenate(x, axis=0))
            r = mm(hi, s_hi) + mm(hi, s_lo) + mm(lo, s_hi)
            for c in (0, 1):
                head[c, pl.ds(e, q, stride=4), :] = r[c * m : c * m + q]
                tail_out[j, c, pl.ds(e, m - q, stride=4), :] = r[c * m + q : (c + 1) * m]

        @pl.when(az < length - 1)
        def _():
            onward(j).start()

        o_ref[:, :, lanes(j)] = head[...]

    @pl.when(az > 0)
    def _():
        @pl.loop(0, spans)
        def _(j):
            onward(j).wait_recv()
            o_ref[:, pl.ds(0, tail), lanes(j)] += tail_in[j]

    for k in range(1, tiles):
        first_out(k).wait_send()
        last_out(k).wait_send()

    @pl.loop(1, blocks)
    def _(i):
        for k in range(1, tiles):
            out(i, k).wait_send()

    for k in range(1, tiles):
        if early:
            first_rows(k).wait_send()
        last_rows(k).wait_send()

    @pl.loop(1, spans)
    def _(j):
        for k in range(1, tiles):
            back(j, k).wait_send()

    @pl.loop(0, spans)
    def _(j):
        for k in range(1, tiles):
            echo(j, k).wait_send()

    @pl.when(az < length - 1)
    def _():
        @pl.loop(0, spans)
        def _(j):
            onward(j).wait_send()


def tail_body(raw_echo, phase_scaling, phase_range, phase_azimuth):
    tiles = lax.axis_size("tile")
    length = lax.axis_size("az")
    pulses = raw_echo.shape[1] * tiles
    extent, width = phase_scaling.shape
    count, ranges = phase_range.shape
    m, q, tail = extent // 4, pulses // 4, extent - pulses
    n_one, spans = ranges // LANES, width // LANES
    block = min(64, count)
    rows, lane = np.arange(m), np.arange(LANES)
    vmem = pl.BlockSpec(memory_space=pltpu.VMEM)
    anyspace = pl.BlockSpec(memory_space=pl.ANY)
    dma = pltpu.SemaphoreType.DMA
    c, s = roots(np.arange(n_one), lane, ranges, -1)
    return pl.pallas_call(
        functools.partial(focus_kernel, tiles, length, block),
        out_shape=jax.ShapeDtypeStruct((2, pulses, width), F32),
        in_specs=[anyspace] * 4 + [vmem] * 6,
        out_specs=vmem,
        scratch_shapes=[
            pltpu.VMEM((2, extent, width), F32),
            pltpu.VMEM((extent, width), F32),
            pltpu.VMEM((n_one, count, LANES), F32),
            pltpu.VMEM((extent, width), F32),
            pltpu.VMEM((2, count, ranges), F32),
            pltpu.VMEM((spans, 2, extent, LANES), F32),
            pltpu.VMEM((spans, 2, max(tail, pulses), LANES), F32),
            pltpu.VMEM((spans, 2, tail, LANES), F32),
            pltpu.VMEM((2, pulses, LANES), F32),
            pltpu.VMEM((n_one, block, 2 * LANES), BF16),
            pltpu.VMEM((n_one, block, 2 * LANES), BF16),
            pltpu.VMEM((2, n_one * block, LANES), F32),
            dma((spans, tiles - 1)),
            dma((spans, tiles - 1)),
            dma((spans,)),
            dma((count // block + 1, tiles - 1)),
            dma((count // block + 1, tiles - 1)),
            dma,
            dma((spans + 1, tiles - 1)),
            dma((spans + 1, tiles - 1)),
            dma((spans,)),
            dma((spans,)),
            dma((spans,)),
            dma((2,)),
            dma((n_one,)),
        ],
        compiler_params=pltpu.CompilerParams(
            collective_id=0, has_side_effects=True, vmem_limit_bytes=63 << 20
        ),
    )(
        raw_echo,
        phase_scaling,
        phase_range,
        phase_azimuth,
        left_table(rows, np.arange(q), m, -1),
        twist_table(4, m, extent, 1),
        right_table(lane, lane, LANES, -1),
        right_table(lane, lane, LANES, 1, 1.0 / ranges),
        np.stack([c, s]).astype(np.float32),
        left_table(rows, rows, m, 1, 1.0 / extent),
    )


def pair_front(extent, pulses):
    m = extent // 4
    return np.stack(
        [left_table(2 * np.arange(m // 2) + y, 2 * np.arange(pulses // 2), extent, -1) for y in (0, 1)]
    )


def pair_twists(extent, fine):
    m = extent // 4
    out = np.zeros((m, LANES), np.float32)
    for e in range(1, 4):
        c, s = roots(fine, [e], extent, 1)
        out[:, 2 * e - 2 : 2 * e - 1], out[:, 2 * e - 1 : 2 * e] = c, s
    for t in range(4):
        c, s = roots(2 * np.arange(m // 2) + t // 2 + m * (t % 2), [1], extent, -1)
        out[: m // 2, 6 + 2 * t : 7 + 2 * t], out[: m // 2, 7 + 2 * t : 8 + 2 * t] = c, s
    return out


def filter_block(
    x_ref, base, block, scal_ref, fwd_ref, inv_ref, twist_ref, phase_ref, hi_ref, lo_ref, mid_ref
):
    n_one = phase_ref.shape[0]
    step = 16
    group = max(1, 256 // block)
    f_hi, f_lo = fwd_ref[0], fwd_ref[1]
    b_hi, b_lo = inv_ref[0], inv_ref[1]
    whole = pl.ds(pl.multiple_of(base, block), block)

    wide = 8 * LANES

    @pl.loop(0, n_one * LANES // wide)
    def _(a):
        at = pl.ds(pl.multiple_of(a * wide, wide), wide)
        x = times((x_ref[0, whole, at], x_ref[1, whole, at]), sincos(scal_ref[whole, at]))
        x_ref[0, whole, at] = x[0]
        x_ref[1, whole, at] = x[1]

    @pl.loop(0, block // step)
    def _(i):
        rows = pl.ds(pl.multiple_of(i * step, step), step)
        at = pl.ds(pl.multiple_of(base + i * step, step), step)
        v = [
            tuple(x_ref[c, at, pl.ds(a * LANES, LANES)] for c in (0, 1))
            for a in range(n_one)
        ]
        for k, x in enumerate(fft(v, -1)):
            if k:
                x = times(x, (twist_ref[0, k : k + 1, :], twist_ref[1, k : k + 1, :]))
            for c in (0, 1):
                h, l = split(x[c])
                hi_ref[k, rows, pl.ds(c * LANES, LANES)] = h
                lo_ref[k, rows, pl.ds(c * LANES, LANES)] = l

    @pl.loop(0, n_one // group)
    def _(i):
        ks = pl.ds(i * group, group)
        flat = (group * block, 2 * LANES)
        h, l = hi_ref[ks].reshape(flat), lo_ref[ks].reshape(flat)
        r = mm(h, f_hi) + mm(l, f_hi) + mm(h, f_lo)
        turn = phase_ref[ks, whole, :]
        r = times((r[:, :LANES], r[:, LANES:]), sincos(turn.reshape(group * block, LANES)))
        h, l = split(jnp.concatenate(r, axis=1))
        r = mm(h, b_hi) + mm(l, b_hi) + mm(h, b_lo)
        at = pl.ds(pl.multiple_of(i * group * block, block), group * block)
        mid_ref[0, at, :] = r[:, :LANES]
        mid_ref[1, at, :] = r[:, LANES:]

    @pl.loop(0, block // 8)
    def _(i):
        at = pl.ds(pl.multiple_of(base + i * 8, 8), 8)
        v = []
        for k in range(n_one):
            x = tuple(mid_ref[c, pl.ds(pl.multiple_of(k * block + i * 8, 8), 8), :] for c in (0, 1))
            if k:
                x = times(x, (twist_ref[0, k : k + 1, :], -twist_ref[1, k : k + 1, :]))
            v.append(x)
        for a, x in enumerate(fft(v, 1)):
            for c in (0, 1):
                x_ref[c, at, pl.ds(a * LANES, LANES)] = x[c]


def turn_in(load, mid, start, stop):
    per = mid.shape[1] // LANES

    @pl.loop(start, stop)
    def _(g):
        mid[g // per, pl.ds(pl.multiple_of(g % per * LANES, LANES), LANES), :] = load(g).T


def turn_out(mid, turn, base, start, stop):
    n_one = turn.shape[0]
    part = mid.shape[1] // n_one
    at = pl.ds(pl.multiple_of(base, LANES), LANES)

    @pl.loop(start, stop)
    def _(k):
        rows = pl.ds(k, part, stride=n_one)
        x = jnp.concatenate([mid[h, rows, :] for h in range(LANES // part)], axis=0)
        turn[k, at, :] = x.T


def pair_kernel(
    n_strip, n_az, block, chunk,
    raw_ref, scaling_ref, range_ref, azimuth_ref, front_ref,
    twists_any, fwd_any, inv_any, range_twist_any, table_any,
    o_ref,
    twists_ref, fwd_ref, inv_ref, range_twist_ref, table_ref,
    cols, prev, dop, scal, swap, turn, phase, ret, for_chip,
    front, turn_front, twist_ref, spin, head, hi_ref, lo_ref, mid,
    load, load_range, load_echo, load_front, load_table, z_send, z_recv, y_send, y_recv, c_send, c_recv, f_send, f_recv,
    s_send, s_recv, p_send, p_recv, down_send, up_send, az_recv, swap_send, swap_recv, x_send, x_recv,
    w_send, w_recv, w_local, v_send, v_recv, v_local,
):
    t = lax.axis_index("tile")
    az = lax.axis_index("az")
    strip = lax.axis_index("strip")
    y, c = t // 2, t % 2
    tiles = 4
    count, ranges = range_ref.shape
    half = count // 2
    extent, width = scaling_ref.shape
    m = extent // 4
    pulses = o_ref.shape[1]
    q = pulses // 4
    rows_own = raw_ref.shape[1]
    spans = width // LANES
    n_one = ranges // LANES
    chunks = n_one // chunk
    blocks = count // block
    part = half // blocks
    parts = chunks // 4
    whole = blocks - 2
    lag, steps = 2, 2
    step = block // steps
    partner, across = {"tile": 2 * y + 1 - c}, {"tile": 2 * (1 - y) + c}
    other = pl.ds(pl.multiple_of(2 * (1 - y) * width, LANES), 2 * width)
    mine = pl.ds(pl.multiple_of(t * width, LANES), width)
    slab = strip * n_az + az

    def remote(src, dst, send, recv, device):
        return pltpu.make_async_remote_copy(
            src_ref=src, dst_ref=dst, send_sem=send, recv_sem=recv,
            device_id=device, device_id_type=pl.DeviceIdType.MESH,
        )

    def pulse_rows(tile):
        return pl.ds(pl.multiple_of(tile * rows_own, rows_own), rows_own)

    def groups(j):
        return pl.ds(j * chunk, chunk)

    def onward(a):
        return remote(
            raw_ref.at[:, :, lanes(a)], prev.at[a], z_send.at[a], z_recv.at[a],
            {"az": lax.rem(az + 1, n_az)},
        )

    def own_echo(a):
        return pltpu.make_async_copy(
            raw_ref.at[:, :, lanes(a)], cols.at[a, :, pulse_rows(t), :], load_echo.at[a]
        )

    def range_piece(a, first, rows, stride=None):
        row = a % (extent // count) * count + first
        return phase.at[a // (extent // count), pl.ds(row, rows, stride=stride), :]

    def own_range(a):
        return pltpu.make_async_copy(range_ref.at[:, lanes(a)], range_piece(a, 0, count), load_range.at[a])

    def own_phase(source, j, k):
        return pltpu.make_async_copy(source.at[:, lanes(j)], phase.at[j], load.at[k, j])

    def echo_across(j):
        return remote(
            prev.at[j], cols.at[j, :, pulse_rows(t), :], y_send.at[j], y_recv.at[j], across,
        )

    def echo_core(j):
        at = cols.at[groups(j), :, pulse_rows(t), :]
        return remote(at, at, c_send.at[j], c_recv.at[j], partner)

    def echo_forward(j):
        at = cols.at[j, :, pulse_rows(2 * (1 - y) + c), :]
        return remote(at, at, f_send.at[j], f_recv.at[j], partner)

    def scaling_core():
        return remote(dop.at[0, :, pl.ds(0, width)], scal.at[:, mine], s_send, s_recv, partner)

    def scaling_chip(k):
        to = {"tile": 2 * (1 - y) + lax.rem(c + k, 2)}
        return remote(
            for_chip.at[lax.rem(c + k, 2)],
            scal.at[pl.ds(pl.multiple_of(slab * block, block), block), mine],
            p_send.at[k], p_recv.at[k], to,
        )

    def turn_part(ref, base, z, s):
        first = base + (z * n_strip + s) * part
        return ref.at[:, pl.ds(pl.multiple_of(first, part), part), :]

    def scal_rows(g):
        return scal.at[pl.ds(pl.multiple_of(g * block, block), block), other]

    def range_chip():
        return remote(
            turn_part(swap, 0, az, strip), turn_part(turn, y * half, az, strip),
            p_send.at[2], p_recv.at[2], across,
        )

    def slice_of(z, k):
        if k == 1:
            return turn_part(turn, (1 - y) * half, z, strip)
        return scal_rows((y if k == 0 else 1 - y) * n_az + z)

    def swap_scaling():
        at = scal_rows(slab)
        return remote(at, at, swap_send, swap_recv, {"strip": 1 - strip})

    def up(i, k):
        at = slice_of(az - i, k)
        return remote(at, at, up_send.at[i, k], az_recv.at[az - i, k], {"az": lax.rem(az + 1, n_az)})

    def arrived(z, k):
        at = slice_of(z, k)
        remote(at, at, up_send.at[0, k], az_recv.at[z, k], {"az": lax.rem(az + 1, n_az)}).wait_recv()

    def down(i, k):
        at = slice_of(az + i, k)
        return remote(
            at, at, down_send.at[i, k], az_recv.at[az + i, k], {"az": lax.rem(az + n_az - 1, n_az)}
        )

    def relay(i, k):
        @pl.when(az >= i)
        def _():
            arrived(az - i, k)
            if k == 1:
                sideways(az - i).start()

            @pl.when(az + 1 < n_az)
            def _():
                up(i, k).start()

    def hand_over(d, k):
        @pl.when(az + d < n_az)
        def _():
            arrived(az + d, k)
            if k == 1:
                sideways(az + d).start()

            @pl.when(az > 0)
            def _():
                down(d, k).start()

    def sideways(z):
        at = slice_of(z, 1)
        return remote(at, at, x_send.at[z], x_recv.at[z], {"strip": 1 - strip})

    def order(n):
        return jnp.where(az + n < n_az, az + n, n_az - 1 - n)

    def place(n):
        s = jnp.where(n < n_az, y, 1 - y)
        z = order(lax.rem(n, n_az))
        base = (s * n_az + z) * block
        row = (2 * s + c) * m + y * half + z * block
        return pl.ds(pl.multiple_of(base, block), block), pl.ds(pl.multiple_of(row, block), block), base, row

    def piece_rows(u):
        _, _, base, row = place(u // steps)
        first = lax.rem(u, steps) * step
        return tuple(pl.ds(pl.multiple_of(x + first, step), step) for x in (base, row))

    def back(u, k):
        to = lax.rem(t + k, tiles)
        src, dst = piece_rows(u)
        at = pl.ds(pl.multiple_of(to * width, LANES), width)
        return remote(
            dop.at[:, src, at], ret.at[:, dst, :], w_send.at[u, k - 1], w_recv.at[u, k - 1], {"tile": to}
        )

    def keep(u):
        src, dst = piece_rows(u)
        return pltpu.make_async_copy(dop.at[:, src, mine], ret.at[:, dst, :], w_local.at[u])

    def back_span(j, n, k):
        to = lax.rem(t + k, tiles)
        src, dst, _, _ = place(n)
        return remote(
            dop.at[:, src, lanes(to * spans + j)], ret.at[:, dst, lanes(j)],
            v_send.at[j, n - whole, k - 1], v_recv.at[j, n - whole, k - 1], {"tile": to},
        )

    def keep_span(j, n):
        src, dst, _, _ = place(n)
        return pltpu.make_async_copy(
            dop.at[:, src, lanes(t * spans + j)], ret.at[:, dst, lanes(j)], v_local.at[j, n - whole]
        )

    get_front = pltpu.make_async_copy(front_ref.at[y], front, load_front)
    get_tables = [
        pltpu.make_async_copy(source, target, load_table.at[i])
        for i, (source, target) in enumerate(
            (
                (twists_any, twists_ref),
                (fwd_any, fwd_ref),
                (inv_any, inv_ref),
                (range_twist_any, range_twist_ref),
                (table_any, table_ref),
            )
        )
    ]
    barrier = greet(
        [{"tile": lax.rem(t + k, tiles)} for k in range(1, tiles)]
        + [{"strip": 1 - strip}]
    )
    neighbours = ((az + 1, az + 1 < n_az), (az + n_az - 1, az > 0))
    for to, there in neighbours:
        @pl.when(there)
        def _():
            pl.semaphore_signal(
                barrier, inc=1, device_id={"az": lax.rem(to, n_az)}, device_id_type=pl.DeviceIdType.MESH
            )


    @pl.loop(0, spans)
    def _(j):
        own_phase(scaling_ref, j, 0).start()

    @pl.when(az == 0)
    def _():
        @pl.loop(0, n_one)
        def _(a):
            prev[a] = jnp.zeros((2, rows_own, LANES), F32)

    @pl.loop(0, spans)
    def _(j):
        own_phase(scaling_ref, j, 0).wait()
        for k in (0, 1):
            first = (2 * strip + k) * m + 2 * az * block + 1 - y
            for_chip[k, :, lanes(j)] = phase[j, pl.ds(first, block, stride=2), :]

    pl.semaphore_wait(barrier, tiles + sum(there.astype(jnp.int32) for _, there in neighbours))
    for k in (0, 1):
        scaling_chip(k).start()

    @pl.when(az < n_az - 1)
    def _():
        @pl.loop(0, n_one)
        def _(a):
            onward(a).start()

    @pl.loop(0, n_one)
    def _(a):
        own_echo(a).start()

    get_front.start()
    for copy in get_tables:
        copy.start()

    sign = (1 - 2 * y).astype(F32)

    @pl.loop(0, chunks + lag + 1)
    def _(j):
        @pl.when(j < chunks)
        def _():
            for i in range(chunk):
                at = j * chunk + i
                own_echo(at).wait()

                @pl.when(az > 0)
                def _():
                    onward(at).wait_recv()

                for k in (0, 1):
                    a = cols[at, k, pulse_rows(t), :]
                    b = prev[at, k] * sign
                    cols[at, k, pulse_rows(t), :] = a + b
                    prev[at, k] = a - b
                echo_across(at).start()
            echo_core(j).start()

        @pl.when(j == 0)
        def _():
            @pl.loop(0, spans)
            def _(i):
                for h in (0, 1):
                    rows = pl.ds(h * half, half)
                    dop[0, rows, lanes(i)] = phase[i, pl.ds((2 * h + 1 - c) * m + y, half, stride=2), :]
                    scal[rows, lanes(t * spans + i)] = phase[i, pl.ds((2 * h + c) * m + y, half, stride=2), :]

            scaling_core().start()

            @pl.loop(0, n_one)
            def _(a):
                own_range(a).start()

            get_tables[0].wait()
            for k in range(6):
                twist_ref[k] = jnp.broadcast_to(twists_ref[:, k : k + 1], (m, LANES))
            for k in (0, 1):
                x = twists_ref[pl.ds(0, half), 6 + k : 7 + k]
                for i in range(1, tiles):
                    x = jnp.where(t == i, twists_ref[pl.ds(0, half), 6 + 2 * i + k : 7 + 2 * i + k], x)
                turn_front[k] = jnp.broadcast_to(x, (half, LANES))

        @pl.when(j == 1)
        def _():
            scaling_core().wait_send()
            get_front.wait()
            odd = lax.rem(lax.broadcasted_iota(jnp.int32, (1, pulses), 1), 2) * c
            for k in (0, 1):
                front[k] = (front[k].astype(F32) * (1 - 2 * odd).astype(F32)).astype(BF16)

        @pl.when(j == 2)
        def _():
            for k in (0, 1):
                scaling_chip(k).wait_recv()
            swap_scaling().start()

        @pl.when(j == 4)
        def _():
            swap_scaling().wait_recv()

            @pl.when(az > 0)
            def _():
                for k in (0, 2):
                    down(0, k).start()

        @pl.when(j == 1)
        def _():
            @pl.loop(0, n_one)
            def _(a):
                own_range(a).wait()

        few = n_one // parts

        @pl.when((j >= 1) & (j < 1 + parts))
        def _():
            i = (j - 1) * few
            turn_in(lambda g: range_piece(g, 1 - y, half, 2)[...], mid, i, i + few)

        @pl.when((j >= 1 + parts) & (j < 1 + 2 * parts))
        def _():
            i = (j - 1 - parts) * few
            turn_out(mid, swap, 0, i, i + few)

        @pl.when((j >= 1 + 2 * parts) & (j < 1 + 3 * parts))
        def _():
            i = (j - 1 - 2 * parts) * few
            turn_in(lambda g: range_piece(g, y, half, 2)[...], mid, i, i + few)

        @pl.when((j >= 1 + 3 * parts) & (j < 1 + 4 * parts))
        def _():
            i = (j - 1 - 3 * parts) * few
            turn_out(mid, turn, y * half, i, i + few)

        @pl.when(j == 1 + 4 * parts)
        def _():
            @pl.loop(0, spans)
            def _(i):
                own_phase(azimuth_ref, i, 1).start()

        @pl.when(j == chunks - 1)
        def _():
            range_chip().start()

            @pl.when(az + 1 < n_az)
            def _():
                up(0, 0).start()

        for d in range(1, n_az):
            for k in (0, 2):
                @pl.when(j == 2 + chunks * d // n_az + k // 2)
                def _():
                    hand_over(d, k)

        @pl.when(j > lag)
        def _():
            now = j - lag - 1
            echo_core(now).wait_recv()
            for i in range(chunk):
                echo_forward(now * chunk + i).wait_recv()
            r = []
            for e in (0, 1):
                rows = pl.ds(e, pulses // 2, stride=2)
                s = jnp.concatenate(
                    [
                        jnp.concatenate([cols[now * chunk + i, k, rows, :] for k in (0, 1)], axis=0)
                        for i in range(chunk)
                    ],
                    axis=1,
                )
                s_hi, s_lo = split(s)
                hi, lo = front[0], front[1]
                x = mm(hi, s_hi) + mm(hi, s_lo) + mm(lo, s_hi)
                r.append((x[:half], x[half:]))
            w = tuple(jnp.concatenate([turn_front[k]] * chunk, axis=1) for k in (0, 1))
            r[1] = times(r[1], w)
            for k in (0, 1):
                a, b = r[0][k], r[1][k]
                at = pl.ds(pl.multiple_of(now * chunk * LANES, LANES), chunk * LANES)
                dop[k, pl.ds(0, half), at] = a + b
                dop[k, pl.ds(half, half), at] = a - b

        @pl.when((j >= lag) & (j < chunks + lag))
        def _():
            for i in range(chunk):
                echo_across((j - lag) * chunk + i).wait_recv()
                echo_forward((j - lag) * chunk + i).start()

    scaling_core().wait_recv()
    for copy in get_tables[1:]:
        copy.wait()

    @pl.loop(0, blocks * steps)
    def _(u):
        @pl.when(u == 1)
        def _():
            relay(1, 0)
            range_chip().wait_recv()
            sideways(az).start()

            @pl.when(az > 0)
            def _():
                down(0, 1).start()

            @pl.when(az + 1 < n_az)
            def _():
                up(0, 1).start()
                up(0, 2).start()

        for i in range(2, n_az):
            @pl.when(u == steps * i)
            def _():
                relay(i, 0)

        for i in range(1, n_az):
            @pl.when(u == steps * (i + 1))
            def _():
                hand_over(i, 1)
                relay(i, 1)

            @pl.when(u == steps * (n_az + i - 1))
            def _():
                relay(i, 2)

        @pl.when(u == n_az * steps)
        def _():
            for i in range(n_az):
                sideways(order(i)).wait_recv()

        filter_block(
            dop, place(u // steps)[2] + lax.rem(u, steps) * step, step,
            scal, fwd_ref, inv_ref, range_twist_ref, turn, hi_ref, lo_ref, mid,
        )

        @pl.when(u < whole * steps)
        def _():
            for k in range(tiles - 1, 0, -1):
                back(u, k).start()
            keep(u).start()

    @pl.loop(0, spans)
    def _(j):
        for n in range(whole, blocks):
            for k in range(tiles - 1, 0, -1):
                back_span(j, n, k).start()
            keep_span(j, n).start()

    @pl.loop(0, spans)
    def _(j):
        own_phase(azimuth_ref, j, 1).wait()

    @pl.loop(0, whole * steps)
    def _(u):
        for k in range(1, tiles):
            back(u, k).wait_recv()
        keep(u).wait()

    @pl.loop(0, spans)
    def _(j):
        for f in range(4):
            angle = jnp.concatenate(
                [phase[j, pl.ds(f * m + p, half, stride=2), :] for p in (0, 1)], axis=0
            )
            spin[0, f], spin[1, f] = sincos(angle)
        for n in range(whole, blocks):
            for k in range(1, tiles):
                back_span(j, n, k).wait_recv()
            keep_span(j, n).wait()
        hi, lo = table_ref[0], table_ref[1]
        v = []
        for f in range(4):
            rows = pl.ds(f * m, m)
            v.append(times((ret[0, rows, lanes(j)], ret[1, rows, lanes(j)]), (spin[0, f], spin[1, f])))
        for e, x in enumerate(four(v, 1)):
            if e:
                x = times(x, (twist_ref[2 * e - 2], twist_ref[2 * e - 1]))
            s_hi, s_lo = split(jnp.concatenate(x, axis=0))
            r = mm(hi, s_hi) + mm(hi, s_lo) + mm(lo, s_hi)
            for k in (0, 1):
                head[k, pl.ds(e, q, stride=4), :] = r[k * q : (k + 1) * q]
        o_ref[:, :, lanes(j)] = head[...]

    @pl.when(az < n_az - 1)
    def _():
        @pl.loop(0, n_one)
        def _(a):
            onward(a).wait_send()

    @pl.loop(0, chunks)
    def _(j):
        for i in range(chunk):
            echo_across(j * chunk + i).wait_send()
            echo_forward(j * chunk + i).wait_send()
        echo_core(j).wait_send()

    range_chip().wait_send()
    for k in (0, 1):
        scaling_chip(k).wait_send()
    swap_scaling().wait_send()
    for z in range(n_az):
        sideways(z).wait_send()
    for k in (0, 1, 2):
        for d in range(n_az - 1):
            @pl.when((az > 0) & (az + d < n_az))
            def _():
                down(d, k).wait_send()

            @pl.when((az + 1 < n_az) & (az >= d))
            def _():
                up(d, k).wait_send()

    @pl.loop(0, whole * steps)
    def _(u):
        for k in range(1, tiles):
            back(u, k).wait_send()

    @pl.loop(0, spans)
    def _(j):
        for n in range(whole, blocks):
            for k in range(1, tiles):
                back_span(j, n, k).wait_send()


def pair_body(raw_echo, phase_scaling, phase_range, phase_azimuth):
    tiles = lax.axis_size("tile")
    n_az, n_strip = lax.axis_size("az"), lax.axis_size("strip")
    pulses = raw_echo.shape[1] * tiles
    extent, width = phase_scaling.shape
    count, ranges = phase_range.shape
    m, q, half = extent // 4, pulses // 4, count // 2
    n_one, spans = ranges // LANES, width // LANES
    blocks = n_strip * n_az
    block = count // blocks
    chunk = 2
    chunks = n_one // chunk
    whole = blocks - 2
    rest = blocks - whole
    fine = np.concatenate([np.arange(0, m, 2), np.arange(1, m, 2)])
    lane = np.arange(LANES)
    vmem = pl.BlockSpec(memory_space=pltpu.VMEM)
    anyspace = pl.BlockSpec(memory_space=pl.ANY)
    dma = pltpu.SemaphoreType.DMA
    c, s = roots(np.arange(n_one), lane, ranges, -1)
    return pl.pallas_call(
        functools.partial(pair_kernel, n_strip, n_az, block, chunk),
        out_shape=pltpu.VMEM((2, pulses, width), F32),
        in_specs=[anyspace] * 10,
        out_specs=vmem,
        scratch_shapes=[
            pltpu.VMEM((m, LANES), F32),
            pltpu.VMEM((2, 2 * LANES, 2 * LANES), BF16),
            pltpu.VMEM((2, 2 * LANES, 2 * LANES), BF16),
            pltpu.VMEM((2, n_one, LANES), F32),
            pltpu.VMEM((2, 2 * q, 2 * m), BF16),
            pltpu.VMEM((n_one, 2, pulses, LANES), F32),
            pltpu.VMEM((n_one, 2, pulses // tiles, LANES), F32),
            pltpu.VMEM((2, count, ranges), F32),
            pltpu.VMEM((count, ranges), F32),
            pltpu.VMEM((n_one, half, LANES), F32),
            pltpu.VMEM((n_one, count, LANES), F32),
            pltpu.VMEM((spans, extent, LANES), F32),
            pltpu.VMEM((2, extent, width), F32),
            pltpu.VMEM((2, block, width), F32),
            pltpu.VMEM((2, count, pulses), BF16),
            pltpu.VMEM((2, half, LANES), F32),
            pltpu.VMEM((6, m, LANES), F32),
            pltpu.VMEM((2, 4, m, LANES), F32),
            pltpu.VMEM((2, pulses, LANES), F32),
            pltpu.VMEM((n_one, block // 2, 2 * LANES), BF16),
            pltpu.VMEM((n_one, block // 2, 2 * LANES), BF16),
            pltpu.VMEM((2, n_one * LANES // 2, LANES), F32),
            dma((2, spans)), dma((n_one,)), dma((n_one,)), dma, dma((5,)),
            dma((n_one,)), dma((n_one,)),
            dma((n_one,)), dma((n_one,)),
            dma((chunks,)), dma((chunks,)),
            dma((n_one,)), dma((n_one,)),
            dma, dma,
            dma((3,)), dma((3,)),
            dma((n_az, 3)), dma((n_az, 3)), dma((n_az, 3)),
            dma, dma,
            dma((n_az,)), dma((n_az,)),
            dma((2 * whole, tiles - 1)), dma((2 * whole, tiles - 1)), dma((2 * whole,)),
            dma((spans, rest, tiles - 1)), dma((spans, rest, tiles - 1)), dma((spans, rest)),
        ],
        compiler_params=pltpu.CompilerParams(
            collective_id=0, has_side_effects=True, vmem_limit_bytes=59 << 20
        ),
    )(
        raw_echo,
        phase_scaling,
        phase_range,
        phase_azimuth,
        pair_front(extent, pulses),
        pair_twists(extent, fine),
        right_table(lane, lane, LANES, -1),
        right_table(lane, lane, LANES, 1, 1.0 / ranges),
        np.stack([c, s]).astype(np.float32),
        left_table(np.arange(q), fine, m, 1, 1.0 / extent),
    )


def paired(raw_echo, phase_scaling, phase_range):
    tiles, n_az, n_strip = (lax.axis_size(a) for a in ("tile", "az", "strip"))
    count = phase_range.shape[0]
    blocks = n_az * n_strip
    return (
        tiles == 4
        and n_strip == 2
        and n_az > 1
        and count == 2 * LANES
        and phase_scaling.shape[0] == 2 * raw_echo.shape[1] * tiles
        and count % (32 * blocks) == 0
        and phase_range.shape[1] % (8 * LANES) == 0
    )


def body(raw_echo, phase_scaling, phase_range, phase_azimuth):
    plan = pair_body if paired(raw_echo, phase_scaling, phase_range) else tail_body
    return plan(raw_echo, phase_scaling, phase_range, phase_azimuth)


def solution(mesh):
    return jax.shard_map(
        body,
        mesh=mesh,
        in_specs=(
            P(None, ("strip", "az", "tile"), None),
            P(None, "tile"),
            P("tile", None),
            P(None, "tile"),
        ),
        out_specs=P(None, ("strip", "az"), "tile"),
        check_vma=False,
    )
```
